32 devices in a mesh: grp: 2 (over y), row: 8 (over z, core), col: 2 (over x).
Axes of the slice: x: 2, y: 2, z: 4, core: 2. Of those that a mesh axis runs over, the one named last changes fastest.
Arguments:
- single: float32 [2, 512, 384], P(None, ('grp', 'row')), parts along dimension 1, may hold values from -6 to 6
- frames: float32 [2, 12, 512], P(None, None, ('grp', 'row')), parts along dimension 2, may hold values from -4 to 4, as said below
- saved_probs: bfloat16 [2, 12, 512, 256], P(None, None, ('grp', 'row'), 'col'), parts along dimension 2, may hold values from 0.0009994507 to 100
- pair: bfloat16 [512, 256, 128], P(('grp', 'row'), 'col'), parts along dimension 0, may hold values from -6 to 6
- cotangent: float32 [512, 384], P(('grp', 'row')), parts along dimension 0, may hold values from -12 to 12
- chains: int32 [512], P(('grp', 'row')), parts along dimension 0, may hold values from 0 to 15, never falling along the last dimension, each value on 1 to 64 neighbouring positions
- links: int32 [32, 16], P('grp'), parts along dimension 0, may hold values 0 or 1
- w_query: bfloat16 [384, 192], replicated, may hold values from -0.3125 to 0.3125
- w_key: bfloat16 [384, 192], replicated, may hold values from -0.3125 to 0.3125
- w_value: bfloat16 [384, 192], replicated, may hold values from -0.3125 to 0.3125
- w_query_points: bfloat16 [384, 144], replicated, may hold values from -0.3125 to 0.3125
- w_key_points: bfloat16 [384, 144], replicated, may hold values from -0.3125 to 0.3125
- w_value_points: bfloat16 [384, 288], replicated, may hold values from -0.3125 to 0.3125
- w_bias: bfloat16 [128, 12], replicated, may hold values from -0.5 to 0.5
- w_out: bfloat16 [2112, 384], replicated, may hold values from -0.125 to 0.125
- head_weights: float32 [12], replicated, may hold values from -1 to 1
Outputs:
- d_single: float32 [512, 384], P(('grp', 'row')), parts along dimension 0
- d_frames: float32 [2, 12, 512], P(None, None, ('grp', 'row')), parts along dimension 2
- d_pair: bfloat16 [512, 256, 128], P(('grp', 'row'), 'col'), parts along dimension 0
The draws below stay inside these ranges and needn't reach their ends.
There are 2 independent parts, one for each index of `grp`. The reference program is written for one: setup_inputs(seed, part) draws one part's arguments, and reference() takes and returns one part's arrays. A program takes and returns all parts, laid end to end along the dimension named above; an argument that names none is the same for every part. Nothing has to cross between parts.
Inputs may be any that keep to these rules, and one draw needn't show every extreme that they name: `chains`: chain numbers never fall along the residues; each chain holds 1 to 64 residues and one holds exactly 64. `frames`: rows 0 to 8 of each residue hold a rotation matrix in row-major order, rows 9 to 11 a translation.
All inputs are finite; a program needn't handle non-finite values.
Results may differ from the reference program's by a relative error of at most 0.0055.
Values sent between devices are 32-bit elements; how exact they have to be, the bound alone decides.
No kernel may reach another device: no remote copies, remote signals or barrier semaphores. Data moves between devices by JAX's collectives and lax.ppermute only.
A program may use at most 64 MiB of HBM per device.

```python
import math
import jax
import jax.numpy as jnp
import numpy as np
from jax import lax

C = 384
H = 12
HD = 16
CZ = 128
PQ = 4
PV = 8
ITERS = 2
NCHAIN = 16
N = 256


def draw_frames(key, part):
    quat_key, shift_key = jax.random.split(jax.random.fold_in(key, 11))
    quaternion = jax.random.normal(quat_key, (ITERS, 4, N), jnp.float32)
    quaternion = quaternion / jnp.sqrt(jnp.sum(quaternion * quaternion, axis=1, keepdims=True) + 1e-12)
    real_part = quaternion[:, 0]
    first_im = quaternion[:, 1]
    second_im = quaternion[:, 2]
    third_im = quaternion[:, 3]
    entries = [real_part * real_part + first_im * first_im - second_im * second_im - third_im * third_im, 2.0 * (first_im * second_im - real_part * third_im), 2.0 * (first_im * third_im + real_part * second_im), 2.0 * (first_im * second_im + real_part * third_im), real_part * real_part - first_im * first_im + second_im * second_im - third_im * third_im, 2.0 * (second_im * third_im - real_part * first_im), 2.0 * (first_im * third_im - real_part * second_im), 2.0 * (second_im * third_im + real_part * first_im), real_part * real_part - first_im * first_im - second_im * second_im + third_im * third_im]
    shift_vec = jnp.clip(jax.random.normal(shift_key, (ITERS, 3, N), jnp.float32), -4.0, 4.0)
    return jnp.concatenate([jnp.stack(entries, axis=1), shift_vec], axis=1)


def place_ends(values, rng, low, largest):
    extent = values.shape
    spot = [jax.random.randint(jax.random.fold_in(rng, axis), (), 0, extent[axis]) for axis in range(len(extent))]
    values = values.at[tuple(spot)].set(low)
    longest = extent.index(max(extent))
    spot[longest] = (spot[longest] + 1) % extent[longest]
    return values.at[tuple(spot)].set(largest)


def steps_of(key, shape, pieces, low, largest):
    loudness = 1.0
    for axis_at, parts in pieces:
        heights = jax.random.uniform(jax.random.fold_in(jax.random.fold_in(key, 6), axis_at), (parts,), jnp.float32, low / len(pieces), largest / len(pieces))
        loudness = loudness * jnp.repeat(jnp.exp(heights), shape[axis_at] // parts).reshape((-1,) + (1,) * (len(shape) - 1 - axis_at))
    return loudness


def split_up(number_of, total, most, skew):
    weights = [(1 << 20) // math.isqrt(standing ** skew) + 1 for standing in range(2, number_of + 1)]
    surplus, holding = total - most - (number_of - 1), [1] * (number_of - 1)
    while surplus > 0:
        candidates = [i for i in range(number_of - 1) if holding[i] < most]
        mass, budget = sum([weights[i] for i in candidates]), surplus
        for i in candidates:
            addition = min(most - holding[i], max(1, budget * weights[i] // mass), surplus)
            holding[i] = holding[i] + addition
            surplus = surplus - addition
    return np.array([most] + holding)


def ragged_sizes(own_key, number_of, total, reach, skew):
    if number_of == 2:
        one = jax.random.randint(own_key, (), max(1, total - reach), min(reach, total - 1) + 1)
        return jnp.stack([one, total - one])
    sizes = jnp.asarray(split_up(number_of, total, reach, skew), jnp.int32)
    pairs = (number_of - 1) // 2
    source_of, sink = sizes[1:1 + 2 * pairs:2], sizes[2:2 + 2 * pairs:2]
    slack = jnp.minimum(source_of - 1, reach - sink)
    shifted = jax.random.randint(jax.random.fold_in(own_key, 1), (pairs,), 0, 1 << 20) % (slack + 1)
    sizes = sizes.at[1:1 + 2 * pairs:2].set(source_of - shifted).at[2:2 + 2 * pairs:2].set(sink + shifted)
    return sizes[jax.random.permutation(jax.random.fold_in(own_key, 2), number_of)]


def gaussian(stream_key, dims, scale, reach, shards=(), dtype=jnp.bfloat16):
    result = jax.random.normal(stream_key, dims, jnp.float32) * scale
    if len(shards) > 0:
        result = steps_of(stream_key, dims, shards, -0.22, 0.18) * result
    return jnp.clip(result, min=-reach, max=reach).astype(dtype)


def setup_inputs(seed: int = 0, part: int = 0) -> dict:
    keys = jax.random.split(jax.random.key(seed), 17)
    part_keys = jax.random.split(jax.random.fold_in(keys[16], part), 17)
    return {
        "single": gaussian(part_keys[0], (ITERS, N, C), 1.0, 6.0, ((1, 8),), jnp.float32),
        "frames": draw_frames(jax.random.fold_in(jax.random.fold_in(keys[16], part), 71), part),
        "saved_probs": jnp.clip(jnp.exp(math.log(100.0) - 11.5134749 * jax.random.uniform(part_keys[2], (ITERS, H, N, N), jnp.float32) ** steps_of(part_keys[2], (ITERS, H, N, N), ((2, 8), (3, 2)), -0.2, 0.2)), 0.0009994507, 100.0).astype(jnp.bfloat16),
        "pair": gaussian(part_keys[3], (N, N, CZ), 1.0, 6.0, ((0, 8), (1, 2))),
        "cotangent": gaussian(part_keys[4], (N, C), 2.0, 12.0, ((0, 8),), jnp.float32),
        "chains": jnp.searchsorted(jnp.cumsum(ragged_sizes(part_keys[5], NCHAIN, N, N // 4, 2)), jnp.arange(N), side="right").astype(jnp.int32),
        "links": place_ends((jax.random.randint(part_keys[6], (NCHAIN, NCHAIN), 0, 3) < 1).astype(jnp.int32), jax.random.fold_in(part_keys[6], 1), 0, 1),
        "w_query": gaussian(keys[7], (C, H * HD), C ** -0.5, 0.3125),
        "w_key": gaussian(keys[8], (C, H * HD), C ** -0.5, 0.3125),
        "w_value": gaussian(keys[9], (C, H * HD), C ** -0.5, 0.3125),
        "w_query_points": gaussian(keys[10], (C, 3 * H * PQ), C ** -0.5, 0.3125),
        "w_key_points": gaussian(keys[11], (C, 3 * H * PQ), C ** -0.5, 0.3125),
        "w_value_points": gaussian(keys[12], (C, 3 * H * PV), C ** -0.5, 0.3125),
        "w_bias": gaussian(keys[13], (CZ, H), CZ ** -0.5, 0.5),
        "w_out": gaussian(keys[14], (H * (HD + 4 * PV + CZ), C), (H * (HD + 4 * PV + CZ)) ** -0.5, 0.125),
        "head_weights": jnp.clip(jax.random.uniform(keys[15], (H,), jnp.float32, -1.0, 1.0), -1.0, 1.0),
    }


FULL_PRECISION = lax.Precision.HIGHEST
NORM_EPS = 1e-08

def split_frames(frames_now):
    amount = frames_now.shape[1]
    return (frames_now[:9].reshape(3, 3, amount), frames_now[9:])

def by_head(points, head_count):
    amount = points.shape[0]
    return points.reshape(amount, 3, head_count, -1).transpose(0, 2, 1, 3).reshape(amount, head_count, -1)

def by_component(points, head_count):
    amount = points.shape[0]
    return points.reshape(amount, head_count, 3, -1).transpose(0, 2, 1, 3).reshape(amount, 3, -1)

def project(single_now, rotation, shift_vec, w_plain, w_points, head_count):
    amount = single_now.shape[0]
    plain_part = jnp.dot(single_now, w_plain.astype(jnp.float32), precision=FULL_PRECISION).reshape(amount, head_count, -1)
    local_pts = jnp.dot(single_now, w_points.astype(jnp.float32), precision=FULL_PRECISION).reshape(amount, 3, -1)
    placed = jnp.einsum('abn,nbk->nak', rotation, local_pts, precision=FULL_PRECISION) + shift_vec.T[:, :, None]
    return (plain_part, local_pts, placed)

def frame_grad(rotation, local_pts, d_placed):
    amount = local_pts.shape[0]
    d_rotation = jnp.einsum('nak,nbk->abn', d_placed, local_pts, precision=FULL_PRECISION).reshape(9, amount)
    d_shift = lax.optimization_barrier(jnp.sum(d_placed, axis=2)).T
    d_local = jnp.einsum('abn,nak->nbk', rotation, d_placed, precision=FULL_PRECISION)
    return (d_rotation, d_shift, d_local)

def back_project(grad_flat, weight):
    return jnp.dot(grad_flat, weight.astype(jnp.float32).T, precision=FULL_PRECISION)

def upstream(gradient, w_out, head_count, head_size, value_points):
    amount = gradient.shape[0]
    joined = jnp.dot(gradient, w_out.astype(jnp.float32).T, precision=FULL_PRECISION)
    first_end = head_count * head_size
    second_end = first_end + 3 * head_count * value_points
    third_end = second_end + head_count * value_points
    out_plain = joined[:, :first_end].reshape(amount, head_count, head_size)
    out_points = joined[:, first_end:second_end].reshape(amount, 3, head_count * value_points)
    out_norm = joined[:, second_end:third_end]
    out_pair = joined[:, third_end:].reshape(amount, head_count, -1)
    return (out_plain, out_points, out_norm, out_pair)

def norm_points(rotation, offset_pts, out_points, out_norm):
    local_out = jnp.einsum('abn,nak->nbk', rotation, offset_pts, precision=FULL_PRECISION)
    length = jnp.sqrt(lax.optimization_barrier(jnp.sum(local_out * local_out, axis=1)) + NORM_EPS)
    return out_points + out_norm[:, None, :] * local_out / length[:, None, :]

def masked_attention(probs_now, chains, links, start, block_size):
    chain_rows = lax.dynamic_slice_in_dim(chains, start, block_size, 0)
    same_chain = (chain_rows[:, None] == chains[None, :]).astype(jnp.float32)
    linked = links[chain_rows][:, chains].astype(jnp.float32)
    mask_float = jnp.maximum(same_chain, linked)
    masked = lax.dynamic_slice_in_dim(probs_now, start, block_size, 1).astype(jnp.float32) * mask_float[None]
    return masked / lax.optimization_barrier(jnp.sum(masked, axis=2, keepdims=True))

def block_terms(probs_now, pair, chains, links, start, block_size, value_parts, upper_parts, pair_up, logit_scale):
    attention = masked_attention(probs_now, chains, links, start, block_size)
    pair_rows = lax.dynamic_slice_in_dim(pair, start, block_size, 0).astype(jnp.float32)
    upper_rows = lax.dynamic_slice_in_dim(upper_parts, start, block_size, 0)
    pair_up_rows = lax.dynamic_slice_in_dim(pair_up, start, block_size, 0).astype(jnp.float32)
    d_attention = jnp.einsum('ihf,jhf->hij', upper_rows, value_parts, precision=FULL_PRECISION)
    d_attention = d_attention + jnp.einsum('ihc,ijc->hij', pair_up_rows, pair_rows, precision=FULL_PRECISION)
    row_dots = lax.optimization_barrier(jnp.sum(attention * d_attention, axis=2, keepdims=True))
    d_logits = logit_scale * attention * (d_attention - row_dots)
    return (attention, d_logits)

def reference(single, frames, saved_probs, pair, cotangent, chains, links, w_query, w_key, w_value, w_query_points, w_key_points, w_value_points, w_bias, w_out, head_weights):
    logit_scale = math.sqrt(1.0 / 3.0)
    plain_scale = 1.0 / math.sqrt(HD)
    point_scale = jax.nn.softplus(head_weights) * math.sqrt(2.0 / (9.0 * PQ))
    block_size = math.gcd(N, 128)
    block_total = N // block_size
    gradient = cotangent
    total_single = jnp.zeros((N, C), jnp.float32)
    frame_list = [None] * ITERS
    stored = [None] * ITERS
    for iteration in reversed(range(ITERS)):
        rotation, shift_vec = split_frames(frames[iteration])
        query_plain, query_local, query_placed = project(single[iteration], rotation, shift_vec, w_query, w_query_points, H)
        key_plain, key_local, key_placed = project(single[iteration], rotation, shift_vec, w_key, w_key_points, H)
        value_plain, value_local, value_placed = project(single[iteration], rotation, shift_vec, w_value, w_value_points, H)
        query_parts = jnp.concatenate([query_plain, by_head(query_placed, H)], axis=2)
        key_parts = jnp.concatenate([key_plain, by_head(key_placed, H)], axis=2)
        value_heads = by_head(value_placed, H)
        value_parts = jnp.concatenate([value_plain, value_heads], axis=2)
        probs_now = saved_probs[iteration]

        def attend_block(index_now):
            start = (index_now * block_size).astype(jnp.int32)
            attention = masked_attention(probs_now, chains, links, start, block_size)
            return jnp.einsum('hij,jhf->ihf', attention, value_heads, precision=FULL_PRECISION)
        point_sum = lax.map(attend_block, jnp.arange(block_total).astype(jnp.int32)).reshape(N, H, -1)
        offset_pts = by_component(point_sum, H) - shift_vec.T[:, :, None]
        out_plain, out_points, out_norm, out_pair = upstream(gradient, w_out, H, HD, PV)
        out_points = norm_points(rotation, offset_pts, out_points, out_norm)
        turned = jnp.einsum('abn,nbk->nak', rotation, out_points, precision=FULL_PRECISION)
        upper_parts = jnp.concatenate([out_plain, by_head(turned, H)], axis=2)
        pair_up = out_pair.astype(jnp.bfloat16)
        stored[iteration] = (value_parts, upper_parts, pair_up)

        def scan_block(carry, index_now):
            key_acc, column_acc, value_acc = carry
            start = (index_now * block_size).astype(jnp.int32)
            attention, d_logits = block_terms(probs_now, pair, chains, links, start, block_size, value_parts, upper_parts, pair_up, logit_scale)
            query_raw = jnp.einsum('hij,jhf->ihf', d_logits, key_parts, precision=FULL_PRECISION)
            query_rows = lax.dynamic_slice_in_dim(query_parts, start, block_size, 0)
            upper_rows = lax.dynamic_slice_in_dim(upper_parts, start, block_size, 0)
            key_acc = key_acc + jnp.einsum('hij,ihf->jhf', d_logits, query_rows, precision=FULL_PRECISION)
            column_acc = column_acc + lax.optimization_barrier(jnp.sum(d_logits, axis=1))
            value_acc = value_acc + jnp.einsum('hij,ihf->jhf', attention, upper_rows, precision=FULL_PRECISION)
            return ((key_acc, column_acc, value_acc), query_raw)
        initial = (jnp.zeros((N, H, HD + 3 * PQ), jnp.float32), jnp.zeros((H, N), jnp.float32), jnp.zeros((N, H, HD + 3 * PV), jnp.float32))
        (key_raw, column_sums, value_raw), query_raw = lax.scan(scan_block, initial, jnp.arange(block_total).astype(jnp.int32))
        query_raw = query_raw.reshape(N, H, -1)
        d_query = plain_scale * query_raw[:, :, :HD]
        d_query_pts = by_component(point_scale[None, :, None] * query_raw[:, :, HD:], H)
        d_key = plain_scale * key_raw[:, :, :HD]
        d_key_pts = by_component(point_scale[None, :, None] * (key_raw[:, :, HD:] - column_sums.T[:, :, None] * by_head(key_placed, H)), H)
        d_value = value_raw[:, :, :HD]
        d_value_pts = by_component(value_raw[:, :, HD:], H)
        query_rotation_grad, query_shift_grad, query_local_grad = frame_grad(rotation, query_local, d_query_pts)
        key_rotation_grad, key_shift_grad, key_local_grad = frame_grad(rotation, key_local, d_key_pts)
        value_rotation_grad, value_shift_grad, value_local_grad = frame_grad(rotation, value_local, d_value_pts)
        out_rotation_grad = jnp.einsum('nak,nbk->abn', offset_pts, out_points, precision=FULL_PRECISION).reshape(9, N)
        out_shift_grad = -lax.optimization_barrier(jnp.sum(turned, axis=2)).T
        frame_list[iteration] = jnp.concatenate([query_rotation_grad + key_rotation_grad + value_rotation_grad + out_rotation_grad, query_shift_grad + key_shift_grad + value_shift_grad + out_shift_grad], axis=0)
        layer_single = back_project(d_query.reshape(N, -1), w_query) + back_project(d_key.reshape(N, -1), w_key)
        layer_single = layer_single + back_project(d_value.reshape(N, -1), w_value)
        layer_single = layer_single + back_project(query_local_grad.reshape(N, -1), w_query_points)
        layer_single = layer_single + back_project(key_local_grad.reshape(N, -1), w_key_points)
        layer_single = layer_single + back_project(value_local_grad.reshape(N, -1), w_value_points)
        gradient = gradient + layer_single
        total_single = total_single + layer_single
    bias_float = w_bias.astype(jnp.float32)

    def pair_block(unused, index_now):
        start = (index_now * block_size).astype(jnp.int32)
        summed = jnp.zeros((block_size, N, CZ), jnp.float32)
        for iteration in range(ITERS):
            value_parts, upper_parts, pair_up = stored[iteration]
            attention, d_logits = block_terms(saved_probs[iteration], pair, chains, links, start, block_size, value_parts, upper_parts, pair_up, logit_scale)
            attention_b = lax.optimization_barrier(attention.astype(jnp.bfloat16)).astype(jnp.float32)
            logits_b = lax.optimization_barrier(d_logits.astype(jnp.bfloat16)).astype(jnp.float32)
            pair_up_rows = lax.dynamic_slice_in_dim(pair_up, start, block_size, 0).astype(jnp.float32)
            summed = summed + jnp.einsum('hij,ihc->ijc', attention_b, pair_up_rows, precision=FULL_PRECISION)
            summed = summed + jnp.einsum('hij,ch->ijc', logits_b, bias_float, precision=FULL_PRECISION)
        return (unused, summed.astype(jnp.bfloat16))
    unused_out, pair_blocks = lax.scan(pair_block, jnp.zeros((), jnp.float32), jnp.arange(block_total).astype(jnp.int32))
    return (total_single, jnp.stack(frame_list), pair_blocks.reshape(N, N, CZ))
```

```python
import functools
import math

import jax
import jax.numpy as jnp
from jax import lax
from jax.experimental import pallas as pl
from jax.experimental.pallas import tpu as pltpu
from jax.sharding import PartitionSpec as P

C = 384
H = 12
HD = 16
CZ = 128
PQ = 4
PV = 8
NCHAIN = 16
NORM_EPS = 1e-08
LOGIT_SCALE = math.sqrt(1.0 / 3.0)
PLAIN_SCALE = 1.0 / math.sqrt(HD)
POINT_SCALE = math.sqrt(2.0 / (9.0 * PQ))

LANES = 640
PACK = 896
FRAME_LANE = 768
CHAIN_LANE = 792
STAT = 96

F32 = jnp.float32
BF16 = jnp.bfloat16
NN = (((1,), (0,)), ((), ()))
NT = (((1,), (1,)), ((), ()))
TN = (((0,), (0,)), ((), ()))


def mm(a, b, dims=NN):
    return lax.dot_general(a, b, dims, preferred_element_type=F32)


def split(x):
    hi = x.astype(BF16)
    return hi, (x - hi.astype(F32)).astype(BF16)


def mm2(x, w, dims=NN):
    hi, lo = split(x)
    rows = x.shape[0]
    both = mm(jnp.concatenate([hi, lo], axis=0), w, dims)
    return both[:rows] + both[rows:]


def mm3(ah, al, bh, bl, dims=NN):
    return mm(ah, bh, dims) + mm(ah, bl, dims) + mm(al, bh, dims)


def iota(shape, axis):
    return lax.broadcasted_iota(jnp.int32, shape, axis)


def key_heads(rows):
    lane = iota((rows, LANES), 1)
    return jnp.where(lane < 256, lane >> 4, (lane & 127) >> 2)


def value_heads(rows):
    lane = iota((rows, LANES), 1)
    inner = lane & 127
    points = jnp.where(inner < STAT, inner >> 3, inner - STAT)
    return jnp.where(lane < 256, lane >> 4, points)


def pick(full, heads, rows):
    out = None
    for h in range(H):
        part = jnp.where(heads == h, full[h * rows : (h + 1) * rows], 0.0)
        out = part if out is None else out + part
    return out


def spread(x, heads):
    return jnp.concatenate([jnp.where(heads == h, x, 0.0) for h in range(H)], axis=0)


def spread2(x, heads):
    hi, lo = split(x)
    hi32, lo32 = hi.astype(F32), lo.astype(F32)
    return spread(hi32, heads).astype(BF16), spread(lo32, heads).astype(BF16)


def columns(frames_block, first):
    cols = [frames_block[:, first + n : first + n + 1] for n in range(12)]
    return [[cols[3 * a + b] for b in range(3)] for a in range(3)], cols[9:]


def block(x, a):
    return x[:, 256 + 128 * a : 384 + 128 * a]


def rotate(rot, pts):
    return [sum(rot[a][b] * pts[b] for b in range(3)) for a in range(3)]


def unrotate(rot, pts):
    return [sum(rot[a][b] * pts[a] for a in range(3)) for b in range(3)]


def place(rot, shift, flat):
    local_pts = [block(flat, a) for a in range(3)]
    turned = rotate(rot, local_pts)
    return jnp.concatenate(
        [flat[:, :256]] + [turned[a] + shift[a] for a in range(3)], axis=1
    )


def lane_matrix(rows, fn):
    r = iota((rows, 128), 0)
    c = iota((rows, 128), 1)
    return (fn(r) == c).astype(F32).astype(BF16)


def upstream_parts(g, w_out_ref, gp_ref, pu_ref, rows):
    hi, lo = split(g)
    both = jnp.concatenate([hi, lo], axis=0)

    def part(first, count):
        r = mm(both, w_out_ref[first : first + count, :], NT)
        return r[:rows] + r[rows:]

    gp_ref[...] = jnp.zeros(gp_ref.shape, F32)
    gp_ref[:, 0:192] = part(0, 192)
    for a in range(4):
        gp_ref[:, 256 + 128 * a : 352 + 128 * a] = part(192 + 96 * a, 96)
    wide = part(576, H * CZ)
    for h in range(H):
        pu_ref[h * rows : (h + 1) * rows, :] = (
            wide[:, h * CZ : (h + 1) * CZ].astype(BF16).astype(F32)
        )


def pair_products(pu_ref, pair_ref, d_ref, rows):
    for i in range(rows):
        lhs = pu_ref[pl.ds(i, H, stride=rows), :].astype(BF16)
        d_ref[pl.ds(i, H, stride=rows), :] = mm(lhs, pair_ref[i], NT)


def prep_body(
    hw_ref, pack_ref, cot_ref, wq_ref, wk_ref, wv_ref, wqp_ref, wkp_ref, wvp_ref, w_out_ref, pair_ref,
    wk_out, wq_out, gp_ref, q1_ref, q0_ref, pu_ref, d_ref, sc_ref,
):
    rows = pack_ref.shape[0]
    upstream_parts(cot_ref[...], w_out_ref, gp_ref, pu_ref, rows)
    pair_products(pu_ref, pair_ref, d_ref, rows)
    wq_out[...] = jnp.zeros(wq_out.shape, BF16)
    wk_out[...] = jnp.zeros(wk_out.shape, BF16)
    wq_out[:, 0:192] = wq_ref[...]
    wk_out[:, 0:192] = wk_ref[...]
    wk_out[:, 640:832] = wv_ref[...]
    for a in range(3):
        wq_out[:, 256 + 128 * a : 304 + 128 * a] = wqp_ref[:, 48 * a : 48 * a + 48]
        wk_out[:, 256 + 128 * a : 304 + 128 * a] = wkp_ref[:, 48 * a : 48 * a + 48]
        wk_out[:, 896 + 128 * a : 992 + 128 * a] = wvp_ref[:, 96 * a : 96 * a + 96]
    lane = iota((8, 128), 1)
    raw = jnp.zeros((8, 128), F32)
    for h in range(H):
        raw = jnp.where((lane >> 2) == h, hw_ref[h], raw)
    soft = jnp.maximum(raw, 0.0) + jnp.log(1.0 + jnp.exp(-jnp.abs(raw)))
    sc_ref[...] = soft * POINT_SCALE
    fr = pack_ref[:, FRAME_LANE : FRAME_LANE + 128]
    for out, first, fcol in ((q1_ref, 0, 0), (q0_ref, C, 12)):
        flat = mm2(pack_ref[:, first : first + C], wq_out[...])
        rot, shift = columns(fr, fcol)
        out[:, :LANES] = place(rot, shift, flat)
        out[:, LANES:] = flat[:, 256:]


def project_keys(x, fr, fcol, wk_ref, kv_ref):
    flat = mm2(x, wk_ref[...])
    rot, shift = columns(fr, fcol)
    kv_ref[:, 0:640] = place(rot, shift, flat[:, :640])
    kv_ref[:, 640:1280] = place(rot, shift, flat[:, 640:])
    kv_ref[:, 1280:1664] = flat[:, 256:640]
    kv_ref[:, 1664:2048] = flat[:, 896:1280]


def value_sums(probs, kv_ref, rows):
    values = kv_ref[:, 640:1280]
    lane = iota(values.shape, 1)
    values = jnp.where((lane >= 256 + STAT) & (lane < 256 + STAT + H), 1.0, values)
    hi, lo = split(values)
    return pick(mm(probs, hi) + mm(probs, lo), value_heads(rows), rows)


def head_dots(prod, rows):
    return mm2(prod, lane_matrix(256, lambda r: STAT + (r >> 4)))


def first_body(
    flag_ref, own_ref, ownx_ref, p1_ref, p1x_ref, p2_ref, p2x_ref, wk_ref, links_ref, probs_ref, gp_ref, d_ref,
    keys_ref, kv_ref, pm_ref, e_ref,
):
    rows = own_ref.shape[0]
    home = flag_ref[0] == 1
    zb = flag_ref[1]
    core = flag_ref[2]

    def put(z, k, value):
        keys_ref[pl.ds(pl.multiple_of((2 * z + k) * rows, rows), rows), :] = value

    put(zb, core, jnp.where(home, own_ref[...], p1_ref[...]))
    put(zb, 1 - core, jnp.where(home, ownx_ref[...], p1x_ref[...]))
    put(1 - zb, core, jnp.where(home, p1_ref[...], p2_ref[...]))
    put(1 - zb, 1 - core, jnp.where(home, p1x_ref[...], p2x_ref[...]))
    fr = keys_ref[:, FRAME_LANE : FRAME_LANE + 128]
    keys = fr.shape[0]
    at = CHAIN_LANE - FRAME_LANE
    key_chain = fr[:, at : at + 1]
    own_chain = own_ref[:, FRAME_LANE : FRAME_LANE + 128][:, at : at + 1]
    key_hot = (iota((keys, NCHAIN), 1).astype(F32) == key_chain).astype(F32).astype(BF16)
    own_hot = (iota((rows, NCHAIN), 1).astype(F32) == own_chain).astype(F32).astype(BF16)
    eye = iota((NCHAIN, NCHAIN), 0) == iota((NCHAIN, NCHAIN), 1)
    allowed = jnp.where(eye, 1.0, links_ref[...].astype(F32)).astype(BF16)
    mask = mm(mm(own_hot, allowed).astype(BF16), key_hot, NT)
    mask_all = jnp.concatenate([mask] * H, axis=0)
    for l in range(2):
        pm_ref[l] = (probs_ref[l].astype(F32) * mask_all).astype(BF16)
    project_keys(keys_ref[:, 0:C], fr, 0, wk_ref, kv_ref)
    probs = pm_ref[1]
    sums = value_sums(probs, kv_ref, rows)
    weighted = mm2(probs.astype(F32) * d_ref[...], jnp.ones((keys, 128), BF16))
    lane = iota((rows, 128), 1)
    dots = pick(weighted, lane - STAT, rows) + head_dots(gp_ref[:, 0:256] * sums[:, 0:256], rows)
    e_ref[:, 0:128] = block(sums, 0)
    e_ref[:, 128:256] = jnp.where(lane < STAT, block(sums, 1), dots)
    e_ref[:, 256:384] = block(sums, 2)


def second_body(keys_ref, wk_ref, pm_ref, pair_ref, kv_ref, e_ref, p32_ref, op_ref):
    rows = pair_ref.shape[0]
    fr = keys_ref[:, FRAME_LANE : FRAME_LANE + 128]
    project_keys(keys_ref[:, C : 2 * C], fr, 12, wk_ref, kv_ref)
    probs = pm_ref[0]
    sums = value_sums(probs, kv_ref, rows)
    for a in range(3):
        e_ref[:, 128 * a : 128 * a + 128] = block(sums, a)
    e_ref[:, 384:640] = sums[:, 0:256]
    p32_ref[...] = probs.astype(F32)
    for i in range(rows):
        lhs = p32_ref[pl.ds(i, H, stride=rows), :].astype(BF16)
        op_ref[pl.ds(i, H, stride=rows), :] = mm(lhs, pair_ref[i])
    for h in range(H):
        e_ref[:, 640 + CZ * h : 640 + CZ * (h + 1)] = op_ref[h * rows : (h + 1) * rows, :]


def backward(
    flag_ref, e, dots, probs, kv_ref, key_fr, own_fr, fcol, q_ref, gp, d_ref, wk_ref, wq_ref, sc, shift_lane,
    share, z_ref, keys_out_ref,
):
    rows = e.shape[0]
    lane = iota((rows, 128), 1)
    stat = (lane >= STAT) & (lane < STAT + H)
    inv = jnp.where(stat, 1.0 / jnp.where(stat, e[:, 0:128], 1.0), 0.0)
    r128 = iota((128, LANES), 0)
    grow = (r128 - STAT == value_heads(128)) & ((iota((128, LANES), 1) & 127) < STAT)
    grow = grow | ((r128 - STAT == (iota((128, LANES), 1) >> 4)) & (iota((128, LANES), 1) < 256))
    inv_lanes = mm2(inv, grow.astype(F32).astype(BF16))
    rot, shift = columns(own_fr, fcol)
    inv_pts = block(inv_lanes, 0)
    ptg = [e[:, 128 * a : 128 * a + 128] * inv_pts for a in range(3)]
    off = [jnp.where(lane < STAT, ptg[a] - shift[a], 0.0) for a in range(3)]
    opt = unrotate(rot, off)
    length = jnp.sqrt(opt[0] * opt[0] + opt[1] * opt[1] + opt[2] * opt[2] + NORM_EPS)
    scale = gp[:, 640:768] / length
    gpt = [block(gp, a) + scale * opt[a] for a in range(3)]
    gptg = rotate(rot, gpt)
    upper = jnp.concatenate([gp[:, 0:256]] + gptg, axis=1)
    point_dots = gptg[0] * ptg[0] + gptg[1] * ptg[1] + gptg[2] * ptg[2]
    rd = dots * inv + mm2(point_dots, lane_matrix(128, lambda r: STAT + (r >> 3)))
    both = jnp.concatenate([spread(rd, lane - STAT), spread(inv, lane - STAT)], axis=0)
    wide = mm2(both, jnp.ones((128, 128), BF16))
    rd_all, inv_all = wide[: H * rows], wide[H * rows :]
    heads_v = value_heads(rows)
    heads_k = key_heads(rows)
    uh, ul = spread2(upper, heads_v)
    vh, vl = split(kv_ref[:, 640:1280])
    d_att = d_ref[...] + mm3(uh, ul, vh, vl, NT)
    p32 = probs.astype(F32)
    att = p32 * inv_all
    dl = LOGIT_SCALE * att * (d_att - rd_all)
    z_ref[0 : H * rows, :] = att
    z_ref[H * rows :, :] = dl
    dh, dlo = split(dl)
    kh, klo = split(kv_ref[:, 0:640])
    qr = pick(mm3(dh, dlo, kh, klo), heads_k, rows)
    d_qg = [sc * block(qr, a) for a in range(3)]
    d_ql = unrotate(rot, d_qg)
    query_grad = mm2(jnp.concatenate([PLAIN_SCALE * qr[:, 0:256]] + d_ql, axis=1), wq_ref[...], NT)
    q_local = [q_ref[:, 640 + 128 * b : 768 + 128 * b] for b in range(3)]
    prods = [d_qg[a] * q_local[b] + share * off[a] * gpt[b] for a in range(3) for b in range(3)]
    prods = prods + [d_qg[a] - share * gptg[a] for a in range(3)]
    gather12 = lane_matrix(12 * 128, lambda r: shift_lane + (r >> 7))
    query_frames = mm2(jnp.concatenate(prods, axis=1), gather12)
    dt = jnp.transpose(dl)
    th, tl = split(dt)
    qh, qlo = spread2(q_ref[:, 0:640], heads_k)
    kr = mm3(th, tl, qh, qlo)
    head_rows = iota((H * rows, 128), 0) // rows
    hot = ((iota((H * rows, 128), 1) >> 2) == head_rows).astype(F32).astype(BF16)
    cs = mm(th, hot) + mm(tl, hot)
    pt = jnp.transpose(p32).astype(BF16)
    sh, sl = spread2(upper * inv_lanes, heads_v)
    vr = mm(pt, sh) + mm(pt, sl)
    krot, _ = columns(key_fr, fcol)
    d_kg = [sc * (block(kr, a) - cs * kv_ref[:, 256 + 128 * a : 384 + 128 * a]) for a in range(3)]
    d_vg = [block(vr, a) for a in range(3)]
    d_kl = unrotate(krot, d_kg)
    d_vl = unrotate(krot, d_vg)
    flat = jnp.concatenate([PLAIN_SCALE * kr[:, 0:256]] + d_kl + [vr[:, 0:256]] + d_vl, axis=1)
    keys_out_ref[:, 0:C] = mm2(flat, wk_ref[...], NT)
    k_local = [kv_ref[:, 1280 + 128 * b : 1408 + 128 * b] for b in range(3)]
    v_local = [kv_ref[:, 1664 + 128 * b : 1792 + 128 * b] for b in range(3)]
    kprods = [d_kg[a] * k_local[b] + d_vg[a] * v_local[b] for a in range(3) for b in range(3)]
    kprods = kprods + [d_kg[a] + d_vg[a] for a in range(3)]
    key_frames = mm2(jnp.concatenate(kprods, axis=1), gather12)
    return query_grad, query_frames, key_frames


def send_blocks(flag_ref, src_ref, mine_a, mine_b, theirs, rows):
    zb = flag_ref[1]
    core = flag_ref[2]

    def get(z, k):
        return src_ref[pl.ds(pl.multiple_of((2 * z + k) * rows, rows), rows), :]

    mine_a[...] = get(zb, core)
    mine_b[...] = get(1 - zb, core)
    theirs[0:rows, :] = get(zb, 1 - core)
    theirs[rows:, :] = get(1 - zb, 1 - core)


def back_one_body(
    share, flag_ref, e_mine, e_other, pm_ref, kv_ref, keys_ref, own_ref, q_ref, gp_ref, d_ref, wk_ref, wq_ref, sc_ref,
    z_ref, mine_a, mine_b, theirs, query_out, frk_ref, frq_ref, work_ref,
):
    rows = own_ref.shape[0]
    e = e_mine[...] + e_other[...]
    query_grad, query_frames, key_frames = backward(
        flag_ref, e, e[:, 128:256], pm_ref[1], kv_ref, keys_ref[:, FRAME_LANE : FRAME_LANE + 128],
        own_ref[:, FRAME_LANE : FRAME_LANE + 128], 0, q_ref, gp_ref[...], d_ref, wk_ref, wq_ref, sc_ref[0:1, :], 12,
        share, z_ref, work_ref,
    )
    query_out[...] = query_grad
    frq_ref[...] = query_frames
    frk_ref[...] = key_frames
    send_blocks(flag_ref, work_ref, mine_a, mine_b, theirs, rows)


def back_zero_body(
    share, flag_ref, cot_ref, r0, r1, r2, r3, r4, r5, e_mine, e_other, pm_ref, kv_ref, keys_ref, own_ref, q_ref, pair_ref,
    w_out_ref, wk_ref, wq_ref, sc_ref, frk_ref, frq_ref,
    z_ref, mine_a, mine_b, theirs, query_out, sum_ref, pu_ref, work_ref, gp_ref, d_ref,
):
    rows = own_ref.shape[0]
    total = (r0[...] + r1[...]) + (r2[...] + r3[...]) + (r4[...] + r5[...])
    sum_ref[...] = total
    upstream_parts(cot_ref[...] + total, w_out_ref, gp_ref, pu_ref, rows)
    pair_products(pu_ref, pair_ref, d_ref, rows)
    gp = gp_ref[...]
    e = e_mine[:, 0:384] + e_other[:, 0:384]
    plain = e_mine[:, 384:640] + e_other[:, 384:640]
    dots = head_dots(gp[:, 0:256] * plain, rows)
    wide = jnp.concatenate(
        [
            pu_ref[h * rows : (h + 1) * rows, :]
            * (e_mine[:, 640 + CZ * h : 640 + CZ * (h + 1)] + e_other[:, 640 + CZ * h : 640 + CZ * (h + 1)])
            for h in range(H)
        ],
        axis=1,
    )
    dots = dots + mm2(wide, lane_matrix(H * CZ, lambda r: STAT + (r >> 7)))
    query_grad, query_frames, key_frames = backward(
        flag_ref, e, dots, pm_ref[0], kv_ref, keys_ref[:, FRAME_LANE : FRAME_LANE + 128],
        own_ref[:, FRAME_LANE : FRAME_LANE + 128], 12, q_ref, gp, d_ref, wk_ref, wq_ref, sc_ref[0:1, :], 0,
        share, z_ref, work_ref,
    )
    query_out[:, 0:C] = query_grad
    query_out[:, C:] = query_frames + frq_ref[...]
    work_ref[:, C:] = key_frames + frk_ref[...]
    send_blocks(flag_ref, work_ref, mine_a, mine_b, theirs, rows)


def pair_body(z1_ref, z0_ref, pu1_ref, pu0_ref, wbt_ref, out_ref):
    rows = out_ref.shape[0]
    wbt = wbt_ref[...].astype(F32)
    for i in range(rows):
        left = jnp.concatenate(
            [z1_ref[pl.ds(i, 2 * H, stride=rows), :], z0_ref[pl.ds(i, 2 * H, stride=rows), :]], axis=0
        )
        right = jnp.concatenate(
            [pu1_ref[pl.ds(i, H, stride=rows), :], wbt, pu0_ref[pl.ds(i, H, stride=rows), :], wbt], axis=0
        ).astype(BF16)
        out_ref[i] = mm(left.astype(BF16), right, TN).astype(BF16)


VMEM = pl.BlockSpec(memory_space=pltpu.VMEM)
SMEM = pl.BlockSpec(memory_space=pltpu.SMEM)


def call(body, name, in_specs, outs, args, scratch=()):
    return pl.pallas_call(
        body,
        name=name,
        in_specs=in_specs,
        out_specs=tuple(VMEM for _ in outs),
        out_shape=tuple(jax.ShapeDtypeStruct(s, d) for s, d in outs),
        scratch_shapes=list(scratch),
        compiler_params=pltpu.CompilerParams(vmem_limit_bytes=32 * 1024 * 1024),
    )(*args)


def joint(pairs):
    return [
        ((a * 2 + k) * 2 + x, (b * 2 + k) * 2 + y) for (x, a), (y, b) in pairs for k in range(2)
    ]


BOTH = ("row", "col")
FETCH_ONE = joint([((0, 0), (0, 1)), ((0, 1), (0, 0)), ((1, 0), (0, 2)), ((1, 1), (0, 3)), ((1, 2), (1, 3)), ((1, 3), (1, 2)), ((0, 2), (1, 0)), ((0, 3), (1, 1))])
FETCH_TWO = joint([((0, 0), (0, 3)), ((0, 1), (0, 2)), ((1, 2), (1, 1)), ((1, 3), (1, 0))])
SCATTER = [
    joint([((x, z), (((s ^ z) >> 1) & 1, 2 * x + ((s ^ z) & 1))) for x in range(2) for z in range(4)])
    for s in range(4)
]
CORE_SWAP = [(i, i ^ 1) for i in range(8)]
COL_SWAP = [(0, 1), (1, 0)]


def local(
    single, frames, saved_probs, pair, cotangent, chains, links, w_query, w_key, w_value, w_query_points,
    w_key_points, w_value_points, w_bias, w_out, head_weights,
):
    rows = single.shape[1]
    keys = pair.shape[1]
    row_total = lax.axis_size("row")
    col_total = lax.axis_size("col")
    fast = row_total == 8 and col_total == 2 and keys == 4 * rows
    small = jnp.concatenate([frames[1], frames[0], chains[None].astype(F32)], axis=0)
    pack = jnp.concatenate(
        [single[1], single[0], small.T, jnp.zeros((rows, PACK - CHAIN_LANE - 1), F32)], axis=1
    )
    col = lax.axis_index("col")
    row = lax.axis_index("row")
    if fast:
        home = (row // 4 == col).astype(jnp.int32)
        flags = jnp.stack([home, (row // 2) % 2, row % 2])
        ownx = lax.ppermute(pack, "row", CORE_SWAP)
        one = lax.ppermute(pack, BOTH, FETCH_ONE)
        two = lax.ppermute(pack, BOTH, FETCH_TWO)
        blocks = (pack, ownx, one, lax.ppermute(one, "row", CORE_SWAP), two, lax.ppermute(two, "row", CORE_SWAP))
        own = pack
    else:
        flags = jnp.array([1, 0, 0], jnp.int32)
        whole = lax.all_gather(pack, "row", axis=0, tiled=True)
        mine = lax.dynamic_slice_in_dim(whole, col * keys, keys, 0)
        quarter = keys // 4
        blocks = tuple(mine[quarter * n : quarter * (n + 1)] for n in (0, 1, 2, 3, 0, 0))
        own = pack

    def col_other(x):
        if col_total == 2:
            return lax.ppermute(x, "col", COL_SWAP)
        return lax.psum(x, "col") - x

    def reduce(mine_a, mine_b, theirs, query):
        if fast:
            query_other = lax.ppermute(query, "col", COL_SWAP)
            got = lax.ppermute(theirs, "row", CORE_SWAP)
            part = (mine_a + got[:rows], mine_b + got[rows:])
            return [query, query_other] + [lax.ppermute(part[s & 1], BOTH, SCATTER[s]) for s in range(4)]
        parts = jnp.concatenate([mine_a, theirs[:rows], mine_b, theirs[rows:]], axis=0)
        summed = lax.all_gather(lax.psum(parts, "row"), "col", axis=0, tiled=True)
        zero = jnp.zeros_like(query)
        back = lax.dynamic_slice_in_dim(summed, row * rows, rows, 0)
        return [lax.psum(query, "col"), back, zero, zero, zero, zero]

    probs = saved_probs.reshape(2, H * rows, keys)
    hr = H * rows
    wk, wq, gp1, q1, q0, pu1, d1, sc = call(
        prep_body, "prep", [SMEM] + [VMEM] * 10,
        [((C, 1280), BF16), ((C, LANES), BF16), ((rows, 768), F32), ((rows, 1024), F32), ((rows, 1024), F32),
         ((hr, CZ), F32), ((hr, keys), F32), ((8, 128), F32)],
        (head_weights, own, cotangent, w_query, w_key, w_value, w_query_points, w_key_points, w_value_points, w_out, pair),
    )
    key_pack, kv1, pm, e1 = call(
        first_body, "first", [SMEM] + [VMEM] * 11,
        [((keys, PACK), F32), ((keys, 2048), F32), ((2, hr, keys), BF16), ((rows, 384), F32)],
        (flags, *blocks, wk, links, probs, gp1, d1),
    )
    e1_other = col_other(e1)
    kv0, e0 = call(
        second_body, "second", [VMEM] * 4,
        [((keys, 2048), F32), ((rows, 640 + H * CZ), F32)],
        (key_pack, wk, pm, pair),
        [pltpu.VMEM((hr, keys), F32), pltpu.VMEM((hr, CZ), F32)],
    )
    e0_other = col_other(e0)
    z1, mine_a, mine_b, theirs, query, frk, frq = call(
        functools.partial(back_one_body, 1.0 / col_total), "back_one", [SMEM] + [VMEM] * 12,
        [((2 * hr, keys), F32), ((rows, C), F32), ((rows, C), F32), ((2 * rows, C), F32), ((rows, C), F32),
         ((keys, 128), F32), ((rows, 128), F32)],
        (flags, e1, e1_other, pm, kv1, key_pack, own, q1, gp1, d1, wk, wq, sc),
        [pltpu.VMEM((keys, C), F32)],
    )
    pieces = reduce(mine_a, mine_b, theirs, query)
    z0, mine_a, mine_b, theirs, query, single_one, pu0 = call(
        functools.partial(back_zero_body, 1.0 / col_total), "back_zero", [SMEM] + [VMEM] * 21,
        [((2 * hr, keys), F32), ((rows, 512), F32), ((rows, 512), F32), ((2 * rows, 512), F32), ((rows, 512), F32),
         ((rows, C), F32), ((hr, CZ), F32)],
        (flags, cotangent, *pieces, e0, e0_other, pm, kv0, key_pack, own, q0, pair, w_out, wk, wq, sc, frk, frq),
        [pltpu.VMEM((keys, 512), F32), pltpu.VMEM((rows, 768), F32), pltpu.VMEM((hr, keys), F32)],
    )
    pieces = reduce(mine_a, mine_b, theirs, query)
    (d_pair,) = call(
        pair_body, "pair_grad", [VMEM] * 5, [((rows, keys, CZ), BF16)], (z1, z0, pu1, pu0, w_bias.T)
    )
    total = sum(pieces)
    d_frames = total[:, C : C + 24].T.reshape(2, 12, rows)
    return (single_one + total[:, :C], d_frames, d_pair)


def solution(mesh):
    return jax.shard_map(
        local,
        mesh=mesh,
        in_specs=(
            P(None, ("grp", "row"), None),
            P(None, None, ("grp", "row")),
            P(None, None, ("grp", "row"), "col"),
            P(("grp", "row"), "col", None),
            P(("grp", "row"), None),
            P(("grp", "row")),
            P("grp", None),
            P(),
            P(),
            P(),
            P(),
            P(),
            P(),
            P(),
            P(),
            P(),
        ),
        out_specs=(
            P(("grp", "row"), None),
            P(None, None, ("grp", "row")),
            P(("grp", "row"), "col", None),
        ),
        check_vma=False,
    )
```

```python
import functools
import math

import jax
import jax.numpy as jnp
from jax import lax
from jax.experimental import pallas as pl
from jax.experimental.pallas import tpu as pltpu
from jax.sharding import PartitionSpec as P

C = 384
H = 12
HD = 16
CZ = 128
PQ = 4
PV = 8
NCHAIN = 16
NORM_EPS = 1e-08
LOGIT_SCALE = math.sqrt(1.0 / 3.0)
PLAIN_SCALE = 1.0 / math.sqrt(HD)
POINT_SCALE = math.sqrt(2.0 / (9.0 * PQ))

LANES = 640
PACK = 896
FRAME_LANE = 768
CHAIN_LANE = 792
STAT = 96

F32 = jnp.float32
BF16 = jnp.bfloat16
NN = (((1,), (0,)), ((), ()))
NT = (((1,), (1,)), ((), ()))
TN = (((0,), (0,)), ((), ()))


def mm(a, b, dims=NN):
    return lax.dot_general(a, b, dims, preferred_element_type=F32)


def split(x):
    hi = x.astype(BF16)
    return hi, (x - hi.astype(F32)).astype(BF16)


def mm2(x, w, dims=NN):
    hi, lo = split(x)
    rows = x.shape[0]
    both = mm(jnp.concatenate([hi, lo], axis=0), w, dims)
    return both[:rows] + both[rows:]


def mm3(ah, al, bh, bl, dims=NN):
    return mm(ah, bh, dims) + mm(ah, bl, dims) + mm(al, bh, dims)


def iota(shape, axis):
    return lax.broadcasted_iota(jnp.int32, shape, axis)


def key_heads(rows):
    lane = iota((rows, LANES), 1)
    return jnp.where(lane < 256, lane >> 4, (lane & 127) >> 2)


def value_heads(rows):
    lane = iota((rows, LANES), 1)
    inner = lane & 127
    points = jnp.where(inner < STAT, inner >> 3, inner - STAT)
    return jnp.where(lane < 256, lane >> 4, points)


def pick(full, heads, rows):
    out = None
    for h in range(H):
        part = jnp.where(heads == h, full[h * rows : (h + 1) * rows], 0.0)
        out = part if out is None else out + part
    return out


def spread(x, heads):
    return jnp.concatenate([jnp.where(heads == h, x, 0.0) for h in range(H)], axis=0)


def spread2(x, heads):
    hi, lo = split(x)
    hi32, lo32 = hi.astype(F32), lo.astype(F32)
    return spread(hi32, heads).astype(BF16), spread(lo32, heads).astype(BF16)


def columns(frames_block, first):
    cols = [frames_block[:, first + n : first + n + 1] for n in range(12)]
    return [[cols[3 * a + b] for b in range(3)] for a in range(3)], cols[9:]


def block(x, a):
    return x[:, 256 + 128 * a : 384 + 128 * a]


def rotate(rot, pts):
    return [sum(rot[a][b] * pts[b] for b in range(3)) for a in range(3)]


def unrotate(rot, pts):
    return [sum(rot[a][b] * pts[a] for a in range(3)) for b in range(3)]


def place(rot, shift, flat):
    local_pts = [block(flat, a) for a in range(3)]
    turned = rotate(rot, local_pts)
    return jnp.concatenate(
        [flat[:, :256]] + [turned[a] + shift[a] for a in range(3)], axis=1
    )


def lane_matrix(rows, fn):
    r = iota((rows, 128), 0)
    c = iota((rows, 128), 1)
    return (fn(r) == c).astype(F32).astype(BF16)


def upstream_parts(g, w_out_ref, gp_ref, pu_ref, rows):
    hi, lo = split(g)
    both = jnp.concatenate([hi, lo], axis=0)

    def part(first, count):
        r = mm(both, w_out_ref[first : first + count, :], NT)
        return r[:rows] + r[rows:]

    gp_ref[...] = jnp.zeros(gp_ref.shape, F32)
    gp_ref[:, 0:192] = part(0, 192)
    for a in range(4):
        gp_ref[:, 256 + 128 * a : 352 + 128 * a] = part(192 + 96 * a, 96)
    wide = part(576, H * CZ)
    for h in range(H):
        pu_ref[h * rows : (h + 1) * rows, :] = (
            wide[:, h * CZ : (h + 1) * CZ].astype(BF16).astype(F32)
        )


def pair_products(pu_ref, pair_ref, d_ref, rows):
    for i in range(rows):
        lhs = pu_ref[pl.ds(i, H, stride=rows), :].astype(BF16)
        d_ref[pl.ds(i, H, stride=rows), :] = mm(lhs, pair_ref[i], NT)


def split3(x):
    hi, _ = split(x)
    rest = x - hi.astype(F32)
    mid, lo = split(rest)
    return hi, mid, lo


def pack_body(single_ref, frames_ref, chains_ref, pack_ref):
    rows = pack_ref.shape[0]
    pack_ref[:, 0:C] = single_ref[1]
    pack_ref[:, C : 2 * C] = single_ref[0]
    out = jnp.zeros((rows, 128), F32)
    for slot, l in ((0, 1), (12, 0)):
        hot = (iota((12, 128), 1) == iota((12, 128), 0) + slot).astype(F32).astype(BF16)
        for part in split3(frames_ref[:, l, :]):
            out = out + mm(part, hot, TN)
    hot = (iota((1, 128), 1) == CHAIN_LANE - FRAME_LANE).astype(F32).astype(BF16)
    pack_ref[:, 2 * C :] = out + mm(chains_ref[...].astype(F32).astype(BF16), hot, TN)


def prep_body(
    hw_ref, pack_ref, cot_hbm, w_out_hbm, pair_hbm, wq_hbm, wk_hbm, wv_hbm, wqp_hbm, wkp_hbm, wvp_hbm,
    wk_out, wq_out, gp_ref, q1_ref, q0_ref, pu_ref, d_ref, sc_ref,
    cot_ref, w_out_ref, pair_ref, wq_ref, wk_ref, wv_ref, wqp_ref, wkp_ref, wvp_ref, sems,
):
    rows = pack_ref.shape[0]
    ends = (
        (cot_hbm, cot_ref), (w_out_hbm, w_out_ref), (pair_hbm, pair_ref), (wq_hbm, wq_ref), (wk_hbm, wk_ref),
        (wv_hbm, wv_ref), (wqp_hbm, wqp_ref), (wkp_hbm, wkp_ref), (wvp_hbm, wvp_ref),
    )
    copies = [pltpu.make_async_copy(src, dst, sems.at[n]) for n, (src, dst) in enumerate(ends)]
    for copy in copies:
        copy.start()
    copies[0].wait()
    copies[1].wait()
    upstream_parts(cot_ref[...], w_out_ref, gp_ref, pu_ref, rows)
    copies[2].wait()
    pair_products(pu_ref, pair_ref, d_ref, rows)
    for copy in copies[3:]:
        copy.wait()
    wq_out[...] = jnp.zeros(wq_out.shape, BF16)
    wk_out[...] = jnp.zeros(wk_out.shape, BF16)
    wq_out[0:192, :] = wq_ref[...]
    wk_out[0:192, :] = wk_ref[...]
    wk_out[640:832, :] = wv_ref[...]
    for a in range(3):
        wq_out[256 + 128 * a : 304 + 128 * a, :] = wqp_ref[48 * a : 48 * a + 48, :]
        wk_out[256 + 128 * a : 304 + 128 * a, :] = wkp_ref[48 * a : 48 * a + 48, :]
        wk_out[896 + 128 * a : 992 + 128 * a, :] = wvp_ref[96 * a : 96 * a + 96, :]
    lane = iota((8, 128), 1)
    raw = jnp.zeros((8, 128), F32)
    for h in range(H):
        raw = jnp.where((lane >> 2) == h, hw_ref[h], raw)
    soft = jnp.maximum(raw, 0.0) + jnp.log(1.0 + jnp.exp(-jnp.abs(raw)))
    sc_ref[...] = soft * POINT_SCALE
    fr = pack_ref[:, FRAME_LANE : FRAME_LANE + 128]
    for out, first, fcol in ((q1_ref, 0, 0), (q0_ref, C, 12)):
        flat = mm2(pack_ref[:, first : first + C], wq_out[...], NT)
        rot, shift = columns(fr, fcol)
        out[:, :LANES] = place(rot, shift, flat)
        out[:, LANES:] = flat[:, 256:]


def project_keys(x, fr, fcol, wk_ref, kv_ref):
    flat = mm2(x, wk_ref[...], NT)
    rot, shift = columns(fr, fcol)
    kv_ref[:, 0:640] = place(rot, shift, flat[:, :640])
    kv_ref[:, 640:1280] = place(rot, shift, flat[:, 640:])
    kv_ref[:, 1280:1664] = flat[:, 256:640]
    kv_ref[:, 1664:2048] = flat[:, 896:1280]


def value_sums(probs, kv_ref, rows):
    values = kv_ref[:, 640:1280]
    lane = iota(values.shape, 1)
    values = jnp.where((lane >= 256 + STAT) & (lane < 256 + STAT + H), 1.0, values)
    hi, lo = split(values)
    return pick(mm(probs, hi) + mm(probs, lo), value_heads(rows), rows)


def head_dots(prod, rows):
    return mm2(prod, lane_matrix(256, lambda r: STAT + (r >> 4)))


def first_body(
    flag_ref, own_ref, ownx_ref, p1_ref, p1x_ref, p2_ref, p2x_ref, wk_ref, links_ref, probs_ref, gp_ref, d_ref,
    keys_ref, kv_ref, pm_ref, e_ref,
):
    rows = own_ref.shape[0]
    home = flag_ref[0] == 1
    zb = flag_ref[1]
    core = flag_ref[2]

    def put(z, k, value):
        keys_ref[pl.ds(pl.multiple_of((2 * z + k) * rows, rows), rows), :] = value

    put(zb, core, jnp.where(home, own_ref[...], p1_ref[...]))
    put(zb, 1 - core, jnp.where(home, ownx_ref[...], p1x_ref[...]))
    put(1 - zb, core, jnp.where(home, p1_ref[...], p2_ref[...]))
    put(1 - zb, 1 - core, jnp.where(home, p1x_ref[...], p2x_ref[...]))
    fr = keys_ref[:, FRAME_LANE : FRAME_LANE + 128]
    keys = fr.shape[0]
    at = CHAIN_LANE - FRAME_LANE
    key_chain = fr[:, at : at + 1]
    own_chain = own_ref[:, FRAME_LANE : FRAME_LANE + 128][:, at : at + 1]
    key_hot = (iota((keys, NCHAIN), 1).astype(F32) == key_chain).astype(F32).astype(BF16)
    own_hot = (iota((rows, NCHAIN), 1).astype(F32) == own_chain).astype(F32).astype(BF16)
    eye = iota((NCHAIN, NCHAIN), 0) == iota((NCHAIN, NCHAIN), 1)
    allowed = jnp.where(eye, 1.0, links_ref[...].astype(F32)).astype(BF16)
    mask = mm(mm(own_hot, allowed).astype(BF16), key_hot, NT)
    mask_all = jnp.concatenate([mask] * H, axis=0)
    for l in range(2):
        pm_ref[l] = (probs_ref[l].astype(F32) * mask_all).astype(BF16)
    project_keys(keys_ref[:, 0:C], fr, 0, wk_ref, kv_ref)
    probs = pm_ref[1]
    sums = value_sums(probs, kv_ref, rows)
    weighted = mm2(probs.astype(F32) * d_ref[...], jnp.ones((keys, 128), BF16))
    lane = iota((rows, 128), 1)
    dots = pick(weighted, lane - STAT, rows) + head_dots(gp_ref[:, 0:256] * sums[:, 0:256], rows)
    e_ref[:, 0:128] = block(sums, 0)
    e_ref[:, 128:256] = jnp.where(lane < STAT, block(sums, 1), dots)
    e_ref[:, 256:384] = block(sums, 2)


def second_body(keys_ref, wk_ref, pm_ref, pair_ref, kv_ref, e_ref, p32_ref, op_ref):
    rows = pair_ref.shape[0]
    fr = keys_ref[:, FRAME_LANE : FRAME_LANE + 128]
    project_keys(keys_ref[:, C : 2 * C], fr, 12, wk_ref, kv_ref)
    probs = pm_ref[0]
    sums = value_sums(probs, kv_ref, rows)
    for a in range(3):
        e_ref[:, 128 * a : 128 * a + 128] = block(sums, a)
    e_ref[:, 384:640] = sums[:, 0:256]
    p32_ref[...] = probs.astype(F32)
    for i in range(rows):
        lhs = p32_ref[pl.ds(i, H, stride=rows), :].astype(BF16)
        op_ref[pl.ds(i, H, stride=rows), :] = mm(lhs, pair_ref[i])
    for h in range(H):
        e_ref[:, 640 + CZ * h : 640 + CZ * (h + 1)] = op_ref[h * rows : (h + 1) * rows, :]


def backward(
    flag_ref, e, dots, probs, kv_ref, key_fr, own_fr, fcol, q_ref, gp, d_ref, wk_ref, sc,
    z_ref, keys_out_ref,
):
    rows = e.shape[0]
    lane = iota((rows, 128), 1)
    stat = (lane >= STAT) & (lane < STAT + H)
    inv = jnp.where(stat, 1.0 / jnp.where(stat, e[:, 0:128], 1.0), 0.0)
    r128 = iota((128, LANES), 0)
    grow = (r128 - STAT == value_heads(128)) & ((iota((128, LANES), 1) & 127) < STAT)
    grow = grow | ((r128 - STAT == (iota((128, LANES), 1) >> 4)) & (iota((128, LANES), 1) < 256))
    inv_lanes = mm2(inv, grow.astype(F32).astype(BF16))
    rot, shift = columns(own_fr, fcol)
    inv_pts = block(inv_lanes, 0)
    ptg = [e[:, 128 * a : 128 * a + 128] * inv_pts for a in range(3)]
    off = [jnp.where(lane < STAT, ptg[a] - shift[a], 0.0) for a in range(3)]
    opt = unrotate(rot, off)
    length = jnp.sqrt(opt[0] * opt[0] + opt[1] * opt[1] + opt[2] * opt[2] + NORM_EPS)
    scale = gp[:, 640:768] / length
    gpt = [block(gp, a) + scale * opt[a] for a in range(3)]
    gptg = rotate(rot, gpt)
    upper = jnp.concatenate([gp[:, 0:256]] + gptg, axis=1)
    point_dots = gptg[0] * ptg[0] + gptg[1] * ptg[1] + gptg[2] * ptg[2]
    rd = dots * inv + mm2(point_dots, lane_matrix(128, lambda r: STAT + (r >> 3)))
    both = jnp.concatenate([spread(rd, lane - STAT), spread(inv, lane - STAT)], axis=0)
    wide = mm2(both, jnp.ones((128, 128), BF16))
    rd_all, inv_all = wide[: H * rows], wide[H * rows :]
    heads_v = value_heads(rows)
    heads_k = key_heads(rows)
    uh, ul = spread2(upper, heads_v)
    vh, vl = split(kv_ref[:, 640:1280])
    d_att = d_ref[...] + mm3(uh, ul, vh, vl, NT)
    p32 = probs.astype(F32)
    att = p32 * inv_all
    dl = LOGIT_SCALE * att * (d_att - rd_all)
    z_ref[0 : H * rows, :] = att
    z_ref[H * rows :, :] = dl
    dt = jnp.transpose(dl)
    th, tl = split(dt)
    qh, qlo = spread2(q_ref[:, 0:640], heads_k)
    kr = mm3(th, tl, qh, qlo)
    head_rows = iota((H * rows, 128), 0) // rows
    hot = ((iota((H * rows, 128), 1) >> 2) == head_rows).astype(F32).astype(BF16)
    cs = mm(th, hot) + mm(tl, hot)
    pt = jnp.transpose(p32).astype(BF16)
    sh, sl = spread2(upper * inv_lanes, heads_v)
    vr = mm(pt, sh) + mm(pt, sl)
    krot, _ = columns(key_fr, fcol)
    d_kg = [sc * (block(kr, a) - cs * kv_ref[:, 256 + 128 * a : 384 + 128 * a]) for a in range(3)]
    d_vg = [block(vr, a) for a in range(3)]
    d_kl = unrotate(krot, d_kg)
    d_vl = unrotate(krot, d_vg)
    flat = jnp.concatenate([PLAIN_SCALE * kr[:, 0:256]] + d_kl + [vr[:, 0:256]] + d_vl, axis=1)
    keys_out_ref[:, 0:C] = mm2(flat, wk_ref[...])
    return jnp.concatenate(off + gpt + gptg, axis=1), jnp.concatenate(d_kg + d_vg, axis=1)


def frame_sums(prods, first_lane):
    return mm2(jnp.concatenate(prods, axis=1), lane_matrix(12 * 128, lambda r: first_lane + (r >> 7)))


def backward_frames(grads, kv_ref, first_lane):
    d_kg = [grads[:, 128 * a : 128 * a + 128] for a in range(3)]
    d_vg = [grads[:, 384 + 128 * a : 512 + 128 * a] for a in range(3)]
    k_local = [kv_ref[:, 1280 + 128 * b : 1408 + 128 * b] for b in range(3)]
    v_local = [kv_ref[:, 1664 + 128 * b : 1792 + 128 * b] for b in range(3)]
    prods = [d_kg[a] * k_local[b] + d_vg[a] * v_local[b] for a in range(3) for b in range(3)]
    return frame_sums(prods + [d_kg[a] + d_vg[a] for a in range(3)], first_lane)


def backward_query(dl, kv_ref, own_fr, fcol, q_ref, pts_ref, wq_ref, sc, first_lane, share):
    rows = own_fr.shape[0]
    dh, dlo = split(dl)
    kh, klo = split(kv_ref[:, 0:640])
    qr = pick(mm3(dh, dlo, kh, klo), key_heads(rows), rows)
    rot, _ = columns(own_fr, fcol)
    d_qg = [sc * block(qr, a) for a in range(3)]
    d_ql = unrotate(rot, d_qg)
    grad = mm2(jnp.concatenate([PLAIN_SCALE * qr[:, 0:256]] + d_ql, axis=1), wq_ref[...])
    q_local = [q_ref[:, 640 + 128 * b : 768 + 128 * b] for b in range(3)]
    off, gpt, gptg = [
        [pts_ref[:, 384 * n + 128 * a : 384 * n + 128 * a + 128] for a in range(3)] for n in range(3)
    ]
    prods = [d_qg[a] * q_local[b] + share * off[a] * gpt[b] for a in range(3) for b in range(3)]
    prods = prods + [d_qg[a] - share * gptg[a] for a in range(3)]
    return grad, frame_sums(prods, first_lane)


def send_blocks(flag_ref, src_ref, mine_a, mine_b, theirs, rows):
    zb = flag_ref[1]
    core = flag_ref[2]

    def get(z, k):
        return src_ref[pl.ds(pl.multiple_of((2 * z + k) * rows, rows), rows), :]

    mine_a[...] = get(zb, core)
    mine_b[...] = get(1 - zb, core)
    theirs[0:rows, :] = get(zb, 1 - core)
    theirs[rows:, :] = get(1 - zb, 1 - core)


def final_body(r0, r1, r2, r3, r4, r5, one_ref, single_out, frames_out):
    total = (r0[...] + r1[...]) + (r2[...] + r3[...]) + (r4[...] + r5[...])
    single_out[...] = one_ref[...] + total[:, 0:C]
    turned = jnp.transpose(total[:, C:])
    for l in range(2):
        frames_out[:, l, :] = turned[12 * l : 12 * l + 12, :]


def frame_part(ref):
    return ref[:, FRAME_LANE : FRAME_LANE + 128]


def back_one_body(
    flag_ref, e_mine, e_other, pm_ref, kv_ref, keys_ref, own_ref, q_ref, gp_ref, d_ref, wk_ref, sc_ref,
    z_ref, mine_a, mine_b, theirs, pts_ref, grads_ref, work_ref,
):
    e = e_mine[...] + e_other[...]
    pts_ref[...], grads_ref[...] = backward(
        flag_ref, e, e[:, 128:256], pm_ref[1], kv_ref, frame_part(keys_ref), frame_part(own_ref), 0, q_ref,
        gp_ref[...], d_ref, wk_ref, sc_ref[0:1, :], z_ref, work_ref,
    )
    send_blocks(flag_ref, work_ref, mine_a, mine_b, theirs, own_ref.shape[0])


def query_one_body(
    share, z_ref, kv_ref, own_ref, q_ref, pts_ref, grads_ref, wq_ref, sc_ref, query_out, frq_ref, frk_ref
):
    half = z_ref.shape[0] // 2
    query_out[...], frq_ref[...] = backward_query(
        z_ref[half:, :], kv_ref, frame_part(own_ref), 0, q_ref, pts_ref, wq_ref, sc_ref[0:1, :], 12, share
    )
    frk_ref[...] = backward_frames(grads_ref[...], kv_ref, 12)


def back_zero_body(
    flag_ref, cot_ref, r0, r1, r2, r3, r4, r5, e_mine, e_other, pm_ref, kv_ref, keys_ref, own_ref, q_ref, pair_ref,
    w_out_ref, wk_ref, sc_ref, frk_ref,
    z_ref, mine_a, mine_b, theirs, pts_ref, sum_ref, pu_ref, work_ref, gp_ref, d_ref,
):
    rows = own_ref.shape[0]
    total = (r0[...] + r1[...]) + (r2[...] + r3[...]) + (r4[...] + r5[...])
    sum_ref[...] = total
    upstream_parts(cot_ref[...] + total, w_out_ref, gp_ref, pu_ref, rows)
    pair_products(pu_ref, pair_ref, d_ref, rows)
    gp = gp_ref[...]
    e = e_mine[:, 0:384] + e_other[:, 0:384]
    plain = e_mine[:, 384:640] + e_other[:, 384:640]
    dots = head_dots(gp[:, 0:256] * plain, rows)
    wide = jnp.concatenate(
        [
            pu_ref[h * rows : (h + 1) * rows, :]
            * (e_mine[:, 640 + CZ * h : 640 + CZ * (h + 1)] + e_other[:, 640 + CZ * h : 640 + CZ * (h + 1)])
            for h in range(H)
        ],
        axis=1,
    )
    dots = dots + mm2(wide, lane_matrix(H * CZ, lambda r: STAT + (r >> 7)))
    pts_ref[...], grads = backward(
        flag_ref, e, dots, pm_ref[0], kv_ref, frame_part(keys_ref), frame_part(own_ref), 12, q_ref, gp, d_ref, wk_ref,
        sc_ref[0:1, :], z_ref, work_ref,
    )
    work_ref[:, C:] = backward_frames(grads, kv_ref, 0) + frk_ref[...]
    send_blocks(flag_ref, work_ref, mine_a, mine_b, theirs, rows)


def query_zero_body(share, z_ref, kv_ref, own_ref, q_ref, pts_ref, wq_ref, sc_ref, frq_ref, query_out):
    half = z_ref.shape[0] // 2
    grad, frames = backward_query(
        z_ref[half:, :], kv_ref, frame_part(own_ref), 12, q_ref, pts_ref, wq_ref, sc_ref[0:1, :], 0, share
    )
    query_out[:, 0:C] = grad
    query_out[:, C:] = frames + frq_ref[...]


def pair_body(z1_ref, z0_ref, pu1_ref, pu0_ref, wbt_ref, out_ref):
    rows = out_ref.shape[0]
    wbt = wbt_ref[...].astype(F32)
    for i in range(rows):
        left = jnp.concatenate(
            [z1_ref[pl.ds(i, 2 * H, stride=rows), :], z0_ref[pl.ds(i, 2 * H, stride=rows), :]], axis=0
        )
        right = jnp.concatenate(
            [pu1_ref[pl.ds(i, H, stride=rows), :], wbt, pu0_ref[pl.ds(i, H, stride=rows), :], wbt], axis=0
        ).astype(BF16)
        out_ref[i] = mm(left.astype(BF16), right, TN).astype(BF16)


VMEM = pl.BlockSpec(memory_space=pltpu.VMEM)
SMEM = pl.BlockSpec(memory_space=pltpu.SMEM)
HBM = pl.BlockSpec(memory_space=pltpu.HBM)


def call(body, name, in_specs, outs, args, scratch=(), micros=1.0):
    return pl.pallas_call(
        body,
        name=name,
        in_specs=in_specs,
        out_specs=tuple(VMEM for _ in outs),
        out_shape=tuple(jax.ShapeDtypeStruct(s, d) for s, d in outs),
        scratch_shapes=list(scratch),
        compiler_params=pltpu.CompilerParams(vmem_limit_bytes=16 * 1024 * 1024),
        cost_estimate=pl.CostEstimate(flops=int(micros * 1e9), transcendentals=0, bytes_accessed=int(micros * 3e6)),
    )(*args)


def joint(pairs):
    return [
        ((a * 2 + k) * 2 + x, (b * 2 + k) * 2 + y) for (x, a), (y, b) in pairs for k in range(2)
    ]


BOTH = ("row", "col")
FETCH_ONE = joint([((0, 0), (0, 1)), ((0, 1), (0, 0)), ((1, 0), (0, 2)), ((1, 1), (0, 3)), ((1, 2), (1, 3)), ((1, 3), (1, 2)), ((0, 2), (1, 0)), ((0, 3), (1, 1))])
FETCH_TWO = joint([((0, 0), (0, 3)), ((0, 1), (0, 2)), ((1, 2), (1, 1)), ((1, 3), (1, 0))])
SCATTER = [
    joint([((x, z), (((s ^ z) >> 1) & 1, 2 * x + ((s ^ z) & 1))) for x in range(2) for z in range(4)])
    for s in range(4)
]
CORE_SWAP = [(i, i ^ 1) for i in range(8)]
COL_SWAP = [(0, 1), (1, 0)]


def local(
    single, frames, saved_probs, pair, cotangent, chains, links, w_query, w_key, w_value, w_query_points,
    w_key_points, w_value_points, w_bias, w_out, head_weights,
):
    rows = single.shape[1]
    keys = pair.shape[1]
    row_total = lax.axis_size("row")
    col_total = lax.axis_size("col")
    fast = row_total == 8 and col_total == 2 and keys == 4 * rows
    (pack,) = call(
        pack_body, "pack", [VMEM] * 3, [((rows, PACK), F32)],
        (single, frames.transpose(1, 0, 2), chains[None]),
    )
    col = lax.axis_index("col")
    row = lax.axis_index("row")
    if fast:
        home = (row // 4 == col).astype(jnp.int32)
        flags = jnp.stack([home, (row // 2) % 2, row % 2])
        ownx = lax.ppermute(pack, "row", CORE_SWAP)
        one = lax.ppermute(pack, BOTH, FETCH_ONE)
        two = lax.ppermute(pack, BOTH, FETCH_TWO)
        own = pack
    else:
        flags = jnp.array([1, 0, 0], jnp.int32)
        whole = lax.all_gather(pack, "row", axis=0, tiled=True)
        mine = lax.dynamic_slice_in_dim(whole, col * keys, keys, 0)
        quarter = keys // 4
        blocks = tuple(mine[quarter * n : quarter * (n + 1)] for n in (0, 1, 2, 3, 0, 0))
        own = pack

    def col_other(x):
        if col_total == 2:
            return lax.ppermute(x, "col", COL_SWAP)
        return lax.psum(x, "col") - x

    def reduce(mine_a, mine_b, theirs, late):
        if fast:
            got = lax.ppermute(theirs, "row", CORE_SWAP)
            query, *rest = late()
            got, query = lax.optimization_barrier((got, query))
            query_other = lax.ppermute(query, "col", COL_SWAP)
            part = (mine_a + got[:rows], mine_b + got[rows:])
            return [query, query_other] + [lax.ppermute(part[s & 1], BOTH, SCATTER[s]) for s in range(4)], rest
        query, *rest = late()
        parts = jnp.concatenate([mine_a, theirs[:rows], mine_b, theirs[rows:]], axis=0)
        summed = lax.all_gather(lax.psum(parts, "row"), "col", axis=0, tiled=True)
        zero = jnp.zeros_like(query)
        back = lax.dynamic_slice_in_dim(summed, row * rows, rows, 0)
        return [lax.psum(query, "col"), back, zero, zero, zero, zero], rest

    probs = saved_probs.reshape(2, H * rows, keys)
    hr = H * rows
    loads = (
        cotangent, w_out, pair, w_query.T, w_key.T, w_value.T, w_query_points.T, w_key_points.T, w_value_points.T,
    )
    wk, wq, gp1, q1, q0, pu1, d1, sc = call(
        prep_body, "prep", [SMEM, VMEM] + [HBM] * 9,
        [((1280, C), BF16), ((LANES, C), BF16), ((rows, 768), F32), ((rows, 1024), F32), ((rows, 1024), F32),
         ((hr, CZ), F32), ((hr, keys), F32), ((8, 128), F32)],
        (head_weights, own, *(pltpu.with_memory_space_constraint(x, pltpu.HBM) for x in loads)),
        [pltpu.VMEM(x.shape, x.dtype) for x in loads] + [pltpu.SemaphoreType.DMA((len(loads),))],
    )
    if fast:
        one, two, wk, wq, gp1, q1, q0, pu1, d1, sc = lax.optimization_barrier(
            (one, two, wk, wq, gp1, q1, q0, pu1, d1, sc)
        )
        blocks = (pack, ownx, one, lax.ppermute(one, "row", CORE_SWAP), two, lax.ppermute(two, "row", CORE_SWAP))
    key_pack, kv1, pm, e1 = call(
        first_body, "first", [SMEM] + [VMEM] * 11,
        [((keys, PACK), F32), ((keys, 2048), F32), ((2, hr, keys), BF16), ((rows, 384), F32)],
        (flags, *blocks, wk, links, probs, gp1, d1),
    )
    e1_other = col_other(e1)
    kv0, e0 = call(
        second_body, "second", [VMEM] * 4,
        [((keys, 2048), F32), ((rows, 640 + H * CZ), F32)],
        (key_pack, wk, pm, pair),
        [pltpu.VMEM((hr, keys), F32), pltpu.VMEM((hr, CZ), F32)],
    )
    e0_other = col_other(e0)
    share = 1.0 / col_total
    e1_other, e0 = lax.optimization_barrier((e1_other, e0))
    z1, mine_a, mine_b, theirs, pts, grads = call(
        back_one_body, "back_one", [SMEM] + [VMEM] * 11,
        [((2 * hr, keys), F32), ((rows, C), F32), ((rows, C), F32), ((2 * rows, C), F32), ((rows, 1152), F32),
         ((keys, 768), F32)],
        (flags, e1, e1_other, pm, kv1, key_pack, own, q1, gp1, d1, wk, sc),
        [pltpu.VMEM((keys, C), F32)],
        6.0,
    )
    pts, e0_other = lax.optimization_barrier((pts, e0_other))
    pieces, (frq, frk) = reduce(
        mine_a, mine_b, theirs,
        lambda: call(
            functools.partial(query_one_body, share), "query_one", [VMEM] * 8,
            [((rows, C), F32), ((rows, 128), F32), ((keys, 128), F32)],
            (z1, kv1, own, q1, pts, grads, wq, sc),
        ),
    )
    z0, mine_a, mine_b, theirs, pts, single_one, pu0 = call(
        back_zero_body, "back_zero", [SMEM] + [VMEM] * 19,
        [((2 * hr, keys), F32), ((rows, 512), F32), ((rows, 512), F32), ((2 * rows, 512), F32), ((rows, 1152), F32),
         ((rows, C), F32), ((hr, CZ), F32)],
        (flags, cotangent, *pieces, e0, e0_other, pm, kv0, key_pack, own, q0, pair, w_out, wk, sc, frk),
        [pltpu.VMEM((keys, 512), F32), pltpu.VMEM((rows, 768), F32), pltpu.VMEM((hr, keys), F32)],
    )
    pieces, _ = reduce(
        mine_a, mine_b, theirs,
        lambda: call(
            functools.partial(query_zero_body, share), "query_zero", [VMEM] * 8, [((rows, 512), F32)],
            (z0, kv0, own, q0, pts, wq, sc, frq),
        ),
    )
    (d_pair,) = call(
        pair_body, "pair_grad", [VMEM] * 5, [((rows, keys, CZ), BF16)], (z1, z0, pu1, pu0, w_bias.T)
    )
    d_single, d_frames = call(
        final_body, "final", [VMEM] * 7, [((rows, C), F32), ((12, 2, rows), F32)], (*pieces, single_one)
    )
    return (d_single, d_frames.transpose(1, 0, 2), d_pair)


def solution(mesh):
    return jax.shard_map(
        local,
        mesh=mesh,
        in_specs=(
            P(None, ("grp", "row"), None),
            P(None, None, ("grp", "row")),
            P(None, None, ("grp", "row"), "col"),
            P(("grp", "row"), "col", None),
            P(("grp", "row"), None),
            P(("grp", "row")),
            P("grp", None),
            P(),
            P(),
            P(),
            P(),
            P(),
            P(),
            P(),
            P(),
            P(),
        ),
        out_specs=(
            P(("grp", "row"), None),
            P(None, None, ("grp", "row")),
            P(("grp", "row"), "col", None),
        ),
        check_vma=False,
    )
```

```python
import functools
import math

import jax
import jax.numpy as jnp
from jax import lax
from jax.experimental import pallas as pl
from jax.experimental.pallas import tpu as pltpu
from jax.sharding import PartitionSpec as P

C = 384
H = 12
HD = 16
CZ = 128
PQ = 4
PV = 8
NCHAIN = 16
NORM_EPS = 1e-08
LOGIT_SCALE = math.sqrt(1.0 / 3.0)
PLAIN_SCALE = 1.0 / math.sqrt(HD)
POINT_SCALE = math.sqrt(2.0 / (9.0 * PQ))

LANES = 640
PACK = 896
FRAME_LANE = 768
CHAIN_LANE = 792
STAT = 96

F32 = jnp.float32
BF16 = jnp.bfloat16
NN = (((1,), (0,)), ((), ()))
NT = (((1,), (1,)), ((), ()))
TN = (((0,), (0,)), ((), ()))


def mm(a, b, dims=NN):
    return lax.dot_general(a, b, dims, preferred_element_type=F32)


def split(x):
    hi = x.astype(BF16)
    return hi, (x - hi.astype(F32)).astype(BF16)


def mm2(x, w, dims=NN):
    hi, lo = split(x)
    rows = x.shape[0]
    both = mm(jnp.concatenate([hi, lo], axis=0), w, dims)
    return both[:rows] + both[rows:]


def mm3(ah, al, bh, bl, dims=NN):
    return mm(ah, bh, dims) + mm(ah, bl, dims) + mm(al, bh, dims)


def iota(shape, axis):
    return lax.broadcasted_iota(jnp.int32, shape, axis)


def key_heads(rows):
    lane = iota((rows, LANES), 1)
    return jnp.where(lane < 256, lane >> 4, (lane & 127) >> 2)


def value_heads(rows):
    lane = iota((rows, LANES), 1)
    inner = lane & 127
    points = jnp.where(inner < STAT, inner >> 3, inner - STAT)
    return jnp.where(lane < 256, lane >> 4, points)


def pick(full, heads, rows):
    out = None
    for h in range(H):
        part = jnp.where(heads == h, full[h * rows : (h + 1) * rows], 0.0)
        out = part if out is None else out + part
    return out


def spread(x, heads):
    return jnp.concatenate([jnp.where(heads == h, x, 0.0) for h in range(H)], axis=0)


def spread2(x, heads):
    hi, lo = split(x)
    hi32, lo32 = hi.astype(F32), lo.astype(F32)
    return spread(hi32, heads).astype(BF16), spread(lo32, heads).astype(BF16)


def columns(frames_block, first):
    cols = [frames_block[:, first + n : first + n + 1] for n in range(12)]
    return [[cols[3 * a + b] for b in range(3)] for a in range(3)], cols[9:]


def block(x, a):
    return x[:, 256 + 128 * a : 384 + 128 * a]


def rotate(rot, pts):
    return [sum(rot[a][b] * pts[b] for b in range(3)) for a in range(3)]


def unrotate(rot, pts):
    return [sum(rot[a][b] * pts[a] for a in range(3)) for b in range(3)]


def place(rot, shift, flat):
    local_pts = [block(flat, a) for a in range(3)]
    turned = rotate(rot, local_pts)
    return jnp.concatenate(
        [flat[:, :256]] + [turned[a] + shift[a] for a in range(3)], axis=1
    )


def lane_matrix(rows, fn):
    r = iota((rows, 128), 0)
    c = iota((rows, 128), 1)
    return (fn(r) == c).astype(F32).astype(BF16)


def upstream_parts(g, w_out_ref, gp_ref, pu_ref, rows):
    hi, lo = split(g)
    both = jnp.concatenate([hi, lo], axis=0)

    def part(first, count):
        r = mm(both, w_out_ref[first : first + count, :], NT)
        return r[:rows] + r[rows:]

    gp_ref[...] = jnp.zeros(gp_ref.shape, F32)
    gp_ref[:, 0:192] = part(0, 192)
    for a in range(4):
        gp_ref[:, 256 + 128 * a : 352 + 128 * a] = part(192 + 96 * a, 96)
    wide = part(576, H * CZ)
    for h in range(H):
        pu_ref[h * rows : (h + 1) * rows, :] = (
            wide[:, h * CZ : (h + 1) * CZ].astype(BF16).astype(F32)
        )


def pair_products(pu_ref, pair_ref, d_ref, rows):
    for i in range(rows):
        lhs = pu_ref[pl.ds(i, H, stride=rows), :].astype(BF16)
        d_ref[pl.ds(i, H, stride=rows), :] = mm(lhs, pair_ref[i], NT)


def split3(x):
    hi, _ = split(x)
    rest = x - hi.astype(F32)
    mid, lo = split(rest)
    return hi, mid, lo


def pack_body(single_hbm, frames_hbm, chains_hbm, pack_ref, frames_ref, chains_ref, sems):
    rows = pack_ref.shape[0]
    ends = (
        (frames_hbm, frames_ref), (chains_hbm, chains_ref), (single_hbm.at[1], pack_ref.at[:, 0:C]),
        (single_hbm.at[0], pack_ref.at[:, C : 2 * C]),
    )
    copies = [pltpu.make_async_copy(src, dst, sems.at[n]) for n, (src, dst) in enumerate(ends)]
    for copy in copies:
        copy.start()
    copies[0].wait()
    copies[1].wait()
    out = jnp.zeros((rows, 128), F32)
    for slot, l in ((0, 1), (12, 0)):
        hot = (iota((12, 128), 1) == iota((12, 128), 0) + slot).astype(F32).astype(BF16)
        for part in split3(frames_ref[:, l, :]):
            out = out + mm(part, hot, TN)
    hot = (iota((1, 128), 1) == CHAIN_LANE - FRAME_LANE).astype(F32).astype(BF16)
    pack_ref[:, 2 * C :] = out + mm(chains_ref[...].astype(F32).astype(BF16), hot, TN)
    copies[2].wait()
    copies[3].wait()


def prep_body(
    hw_ref, pack_ref, cot_hbm, w_out_hbm, pair_hbm, wq_hbm, wk_hbm, wv_hbm, wqp_hbm, wkp_hbm, wvp_hbm,
    wk_out, wq_out, gp_ref, q1_ref, q0_ref, pu_ref, d_ref, sc_ref,
    cot_ref, w_out_ref, pair_ref, wq_ref, wk_ref, wv_ref, wqp_ref, wkp_ref, wvp_ref, sems,
):
    rows = pack_ref.shape[0]
    ends = (
        (cot_hbm, cot_ref), (w_out_hbm, w_out_ref), (pair_hbm, pair_ref), (wq_hbm, wq_ref), (wk_hbm, wk_ref),
        (wv_hbm, wv_ref), (wqp_hbm, wqp_ref), (wkp_hbm, wkp_ref), (wvp_hbm, wvp_ref),
    )
    copies = [pltpu.make_async_copy(src, dst, sems.at[n]) for n, (src, dst) in enumerate(ends)]
    for copy in copies:
        copy.start()
    copies[0].wait()
    copies[1].wait()
    upstream_parts(cot_ref[...], w_out_ref, gp_ref, pu_ref, rows)
    copies[2].wait()
    pair_products(pu_ref, pair_ref, d_ref, rows)
    for copy in copies[3:]:
        copy.wait()
    wq_out[...] = jnp.zeros(wq_out.shape, BF16)
    wk_out[...] = jnp.zeros(wk_out.shape, BF16)
    wq_out[0:192, :] = wq_ref[...]
    wk_out[0:192, :] = wk_ref[...]
    wk_out[640:832, :] = wv_ref[...]
    for a in range(3):
        wq_out[256 + 128 * a : 304 + 128 * a, :] = wqp_ref[48 * a : 48 * a + 48, :]
        wk_out[256 + 128 * a : 304 + 128 * a, :] = wkp_ref[48 * a : 48 * a + 48, :]
        wk_out[896 + 128 * a : 992 + 128 * a, :] = wvp_ref[96 * a : 96 * a + 96, :]
    lane = iota((8, 128), 1)
    raw = jnp.zeros((8, 128), F32)
    for h in range(H):
        raw = jnp.where((lane >> 2) == h, hw_ref[h], raw)
    soft = jnp.maximum(raw, 0.0) + jnp.log(1.0 + jnp.exp(-jnp.abs(raw)))
    sc_ref[...] = soft * POINT_SCALE
    fr = pack_ref[:, FRAME_LANE : FRAME_LANE + 128]
    for out, first, fcol in ((q1_ref, 0, 0), (q0_ref, C, 12)):
        flat = mm2(pack_ref[:, first : first + C], wq_out[...], NT)
        rot, shift = columns(fr, fcol)
        out[:, :LANES] = place(rot, shift, flat)
        out[:, LANES:] = flat[:, 256:]


def project_keys(x, fr, fcol, wk_ref, kv_ref):
    flat = mm2(x, wk_ref[...], NT)
    rot, shift = columns(fr, fcol)
    kv_ref[:, 0:640] = place(rot, shift, flat[:, :640])
    kv_ref[:, 640:1280] = place(rot, shift, flat[:, 640:])
    kv_ref[:, 1280:1664] = flat[:, 256:640]
    kv_ref[:, 1664:2048] = flat[:, 896:1280]


def value_sums(probs, kv_ref, rows):
    values = kv_ref[:, 640:1280]
    lane = iota(values.shape, 1)
    values = jnp.where((lane >= 256 + STAT) & (lane < 256 + STAT + H), 1.0, values)
    hi, lo = split(values)
    return pick(mm(probs, hi) + mm(probs, lo), value_heads(rows), rows)


def head_dots(prod, rows):
    return mm2(prod, lane_matrix(256, lambda r: STAT + (r >> 4)))


def first_body(
    flag_ref, own_ref, ownx_ref, p1_ref, p1x_ref, p2_ref, p2x_ref, wk_ref, links_ref, probs_ref, gp_ref, d_ref,
    keys_ref, kv_ref, pm_ref, e_ref,
):
    rows = own_ref.shape[0]
    home = flag_ref[0] == 1
    zb = flag_ref[1]
    core = flag_ref[2]

    def put(z, k, value):
        keys_ref[pl.ds(pl.multiple_of((2 * z + k) * rows, rows), rows), :] = value

    put(zb, core, jnp.where(home, own_ref[...], p1_ref[...]))
    put(zb, 1 - core, jnp.where(home, ownx_ref[...], p1x_ref[...]))
    put(1 - zb, core, jnp.where(home, p1_ref[...], p2_ref[...]))
    put(1 - zb, 1 - core, jnp.where(home, p1x_ref[...], p2x_ref[...]))
    fr = keys_ref[:, FRAME_LANE : FRAME_LANE + 128]
    keys = fr.shape[0]
    at = CHAIN_LANE - FRAME_LANE
    key_chain = fr[:, at : at + 1]
    own_chain = own_ref[:, FRAME_LANE : FRAME_LANE + 128][:, at : at + 1]
    key_hot = (iota((keys, NCHAIN), 1).astype(F32) == key_chain).astype(F32).astype(BF16)
    own_hot = (iota((rows, NCHAIN), 1).astype(F32) == own_chain).astype(F32).astype(BF16)
    eye = iota((NCHAIN, NCHAIN), 0) == iota((NCHAIN, NCHAIN), 1)
    allowed = jnp.where(eye, 1.0, links_ref[...].astype(F32)).astype(BF16)
    mask = mm(mm(own_hot, allowed).astype(BF16), key_hot, NT)
    mask_all = jnp.concatenate([mask] * H, axis=0)
    for l in range(2):
        pm_ref[l] = (probs_ref[l].astype(F32) * mask_all).astype(BF16)
    project_keys(keys_ref[:, 0:C], fr, 0, wk_ref, kv_ref)
    probs = pm_ref[1]
    sums = value_sums(probs, kv_ref, rows)
    weighted = mm2(probs.astype(F32) * d_ref[...], jnp.ones((keys, 128), BF16))
    lane = iota((rows, 128), 1)
    dots = pick(weighted, lane - STAT, rows) + head_dots(gp_ref[:, 0:256] * sums[:, 0:256], rows)
    e_ref[:, 0:128] = block(sums, 0)
    e_ref[:, 128:256] = jnp.where(lane < STAT, block(sums, 1), dots)
    e_ref[:, 256:384] = block(sums, 2)


def second_body(keys_ref, wk_ref, pm_ref, pair_ref, kv_ref, e_ref, p32_ref, op_ref):
    rows = pair_ref.shape[0]
    fr = keys_ref[:, FRAME_LANE : FRAME_LANE + 128]
    project_keys(keys_ref[:, C : 2 * C], fr, 12, wk_ref, kv_ref)
    probs = pm_ref[0]
    sums = value_sums(probs, kv_ref, rows)
    for a in range(3):
        e_ref[:, 128 * a : 128 * a + 128] = block(sums, a)
    e_ref[:, 384:640] = sums[:, 0:256]
    p32_ref[...] = probs.astype(F32)
    for i in range(rows):
        lhs = p32_ref[pl.ds(i, H, stride=rows), :].astype(BF16)
        op_ref[pl.ds(i, H, stride=rows), :] = mm(lhs, pair_ref[i])
    for h in range(H):
        e_ref[:, 640 + CZ * h : 640 + CZ * (h + 1)] = op_ref[h * rows : (h + 1) * rows, :]


def backward(
    flag_ref, e, dots, probs, kv_ref, key_fr, own_fr, fcol, q_ref, gp, d_ref, wk_ref, sc,
    z_ref, keys_out_ref,
):
    rows = e.shape[0]
    lane = iota((rows, 128), 1)
    stat = (lane >= STAT) & (lane < STAT + H)
    inv = jnp.where(stat, 1.0 / jnp.where(stat, e[:, 0:128], 1.0), 0.0)
    r128 = iota((128, LANES), 0)
    grow = (r128 - STAT == value_heads(128)) & ((iota((128, LANES), 1) & 127) < STAT)
    grow = grow | ((r128 - STAT == (iota((128, LANES), 1) >> 4)) & (iota((128, LANES), 1) < 256))
    inv_lanes = mm2(inv, grow.astype(F32).astype(BF16))
    rot, shift = columns(own_fr, fcol)
    inv_pts = block(inv_lanes, 0)
    ptg = [e[:, 128 * a : 128 * a + 128] * inv_pts for a in range(3)]
    off = [jnp.where(lane < STAT, ptg[a] - shift[a], 0.0) for a in range(3)]
    opt = unrotate(rot, off)
    length = jnp.sqrt(opt[0] * opt[0] + opt[1] * opt[1] + opt[2] * opt[2] + NORM_EPS)
    scale = gp[:, 640:768] / length
    gpt = [block(gp, a) + scale * opt[a] for a in range(3)]
    gptg = rotate(rot, gpt)
    upper = jnp.concatenate([gp[:, 0:256]] + gptg, axis=1)
    point_dots = gptg[0] * ptg[0] + gptg[1] * ptg[1] + gptg[2] * ptg[2]
    rd = dots * inv + mm2(point_dots, lane_matrix(128, lambda r: STAT + (r >> 3)))
    both = jnp.concatenate([spread(rd, lane - STAT), spread(inv, lane - STAT)], axis=0)
    wide = mm2(both, jnp.ones((128, 128), BF16))
    rd_all, inv_all = wide[: H * rows], wide[H * rows :]
    heads_v = value_heads(rows)
    heads_k = key_heads(rows)
    uh, ul = spread2(upper, heads_v)
    vh, vl = split(kv_ref[:, 640:1280])
    d_att = d_ref[...] + mm3(uh, ul, vh, vl, NT)
    p32 = probs.astype(F32)
    att = p32 * inv_all
    dl = LOGIT_SCALE * att * (d_att - rd_all)
    z_ref[0 : H * rows, :] = att
    z_ref[H * rows :, :] = dl
    dt = jnp.transpose(dl)
    th, tl = split(dt)
    qh, qlo = spread2(q_ref[:, 0:640], heads_k)
    kr = mm3(th, tl, qh, qlo)
    head_rows = iota((H * rows, 128), 0) // rows
    hot = ((iota((H * rows, 128), 1) >> 2) == head_rows).astype(F32).astype(BF16)
    cs = mm(th, hot) + mm(tl, hot)
    pt = jnp.transpose(p32).astype(BF16)
    sh, sl = spread2(upper * inv_lanes, heads_v)
    vr = mm(pt, sh) + mm(pt, sl)
    krot, _ = columns(key_fr, fcol)
    d_kg = [sc * (block(kr, a) - cs * kv_ref[:, 256 + 128 * a : 384 + 128 * a]) for a in range(3)]
    d_vg = [block(vr, a) for a in range(3)]
    d_kl = unrotate(krot, d_kg)
    d_vl = unrotate(krot, d_vg)
    flat = jnp.concatenate([PLAIN_SCALE * kr[:, 0:256]] + d_kl + [vr[:, 0:256]] + d_vl, axis=1)
    keys_out_ref[:, 0:C] = mm2(flat, wk_ref[...])
    return jnp.concatenate(off + gpt + gptg, axis=1), jnp.concatenate(d_kg + d_vg, axis=1)


def frame_sums(prods, first_lane):
    return mm2(jnp.concatenate(prods, axis=1), lane_matrix(12 * 128, lambda r: first_lane + (r >> 7)))


def backward_frames(grads, kv_ref, first_lane):
    d_kg = [grads[:, 128 * a : 128 * a + 128] for a in range(3)]
    d_vg = [grads[:, 384 + 128 * a : 512 + 128 * a] for a in range(3)]
    k_local = [kv_ref[:, 1280 + 128 * b : 1408 + 128 * b] for b in range(3)]
    v_local = [kv_ref[:, 1664 + 128 * b : 1792 + 128 * b] for b in range(3)]
    prods = [d_kg[a] * k_local[b] + d_vg[a] * v_local[b] for a in range(3) for b in range(3)]
    return frame_sums(prods + [d_kg[a] + d_vg[a] for a in range(3)], first_lane)


def backward_query(dl, kv_ref, own_fr, fcol, q_ref, pts_ref, wq_ref, sc, first_lane, share):
    rows = own_fr.shape[0]
    dh, dlo = split(dl)
    kh, klo = split(kv_ref[:, 0:640])
    qr = pick(mm3(dh, dlo, kh, klo), key_heads(rows), rows)
    rot, _ = columns(own_fr, fcol)
    d_qg = [sc * block(qr, a) for a in range(3)]
    d_ql = unrotate(rot, d_qg)
    grad = mm2(jnp.concatenate([PLAIN_SCALE * qr[:, 0:256]] + d_ql, axis=1), wq_ref[...])
    q_local = [q_ref[:, 640 + 128 * b : 768 + 128 * b] for b in range(3)]
    off, gpt, gptg = [
        [pts_ref[:, 384 * n + 128 * a : 384 * n + 128 * a + 128] for a in range(3)] for n in range(3)
    ]
    prods = [d_qg[a] * q_local[b] + share * off[a] * gpt[b] for a in range(3) for b in range(3)]
    prods = prods + [d_qg[a] - share * gptg[a] for a in range(3)]
    return grad, frame_sums(prods, first_lane)


def send_blocks(flag_ref, src_ref, mine_a, mine_b, theirs, rows):
    zb = flag_ref[1]
    core = flag_ref[2]

    def get(z, k):
        return src_ref[pl.ds(pl.multiple_of((2 * z + k) * rows, rows), rows), :]

    mine_a[...] = get(zb, core)
    mine_b[...] = get(1 - zb, core)
    theirs[0:rows, :] = get(zb, 1 - core)
    theirs[rows:, :] = get(1 - zb, 1 - core)


def add_pieces(flag_ref, query, query_other, part, one, two):
    return (query[...] + query_other[...]) + (one[...] + jnp.where(flag_ref[0] == 1, part[...], two[...]))


def final_body(flag_ref, r0, r1, r2, r3, r4, one_ref, single_out, frames_out):
    total = add_pieces(flag_ref, r0, r1, r2, r3, r4)
    single_out[...] = one_ref[...] + total[:, 0:C]
    turned = jnp.transpose(total[:, C:])
    for l in range(2):
        frames_out[:, l, :] = turned[12 * l : 12 * l + 12, :]


def frame_part(ref):
    return ref[:, FRAME_LANE : FRAME_LANE + 128]


def back_one_body(
    flag_ref, e_mine, e_other, pm_ref, kv_ref, keys_ref, own_ref, q_ref, gp_ref, d_ref, wk_ref, sc_ref,
    z_ref, mine_a, mine_b, theirs, pts_ref, grads_ref, work_ref,
):
    e = e_mine[...] + e_other[...]
    pts_ref[...], grads_ref[...] = backward(
        flag_ref, e, e[:, 128:256], pm_ref[1], kv_ref, frame_part(keys_ref), frame_part(own_ref), 0, q_ref,
        gp_ref[...], d_ref, wk_ref, sc_ref[0:1, :], z_ref, work_ref,
    )
    send_blocks(flag_ref, work_ref, mine_a, mine_b, theirs, own_ref.shape[0])


def query_one_body(
    share, z_ref, kv_ref, own_ref, q_ref, pts_ref, grads_ref, wq_ref, sc_ref, query_out, frq_ref, frk_ref
):
    half = z_ref.shape[0] // 2
    query_out[...], frq_ref[...] = backward_query(
        z_ref[half:, :], kv_ref, frame_part(own_ref), 0, q_ref, pts_ref, wq_ref, sc_ref[0:1, :], 12, share
    )
    frk_ref[...] = backward_frames(grads_ref[...], kv_ref, 12)


def back_zero_body(
    flag_ref, cot_ref, r0, r1, r2, r3, r4, e_mine, e_other, pm_ref, kv_ref, keys_ref, own_ref, q_ref, pair_ref,
    w_out_ref, wk_ref, sc_ref, frk_ref,
    z_ref, mine_a, mine_b, theirs, pts_ref, sum_ref, pu_ref, work_ref, gp_ref, d_ref,
):
    rows = own_ref.shape[0]
    total = add_pieces(flag_ref, r0, r1, r2, r3, r4)
    sum_ref[...] = total
    upstream_parts(cot_ref[...] + total, w_out_ref, gp_ref, pu_ref, rows)
    pair_products(pu_ref, pair_ref, d_ref, rows)
    gp = gp_ref[...]
    e = e_mine[:, 0:384] + e_other[:, 0:384]
    plain = e_mine[:, 384:640] + e_other[:, 384:640]
    dots = head_dots(gp[:, 0:256] * plain, rows)
    wide = jnp.concatenate(
        [
            pu_ref[h * rows : (h + 1) * rows, :]
            * (e_mine[:, 640 + CZ * h : 640 + CZ * (h + 1)] + e_other[:, 640 + CZ * h : 640 + CZ * (h + 1)])
            for h in range(H)
        ],
        axis=1,
    )
    dots = dots + mm2(wide, lane_matrix(H * CZ, lambda r: STAT + (r >> 7)))
    pts_ref[...], grads = backward(
        flag_ref, e, dots, pm_ref[0], kv_ref, frame_part(keys_ref), frame_part(own_ref), 12, q_ref, gp, d_ref, wk_ref,
        sc_ref[0:1, :], z_ref, work_ref,
    )
    work_ref[:, C:] = backward_frames(grads, kv_ref, 0) + frk_ref[...]
    send_blocks(flag_ref, work_ref, mine_a, mine_b, theirs, rows)


def query_zero_body(share, z_ref, kv_ref, own_ref, q_ref, pts_ref, wq_ref, sc_ref, frq_ref, query_out):
    half = z_ref.shape[0] // 2
    grad, frames = backward_query(
        z_ref[half:, :], kv_ref, frame_part(own_ref), 12, q_ref, pts_ref, wq_ref, sc_ref[0:1, :], 0, share
    )
    query_out[:, 0:C] = grad
    query_out[:, C:] = frames + frq_ref[...]


def pair_body(z1_ref, z0_ref, pu1_ref, pu0_ref, wbt_ref, out_ref):
    rows = out_ref.shape[0]
    wbt = wbt_ref[...].astype(F32)
    for i in range(rows):
        left = jnp.concatenate(
            [z1_ref[pl.ds(i, 2 * H, stride=rows), :], z0_ref[pl.ds(i, 2 * H, stride=rows), :]], axis=0
        )
        right = jnp.concatenate(
            [pu1_ref[pl.ds(i, H, stride=rows), :], wbt, pu0_ref[pl.ds(i, H, stride=rows), :], wbt], axis=0
        ).astype(BF16)
        out_ref[i] = mm(left.astype(BF16), right, TN).astype(BF16)


VMEM = pl.BlockSpec(memory_space=pltpu.VMEM)
SMEM = pl.BlockSpec(memory_space=pltpu.SMEM)
HBM = pl.BlockSpec(memory_space=pltpu.HBM)


def call(body, name, in_specs, outs, args, scratch=(), micros=1.0):
    return pl.pallas_call(
        body,
        name=name,
        in_specs=in_specs,
        out_specs=tuple(VMEM for _ in outs),
        out_shape=tuple(jax.ShapeDtypeStruct(s, d) for s, d in outs),
        scratch_shapes=list(scratch),
        compiler_params=pltpu.CompilerParams(vmem_limit_bytes=16 * 1024 * 1024),
        cost_estimate=pl.CostEstimate(flops=int(micros * 1e9), transcendentals=0, bytes_accessed=int(micros * 3e6)),
    )(*args)


def in_hbm(*arrays):
    return tuple(pltpu.with_memory_space_constraint(x, pltpu.HBM) for x in arrays)


def joint(pairs):
    return [
        ((a * 2 + k) * 2 + x, (b * 2 + k) * 2 + y) for (x, a), (y, b) in pairs for k in range(2)
    ]


BOTH = ("row", "col")
FETCH_ONE = joint([((0, 0), (0, 1)), ((0, 1), (0, 0)), ((1, 0), (0, 2)), ((1, 1), (0, 3)), ((1, 2), (1, 3)), ((1, 3), (1, 2)), ((0, 2), (1, 0)), ((0, 3), (1, 1))])
FETCH_TWO = joint([((0, 0), (0, 3)), ((0, 1), (0, 2)), ((1, 2), (1, 1)), ((1, 3), (1, 0)), ((1, 0), (0, 0)), ((1, 1), (0, 1)), ((0, 2), (1, 2)), ((0, 3), (1, 3))])
SEND_ONE = joint([((0, 0), (1, 0)), ((0, 1), (1, 1)), ((0, 2), (0, 0)), ((0, 3), (0, 1)), ((1, 2), (0, 2)), ((1, 3), (0, 3)), ((1, 0), (1, 2)), ((1, 1), (1, 3))])
SEND_TWO = joint([((0, 2), (1, 0)), ((0, 3), (1, 1)), ((1, 0), (0, 2)), ((1, 1), (0, 3)), ((0, 0), (0, 1)), ((0, 1), (0, 0)), ((1, 2), (1, 3)), ((1, 3), (1, 2))])
CORE_SWAP = [(i, i ^ 1) for i in range(8)]
Z_SWAP = [(i, i ^ 2) for i in range(8)]
COL_SWAP = [(0, 1), (1, 0)]


def local(
    single, frames, saved_probs, pair, cotangent, chains, links, w_query, w_key, w_value, w_query_points,
    w_key_points, w_value_points, w_bias, w_out, head_weights,
):
    rows = single.shape[1]
    keys = pair.shape[1]
    row_total = lax.axis_size("row")
    col_total = lax.axis_size("col")
    fast = row_total == 8 and col_total == 2 and keys == 4 * rows
    (pack,) = call(
        pack_body, "pack", [HBM] * 3, [((rows, PACK), F32)], in_hbm(single, frames.transpose(1, 0, 2), chains[None]),
        [pltpu.VMEM((12, 2, rows), F32), pltpu.VMEM((1, rows), jnp.int32), pltpu.SemaphoreType.DMA((4,))],
    )
    col = lax.axis_index("col")
    row = lax.axis_index("row")
    if fast:
        home = (row // 4 == col).astype(jnp.int32)
        flags = jnp.stack([home, (row // 2) % 2, row % 2])
        ownx = lax.ppermute(pack, "row", CORE_SWAP)
        one = lax.ppermute(pack, BOTH, FETCH_ONE)
        two = lax.ppermute(pack, BOTH, FETCH_TWO)
        own = pack
    else:
        flags = jnp.array([1, 0, 0], jnp.int32)
        whole = lax.all_gather(pack, "row", axis=0, tiled=True)
        mine = lax.dynamic_slice_in_dim(whole, col * keys, keys, 0)
        quarter = keys // 4
        blocks = tuple(mine[quarter * n : quarter * (n + 1)] for n in (0, 1, 2, 3, 0, 0))
        own = pack

    def col_other(x):
        if col_total == 2:
            return lax.ppermute(x, "col", COL_SWAP)
        return lax.psum(x, "col") - x

    def reduce(mine_a, mine_b, theirs, late, beside):
        if fast:
            got = lax.ppermute(theirs, "row", CORE_SWAP)
            query, *rest = late()
            got, query = lax.optimization_barrier((got, query))
            query_other = lax.ppermute(query, "col", COL_SWAP)
            half = lax.ppermute(mine_b + got[rows:], "row", Z_SWAP)
            half, beside = lax.optimization_barrier((half, beside))
            part = mine_a + got[:rows] + half
            sent = [lax.ppermute(part, BOTH, SEND_ONE), lax.ppermute(part, BOTH, SEND_TWO)]
            return [query, query_other, part] + sent, rest, beside
        query, *rest = late()
        parts = jnp.concatenate([mine_a, theirs[:rows], mine_b, theirs[rows:]], axis=0)
        summed = lax.all_gather(lax.psum(parts, "row"), "col", axis=0, tiled=True)
        back = lax.dynamic_slice_in_dim(summed, row * rows, rows, 0)
        zero = jnp.zeros_like(query)
        return [lax.psum(query, "col"), zero, back, zero, zero], rest, beside

    probs = saved_probs.reshape(2, H * rows, keys)
    hr = H * rows
    loads = (
        cotangent, w_out, pair, w_query.T, w_key.T, w_value.T, w_query_points.T, w_key_points.T, w_value_points.T,
    )
    wk, wq, gp1, q1, q0, pu1, d1, sc = call(
        prep_body, "prep", [SMEM, VMEM] + [HBM] * 9,
        [((1280, C), BF16), ((LANES, C), BF16), ((rows, 768), F32), ((rows, 1024), F32), ((rows, 1024), F32),
         ((hr, CZ), F32), ((hr, keys), F32), ((8, 128), F32)],
        (head_weights, own, *in_hbm(*loads)),
        [pltpu.VMEM(x.shape, x.dtype) for x in loads] + [pltpu.SemaphoreType.DMA((len(loads),))],
    )
    if fast:
        one, two, wk, wq, gp1, q1, q0, pu1, d1, sc = lax.optimization_barrier(
            (one, two, wk, wq, gp1, q1, q0, pu1, d1, sc)
        )
        blocks = (pack, ownx, one, lax.ppermute(one, "row", CORE_SWAP), two, lax.ppermute(two, "row", CORE_SWAP))
    key_pack, kv1, pm, e1 = call(
        first_body, "first", [SMEM] + [VMEM] * 11,
        [((keys, PACK), F32), ((keys, 2048), F32), ((2, hr, keys), BF16), ((rows, 384), F32)],
        (flags, *blocks, wk, links, probs, gp1, d1),
    )
    e1_other = col_other(e1)
    kv0, e0 = call(
        second_body, "second", [VMEM] * 4,
        [((keys, 2048), F32), ((rows, 640 + H * CZ), F32)],
        (key_pack, wk, pm, pair),
        [pltpu.VMEM((hr, keys), F32), pltpu.VMEM((hr, CZ), F32)],
    )
    e0_other = col_other(e0)
    share = 1.0 / col_total
    e1_other, e0 = lax.optimization_barrier((e1_other, e0))
    z1, mine_a, mine_b, theirs, pts, grads = call(
        back_one_body, "back_one", [SMEM] + [VMEM] * 11,
        [((2 * hr, keys), F32), ((rows, C), F32), ((rows, C), F32), ((2 * rows, C), F32), ((rows, 1152), F32),
         ((keys, 768), F32)],
        (flags, e1, e1_other, pm, kv1, key_pack, own, q1, gp1, d1, wk, sc),
        [pltpu.VMEM((keys, C), F32)],
        6.0,
    )
    pieces, (frq, frk), e0_other = reduce(
        mine_a, mine_b, theirs,
        lambda: call(
            functools.partial(query_one_body, share), "query_one", [VMEM] * 8,
            [((rows, C), F32), ((rows, 128), F32), ((keys, 128), F32)],
            (z1, kv1, own, q1, pts, grads, wq, sc),
            (),
            0.01,
        ),
        e0_other,
    )
    z0, mine_a, mine_b, theirs, pts, single_one, pu0 = call(
        back_zero_body, "back_zero", [SMEM] + [VMEM] * 18,
        [((2 * hr, keys), F32), ((rows, 512), F32), ((rows, 512), F32), ((2 * rows, 512), F32), ((rows, 1152), F32),
         ((rows, C), F32), ((hr, CZ), F32)],
        (flags, cotangent, *pieces, e0, e0_other, pm, kv0, key_pack, own, q0, pair, w_out, wk, sc, frk),
        [pltpu.VMEM((keys, 512), F32), pltpu.VMEM((rows, 768), F32), pltpu.VMEM((hr, keys), F32)],
    )
    (d_pair,) = call(
        pair_body, "pair_grad", [VMEM] * 5, [((rows, keys, CZ), BF16)], (z1, z0, pu1, pu0, w_bias.T)
    )
    pieces, _, d_pair = reduce(
        mine_a, mine_b, theirs,
        lambda: call(
            functools.partial(query_zero_body, share), "query_zero", [VMEM] * 8, [((rows, 512), F32)],
            (z0, kv0, own, q0, pts, wq, sc, frq),
        ),
        d_pair,
    )
    d_single, d_frames = call(
        final_body, "final", [SMEM] + [VMEM] * 6, [((rows, C), F32), ((12, 2, rows), F32)],
        (flags, *pieces, single_one),
    )
    return (d_single, d_frames.transpose(1, 0, 2), d_pair)


def solution(mesh):
    return jax.shard_map(
        local,
        mesh=mesh,
        in_specs=(
            P(None, ("grp", "row"), None),
            P(None, None, ("grp", "row")),
            P(None, None, ("grp", "row"), "col"),
            P(("grp", "row"), "col", None),
            P(("grp", "row"), None),
            P(("grp", "row")),
            P("grp", None),
            P(),
            P(),
            P(),
            P(),
            P(),
            P(),
            P(),
            P(),
            P(),
        ),
        out_specs=(
            P(("grp", "row"), None),
            P(None, None, ("grp", "row")),
            P(("grp", "row"), "col", None),
        ),
        check_vma=False,
    )
```

```python
import functools
import math

import jax
import jax.numpy as jnp
from jax import lax
from jax.experimental import pallas as pl
from jax.experimental.pallas import tpu as pltpu
from jax.sharding import PartitionSpec as P

C = 384
H = 12
HD = 16
CZ = 128
PQ = 4
PV = 8
NCHAIN = 16
NORM_EPS = 1e-08
LOGIT_SCALE = math.sqrt(1.0 / 3.0)
PLAIN_SCALE = 1.0 / math.sqrt(HD)
POINT_SCALE = math.sqrt(2.0 / (9.0 * PQ))

LANES = 640
PACK = 896
FRAME_LANE = 768
CHAIN_LANE = 792
STAT = 96
EARLY = 4

F32 = jnp.float32
BF16 = jnp.bfloat16
NN = (((1,), (0,)), ((), ()))
NT = (((1,), (1,)), ((), ()))
TN = (((0,), (0,)), ((), ()))


def mm(a, b, dims=NN):
    return lax.dot_general(a, b, dims, preferred_element_type=F32)


def split(x):
    hi = x.astype(BF16)
    return hi, (x - hi.astype(F32)).astype(BF16)


def mm2(x, w, dims=NN):
    hi, lo = split(x)
    rows = x.shape[0]
    both = mm(jnp.concatenate([hi, lo], axis=0), w, dims)
    return both[:rows] + both[rows:]


def mm3(ah, al, bh, bl, dims=NN):
    return mm(ah, bh, dims) + mm(ah, bl, dims) + mm(al, bh, dims)


def iota(shape, axis):
    return lax.broadcasted_iota(jnp.int32, shape, axis)


def key_heads(rows):
    lane = iota((rows, LANES), 1)
    return jnp.where(lane < 256, lane >> 4, (lane & 127) >> 2)


def value_heads(rows):
    lane = iota((rows, LANES), 1)
    inner = lane & 127
    points = jnp.where(inner < STAT, inner >> 3, inner - STAT)
    return jnp.where(lane < 256, lane >> 4, points)


def pick(full, heads, rows):
    out = None
    for h in range(H):
        part = jnp.where(heads == h, full[h * rows : (h + 1) * rows], 0.0)
        out = part if out is None else out + part
    return out


def spread(x, heads):
    return jnp.concatenate([jnp.where(heads == h, x, 0.0) for h in range(H)], axis=0)


def spread2(x, heads):
    hi, lo = split(x)
    hi32, lo32 = hi.astype(F32), lo.astype(F32)
    return spread(hi32, heads).astype(BF16), spread(lo32, heads).astype(BF16)


def columns(frames_block, first):
    cols = [frames_block[:, first + n : first + n + 1] for n in range(12)]
    return [[cols[3 * a + b] for b in range(3)] for a in range(3)], cols[9:]


def block(x, a):
    return x[:, 256 + 128 * a : 384 + 128 * a]


def rotate(rot, pts):
    return [sum(rot[a][b] * pts[b] for b in range(3)) for a in range(3)]


def unrotate(rot, pts):
    return [sum(rot[a][b] * pts[a] for a in range(3)) for b in range(3)]


def place(rot, shift, flat):
    local_pts = [block(flat, a) for a in range(3)]
    turned = rotate(rot, local_pts)
    return jnp.concatenate(
        [flat[:, :256]] + [turned[a] + shift[a] for a in range(3)], axis=1
    )


def lane_matrix(rows, fn):
    r = iota((rows, 128), 0)
    c = iota((rows, 128), 1)
    return (fn(r) == c).astype(F32).astype(BF16)


def upstream_parts(g, w_out_ref, gp_ref, pu_ref, rows):
    hi, lo = split(g)
    both = jnp.concatenate([hi, lo], axis=0)

    def part(first, count):
        r = mm(both, w_out_ref[first : first + count, :], NT)
        return r[:rows] + r[rows:]

    gp_ref[...] = jnp.zeros(gp_ref.shape, F32)
    gp_ref[:, 0:192] = part(0, 192)
    for a in range(4):
        gp_ref[:, 256 + 128 * a : 352 + 128 * a] = part(192 + 96 * a, 96)
    wide = part(576, H * CZ)
    for h in range(H):
        pu_ref[h * rows : (h + 1) * rows, :] = (
            wide[:, h * CZ : (h + 1) * CZ].astype(BF16).astype(F32)
        )


def pair_products(pu_ref, pair_ref, d_ref, rows):
    for i in range(rows):
        lhs = pu_ref[pl.ds(i, H, stride=rows), :].astype(BF16)
        d_ref[pl.ds(i, H, stride=rows), :] = mm(lhs, pair_ref[i], NT)


def split3(x):
    hi, _ = split(x)
    rest = x - hi.astype(F32)
    mid, lo = split(rest)
    return hi, mid, lo


def pack_body(single_hbm, frames_hbm, chains_hbm, pack_ref, frames_ref, chains_ref, sems):
    rows = pack_ref.shape[0]
    ends = (
        (frames_hbm, frames_ref), (chains_hbm, chains_ref), (single_hbm.at[1], pack_ref.at[:, 0:C]),
        (single_hbm.at[0], pack_ref.at[:, C : 2 * C]),
    )
    copies = [pltpu.make_async_copy(src, dst, sems.at[n]) for n, (src, dst) in enumerate(ends)]
    for copy in copies:
        copy.start()
    copies[0].wait()
    copies[1].wait()
    out = jnp.zeros((rows, 128), F32)
    for slot, l in ((0, 1), (12, 0)):
        hot = (iota((12, 128), 1) == iota((12, 128), 0) + slot).astype(F32).astype(BF16)
        for part in split3(frames_ref[:, l, :]):
            out = out + mm(part, hot, TN)
    hot = (iota((1, 128), 1) == CHAIN_LANE - FRAME_LANE).astype(F32).astype(BF16)
    pack_ref[:, 2 * C :] = out + mm(chains_ref[...].astype(F32).astype(BF16), hot, TN)
    copies[2].wait()
    copies[3].wait()


def prep_body(
    hw_ref, pack_ref, cot_hbm, w_out_hbm, pair_hbm, wq_hbm, wk_hbm, wv_hbm, wqp_hbm, wkp_hbm, wvp_hbm,
    wk_out, wq_out, gp_ref, q1_ref, q0_ref, pu_ref, d_ref, sc_ref,
    cot_ref, w_out_ref, pair_ref, wq_ref, wk_ref, wv_ref, wqp_ref, wkp_ref, wvp_ref, sems,
):
    rows = pack_ref.shape[0]
    ends = (
        (cot_hbm, cot_ref), (w_out_hbm, w_out_ref), (pair_hbm, pair_ref), (wq_hbm, wq_ref), (wk_hbm, wk_ref),
        (wv_hbm, wv_ref), (wqp_hbm, wqp_ref), (wkp_hbm, wkp_ref), (wvp_hbm, wvp_ref),
    )
    copies = [pltpu.make_async_copy(src, dst, sems.at[n]) for n, (src, dst) in enumerate(ends)]
    for copy in copies:
        copy.start()
    copies[0].wait()
    copies[1].wait()
    upstream_parts(cot_ref[...], w_out_ref, gp_ref, pu_ref, rows)
    copies[2].wait()
    pair_products(pu_ref, pair_ref, d_ref, rows)
    for copy in copies[3:]:
        copy.wait()
    wq_out[...] = jnp.zeros(wq_out.shape, BF16)
    wk_out[...] = jnp.zeros(wk_out.shape, BF16)
    wq_out[0:192, :] = wq_ref[...]
    wk_out[0:192, :] = wk_ref[...]
    wk_out[640:832, :] = wv_ref[...]
    for a in range(3):
        wq_out[256 + 128 * a : 304 + 128 * a, :] = wqp_ref[48 * a : 48 * a + 48, :]
        wk_out[256 + 128 * a : 304 + 128 * a, :] = wkp_ref[48 * a : 48 * a + 48, :]
        wk_out[896 + 128 * a : 992 + 128 * a, :] = wvp_ref[96 * a : 96 * a + 96, :]
    lane = iota((8, 128), 1)
    raw = jnp.zeros((8, 128), F32)
    for h in range(H):
        raw = jnp.where((lane >> 2) == h, hw_ref[h], raw)
    soft = jnp.maximum(raw, 0.0) + jnp.log(1.0 + jnp.exp(-jnp.abs(raw)))
    sc_ref[...] = soft * POINT_SCALE
    fr = pack_ref[:, FRAME_LANE : FRAME_LANE + 128]
    for out, first, fcol in ((q1_ref, 0, 0), (q0_ref, C, 12)):
        flat = mm2(pack_ref[:, first : first + C], wq_out[...], NT)
        rot, shift = columns(fr, fcol)
        out[:, :LANES] = place(rot, shift, flat)
        out[:, LANES:] = flat[:, 256:]


def project_keys(x, fr, fcol, wk_ref, kv_ref):
    flat = mm2(x, wk_ref[...], NT)
    rot, shift = columns(fr, fcol)
    kv_ref[:, 0:640] = place(rot, shift, flat[:, :640])
    kv_ref[:, 640:1280] = place(rot, shift, flat[:, 640:])
    kv_ref[:, 1280:1664] = flat[:, 256:640]
    kv_ref[:, 1664:2048] = flat[:, 896:1280]


def value_sums(probs, kv_ref, rows):
    values = kv_ref[:, 640:1280]
    lane = iota(values.shape, 1)
    values = jnp.where((lane >= 256 + STAT) & (lane < 256 + STAT + H), 1.0, values)
    hi, lo = split(values)
    return pick(mm(probs, hi) + mm(probs, lo), value_heads(rows), rows)


def head_dots(prod, rows):
    return mm2(prod, lane_matrix(256, lambda r: STAT + (r >> 4)))


def first_body(
    flag_ref, own_ref, ownx_ref, p1_ref, p1x_ref, p2_ref, p2x_ref, wk_ref, links_ref, probs_ref, gp_ref, d_ref,
    keys_ref, kv_ref, pm_ref, e_ref,
):
    rows = own_ref.shape[0]
    home = flag_ref[0] == 1
    zb = flag_ref[1]
    core = flag_ref[2]

    def put(z, k, value):
        keys_ref[pl.ds(pl.multiple_of((2 * z + k) * rows, rows), rows), :] = value

    put(zb, core, jnp.where(home, own_ref[...], p1_ref[...]))
    put(zb, 1 - core, jnp.where(home, ownx_ref[...], p1x_ref[...]))
    put(1 - zb, core, jnp.where(home, p1_ref[...], p2_ref[...]))
    put(1 - zb, 1 - core, jnp.where(home, p1x_ref[...], p2x_ref[...]))
    fr = keys_ref[:, FRAME_LANE : FRAME_LANE + 128]
    keys = fr.shape[0]
    at = CHAIN_LANE - FRAME_LANE
    key_chain = fr[:, at : at + 1]
    own_chain = own_ref[:, FRAME_LANE : FRAME_LANE + 128][:, at : at + 1]
    key_hot = (iota((keys, NCHAIN), 1).astype(F32) == key_chain).astype(F32).astype(BF16)
    own_hot = (iota((rows, NCHAIN), 1).astype(F32) == own_chain).astype(F32).astype(BF16)
    eye = iota((NCHAIN, NCHAIN), 0) == iota((NCHAIN, NCHAIN), 1)
    allowed = jnp.where(eye, 1.0, links_ref[...].astype(F32)).astype(BF16)
    mask = mm(mm(own_hot, allowed).astype(BF16), key_hot, NT)
    mask_all = jnp.concatenate([mask] * H, axis=0)
    for l in range(2):
        pm_ref[l] = (probs_ref[l].astype(F32) * mask_all).astype(BF16)
    project_keys(keys_ref[:, 0:C], fr, 0, wk_ref, kv_ref)
    probs = pm_ref[1]
    sums = value_sums(probs, kv_ref, rows)
    weighted = mm2(probs.astype(F32) * d_ref[...], jnp.ones((keys, 128), BF16))
    lane = iota((rows, 128), 1)
    dots = pick(weighted, lane - STAT, rows) + head_dots(gp_ref[:, 0:256] * sums[:, 0:256], rows)
    e_ref[:, 0:128] = block(sums, 0)
    e_ref[:, 128:256] = jnp.where(lane < STAT, block(sums, 1), dots)
    e_ref[:, 256:384] = block(sums, 2)


def second_body(keys_ref, wk_ref, pm_ref, pair_ref, kv_ref, e_ref, tail_ref, p32_ref, op_ref):
    rows = pair_ref.shape[0]
    fr = keys_ref[:, FRAME_LANE : FRAME_LANE + 128]
    project_keys(keys_ref[:, C : 2 * C], fr, 12, wk_ref, kv_ref)
    probs = pm_ref[0]
    sums = value_sums(probs, kv_ref, rows)
    for a in range(3):
        e_ref[:, 128 * a : 128 * a + 128] = block(sums, a)
    e_ref[:, 384:640] = sums[:, 0:256]
    p32_ref[...] = probs.astype(F32)
    for i in range(rows):
        lhs = p32_ref[pl.ds(i, H, stride=rows), :].astype(BF16)
        op_ref[pl.ds(i, H, stride=rows), :] = mm(lhs, pair_ref[i])
    for h in range(H):
        ref, first = (e_ref, 640 + CZ * h) if h < EARLY else (tail_ref, CZ * (h - EARLY))
        ref[:, first : first + CZ] = op_ref[h * rows : (h + 1) * rows, :]


def backward(
    flag_ref, e, dots, probs, kv_ref, key_fr, own_fr, fcol, q_ref, gp, d_ref, wk_ref, sc,
    z_ref, keys_out_ref,
):
    rows = e.shape[0]
    lane = iota((rows, 128), 1)
    stat = (lane >= STAT) & (lane < STAT + H)
    inv = jnp.where(stat, 1.0 / jnp.where(stat, e[:, 0:128], 1.0), 0.0)
    r128 = iota((128, LANES), 0)
    grow = (r128 - STAT == value_heads(128)) & ((iota((128, LANES), 1) & 127) < STAT)
    grow = grow | ((r128 - STAT == (iota((128, LANES), 1) >> 4)) & (iota((128, LANES), 1) < 256))
    inv_lanes = mm2(inv, grow.astype(F32).astype(BF16))
    rot, shift = columns(own_fr, fcol)
    inv_pts = block(inv_lanes, 0)
    ptg = [e[:, 128 * a : 128 * a + 128] * inv_pts for a in range(3)]
    off = [jnp.where(lane < STAT, ptg[a] - shift[a], 0.0) for a in range(3)]
    opt = unrotate(rot, off)
    length = jnp.sqrt(opt[0] * opt[0] + opt[1] * opt[1] + opt[2] * opt[2] + NORM_EPS)
    scale = gp[:, 640:768] / length
    gpt = [block(gp, a) + scale * opt[a] for a in range(3)]
    gptg = rotate(rot, gpt)
    upper = jnp.concatenate([gp[:, 0:256]] + gptg, axis=1)
    point_dots = gptg[0] * ptg[0] + gptg[1] * ptg[1] + gptg[2] * ptg[2]
    rd = dots * inv + mm2(point_dots, lane_matrix(128, lambda r: STAT + (r >> 3)))
    both = jnp.concatenate([spread(rd, lane - STAT), spread(inv, lane - STAT)], axis=0)
    wide = mm2(both, jnp.ones((128, 128), BF16))
    rd_all, inv_all = wide[: H * rows], wide[H * rows :]
    heads_v = value_heads(rows)
    heads_k = key_heads(rows)
    uh, ul = spread2(upper, heads_v)
    vh, vl = split(kv_ref[:, 640:1280])
    d_att = d_ref[...] + mm3(uh, ul, vh, vl, NT)
    p32 = probs.astype(F32)
    att = p32 * inv_all
    dl = LOGIT_SCALE * att * (d_att - rd_all)
    z_ref[0 : H * rows, :] = att
    z_ref[H * rows :, :] = dl
    dt = jnp.transpose(dl)
    th, tl = split(dt)
    qh, qlo = spread2(q_ref[:, 0:640], heads_k)
    kr = mm3(th, tl, qh, qlo)
    head_rows = iota((H * rows, 128), 0) // rows
    hot = ((iota((H * rows, 128), 1) >> 2) == head_rows).astype(F32).astype(BF16)
    cs = mm(th, hot) + mm(tl, hot)
    pt = jnp.transpose(p32).astype(BF16)
    sh, sl = spread2(upper * inv_lanes, heads_v)
    vr = mm(pt, sh) + mm(pt, sl)
    krot, _ = columns(key_fr, fcol)
    d_kg = [sc * (block(kr, a) - cs * kv_ref[:, 256 + 128 * a : 384 + 128 * a]) for a in range(3)]
    d_vg = [block(vr, a) for a in range(3)]
    d_kl = unrotate(krot, d_kg)
    d_vl = unrotate(krot, d_vg)
    flat = jnp.concatenate([PLAIN_SCALE * kr[:, 0:256]] + d_kl + [vr[:, 0:256]] + d_vl, axis=1)
    keys_out_ref[:, 0:C] = mm2(flat, wk_ref[...])
    return jnp.concatenate(off + gpt + gptg, axis=1), jnp.concatenate(d_kg + d_vg, axis=1)


def frame_sums(prods, first_lane):
    return mm2(jnp.concatenate(prods, axis=1), lane_matrix(12 * 128, lambda r: first_lane + (r >> 7)))


def backward_frames(grads, kv_ref, first_lane):
    d_kg = [grads[:, 128 * a : 128 * a + 128] for a in range(3)]
    d_vg = [grads[:, 384 + 128 * a : 512 + 128 * a] for a in range(3)]
    k_local = [kv_ref[:, 1280 + 128 * b : 1408 + 128 * b] for b in range(3)]
    v_local = [kv_ref[:, 1664 + 128 * b : 1792 + 128 * b] for b in range(3)]
    prods = [d_kg[a] * k_local[b] + d_vg[a] * v_local[b] for a in range(3) for b in range(3)]
    return frame_sums(prods + [d_kg[a] + d_vg[a] for a in range(3)], first_lane)


def backward_query(dl, kv_ref, own_fr, fcol, q_ref, pts_ref, wq_ref, sc, first_lane, share):
    rows = own_fr.shape[0]
    dh, dlo = split(dl)
    kh, klo = split(kv_ref[:, 0:640])
    qr = pick(mm3(dh, dlo, kh, klo), key_heads(rows), rows)
    rot, _ = columns(own_fr, fcol)
    d_qg = [sc * block(qr, a) for a in range(3)]
    d_ql = unrotate(rot, d_qg)
    grad = mm2(jnp.concatenate([PLAIN_SCALE * qr[:, 0:256]] + d_ql, axis=1), wq_ref[...])
    q_local = [q_ref[:, 640 + 128 * b : 768 + 128 * b] for b in range(3)]
    off, gpt, gptg = [
        [pts_ref[:, 384 * n + 128 * a : 384 * n + 128 * a + 128] for a in range(3)] for n in range(3)
    ]
    prods = [d_qg[a] * q_local[b] + share * off[a] * gpt[b] for a in range(3) for b in range(3)]
    prods = prods + [d_qg[a] - share * gptg[a] for a in range(3)]
    return grad, frame_sums(prods, first_lane)


def send_blocks(flag_ref, src_ref, mine_a, mine_b, theirs, rows):
    zb = flag_ref[1]
    core = flag_ref[2]

    def get(z, k):
        return src_ref[pl.ds(pl.multiple_of((2 * z + k) * rows, rows), rows), :]

    mine_a[...] = get(zb, core)
    mine_b[...] = get(1 - zb, core)
    theirs[0:rows, :] = get(zb, 1 - core)
    theirs[rows:, :] = get(1 - zb, 1 - core)


def add_pieces(flag_ref, query, query_other, part, one, two):
    return (query[...] + query_other[...]) + (one[...] + jnp.where(flag_ref[0] == 1, part[...], two[...]))


def final_body(flag_ref, r0, r1, r2, r3, r4, one_ref, single_out, frames_out):
    total = add_pieces(flag_ref, r0, r1, r2, r3, r4)
    single_out[...] = one_ref[...] + total[:, 0:C]
    turned = jnp.transpose(total[:, C:])
    for l in range(2):
        frames_out[:, l, :] = turned[12 * l : 12 * l + 12, :]


def frame_part(ref):
    return ref[:, FRAME_LANE : FRAME_LANE + 128]


def back_one_body(
    flag_ref, e_mine, e_other, pm_ref, kv_ref, keys_ref, own_ref, q_ref, gp_ref, d_ref, wk_ref, sc_ref,
    z_ref, mine_a, mine_b, theirs, pts_ref, grads_ref, work_ref,
):
    e = e_mine[...] + e_other[...]
    pts_ref[...], grads_ref[...] = backward(
        flag_ref, e, e[:, 128:256], pm_ref[1], kv_ref, frame_part(keys_ref), frame_part(own_ref), 0, q_ref,
        gp_ref[...], d_ref, wk_ref, sc_ref[0:1, :], z_ref, work_ref,
    )
    send_blocks(flag_ref, work_ref, mine_a, mine_b, theirs, own_ref.shape[0])


def query_one_body(
    share, z_ref, kv_ref, own_ref, q_ref, pts_ref, grads_ref, wq_ref, sc_ref, query_out, frq_ref, frk_ref
):
    half = z_ref.shape[0] // 2
    query_out[...], frq_ref[...] = backward_query(
        z_ref[half:, :], kv_ref, frame_part(own_ref), 0, q_ref, pts_ref, wq_ref, sc_ref[0:1, :], 12, share
    )
    frk_ref[...] = backward_frames(grads_ref[...], kv_ref, 12)


def back_zero_body(
    flag_ref, cot_ref, r0, r1, r2, r3, r4, e_mine, e_other, tail_mine, tail_other, pm_ref, kv_ref, keys_ref, own_ref, q_ref, pair_ref,
    w_out_ref, wk_ref, sc_ref, frk_ref,
    z_ref, mine_a, mine_b, theirs, pts_ref, sum_ref, pu_ref, work_ref, gp_ref, d_ref,
):
    rows = own_ref.shape[0]
    total = add_pieces(flag_ref, r0, r1, r2, r3, r4)
    sum_ref[...] = total
    upstream_parts(cot_ref[...] + total, w_out_ref, gp_ref, pu_ref, rows)
    pair_products(pu_ref, pair_ref, d_ref, rows)
    gp = gp_ref[...]
    e = e_mine[:, 0:384] + e_other[:, 0:384]
    plain = e_mine[:, 384:640] + e_other[:, 384:640]
    dots = head_dots(gp[:, 0:256] * plain, rows)
    wide = jnp.concatenate(
        [
            pu_ref[h * rows : (h + 1) * rows, :]
            * (
                e_mine[:, 640 + CZ * h : 640 + CZ * (h + 1)] + e_other[:, 640 + CZ * h : 640 + CZ * (h + 1)]
                if h < EARLY
                else tail_mine[:, CZ * (h - EARLY) : CZ * (h - EARLY + 1)]
                + tail_other[:, CZ * (h - EARLY) : CZ * (h - EARLY + 1)]
            )
            for h in range(H)
        ],
        axis=1,
    )
    dots = dots + mm2(wide, lane_matrix(H * CZ, lambda r: STAT + (r >> 7)))
    pts_ref[...], grads = backward(
        flag_ref, e, dots, pm_ref[0], kv_ref, frame_part(keys_ref), frame_part(own_ref), 12, q_ref, gp, d_ref, wk_ref,
        sc_ref[0:1, :], z_ref, work_ref,
    )
    work_ref[:, C:] = backward_frames(grads, kv_ref, 0) + frk_ref[...]
    send_blocks(flag_ref, work_ref, mine_a, mine_b, theirs, rows)


def query_zero_body(share, z_ref, kv_ref, own_ref, q_ref, pts_ref, wq_ref, sc_ref, frq_ref, query_out):
    half = z_ref.shape[0] // 2
    grad, frames = backward_query(
        z_ref[half:, :], kv_ref, frame_part(own_ref), 12, q_ref, pts_ref, wq_ref, sc_ref[0:1, :], 0, share
    )
    query_out[:, 0:C] = grad
    query_out[:, C:] = frames + frq_ref[...]


def pair_body(z1_ref, z0_ref, pu1_ref, pu0_ref, wbt_ref, out_ref):
    rows = out_ref.shape[0]
    wbt = wbt_ref[...].astype(F32)
    for i in range(rows):
        left = jnp.concatenate(
            [z1_ref[pl.ds(i, 2 * H, stride=rows), :], z0_ref[pl.ds(i, 2 * H, stride=rows), :]], axis=0
        )
        right = jnp.concatenate(
            [pu1_ref[pl.ds(i, H, stride=rows), :], wbt, pu0_ref[pl.ds(i, H, stride=rows), :], wbt], axis=0
        ).astype(BF16)
        out_ref[i] = mm(left.astype(BF16), right, TN).astype(BF16)


VMEM = pl.BlockSpec(memory_space=pltpu.VMEM)
SMEM = pl.BlockSpec(memory_space=pltpu.SMEM)
HBM = pl.BlockSpec(memory_space=pltpu.HBM)


def call(body, name, in_specs, outs, args, scratch=(), micros=1.0):
    return pl.pallas_call(
        body,
        name=name,
        in_specs=in_specs,
        out_specs=tuple(VMEM for _ in outs),
        out_shape=tuple(jax.ShapeDtypeStruct(s, d) for s, d in outs),
        scratch_shapes=list(scratch),
        compiler_params=pltpu.CompilerParams(vmem_limit_bytes=16 * 1024 * 1024),
        cost_estimate=pl.CostEstimate(flops=int(micros * 1e9), transcendentals=0, bytes_accessed=int(micros * 3e6)),
    )(*args)


def in_hbm(*arrays):
    return tuple(pltpu.with_memory_space_constraint(x, pltpu.HBM) for x in arrays)


def joint(pairs):
    return [
        ((a * 2 + k) * 2 + x, (b * 2 + k) * 2 + y) for (x, a), (y, b) in pairs for k in range(2)
    ]


BOTH = ("row", "col")
FETCH_ONE = joint([((0, 0), (0, 1)), ((0, 1), (0, 0)), ((1, 0), (0, 2)), ((1, 1), (0, 3)), ((1, 2), (1, 3)), ((1, 3), (1, 2)), ((0, 2), (1, 0)), ((0, 3), (1, 1))])
FETCH_TWO = joint([((0, 0), (0, 3)), ((0, 1), (0, 2)), ((1, 2), (1, 1)), ((1, 3), (1, 0)), ((1, 0), (0, 0)), ((1, 1), (0, 1)), ((0, 2), (1, 2)), ((0, 3), (1, 3))])
SEND_ONE = joint([((0, 0), (1, 0)), ((0, 1), (1, 1)), ((0, 2), (0, 0)), ((0, 3), (0, 1)), ((1, 2), (0, 2)), ((1, 3), (0, 3)), ((1, 0), (1, 2)), ((1, 1), (1, 3))])
SEND_TWO = joint([((0, 2), (1, 0)), ((0, 3), (1, 1)), ((1, 0), (0, 2)), ((1, 1), (0, 3)), ((0, 0), (0, 1)), ((0, 1), (0, 0)), ((1, 2), (1, 3)), ((1, 3), (1, 2))])
CORE_SWAP = [(i, i ^ 1) for i in range(8)]
Z_SWAP = [(i, i ^ 2) for i in range(8)]
COL_SWAP = [(0, 1), (1, 0)]


def local(
    single, frames, saved_probs, pair, cotangent, chains, links, w_query, w_key, w_value, w_query_points,
    w_key_points, w_value_points, w_bias, w_out, head_weights,
):
    rows = single.shape[1]
    keys = pair.shape[1]
    row_total = lax.axis_size("row")
    col_total = lax.axis_size("col")
    fast = row_total == 8 and col_total == 2 and keys == 4 * rows
    (pack,) = call(
        pack_body, "pack", [HBM] * 3, [((rows, PACK), F32)], in_hbm(single, frames.transpose(1, 0, 2), chains[None]),
        [pltpu.VMEM((12, 2, rows), F32), pltpu.VMEM((1, rows), jnp.int32), pltpu.SemaphoreType.DMA((4,))],
    )
    col = lax.axis_index("col")
    row = lax.axis_index("row")
    if fast:
        home = (row // 4 == col).astype(jnp.int32)
        flags = jnp.stack([home, (row // 2) % 2, row % 2])
        ownx = lax.ppermute(pack, "row", CORE_SWAP)
        one = lax.ppermute(pack, BOTH, FETCH_ONE)
        two = lax.ppermute(pack, BOTH, FETCH_TWO)
        own = pack
    else:
        flags = jnp.array([1, 0, 0], jnp.int32)
        whole = lax.all_gather(pack, "row", axis=0, tiled=True)
        mine = lax.dynamic_slice_in_dim(whole, col * keys, keys, 0)
        quarter = keys // 4
        blocks = tuple(mine[quarter * n : quarter * (n + 1)] for n in (0, 1, 2, 3, 0, 0))
        own = pack

    def col_other(x):
        if col_total == 2:
            return lax.ppermute(x, "col", COL_SWAP)
        return lax.psum(x, "col") - x

    def reduce(mine_a, mine_b, theirs, late, first_beside, beside):
        if fast:
            got = lax.ppermute(theirs, "row", CORE_SWAP)
            query, *rest = late()
            got, query, first_beside = lax.optimization_barrier((got, query, first_beside))
            query_other = lax.ppermute(query, "col", COL_SWAP)
            half = lax.ppermute(mine_b + got[rows:], "row", Z_SWAP)
            half, beside = lax.optimization_barrier((half, beside))
            part = mine_a + got[:rows] + half
            sent = [lax.ppermute(part, BOTH, SEND_ONE), lax.ppermute(part, BOTH, SEND_TWO)]
            return [query, query_other, part] + sent, rest, (first_beside, beside)
        query, *rest = late()
        parts = jnp.concatenate([mine_a, theirs[:rows], mine_b, theirs[rows:]], axis=0)
        summed = lax.all_gather(lax.psum(parts, "row"), "col", axis=0, tiled=True)
        back = lax.dynamic_slice_in_dim(summed, row * rows, rows, 0)
        zero = jnp.zeros_like(query)
        return [lax.psum(query, "col"), zero, back, zero, zero], rest, (first_beside, beside)

    probs = saved_probs.reshape(2, H * rows, keys)
    hr = H * rows
    loads = (
        cotangent, w_out, pair, w_query.T, w_key.T, w_value.T, w_query_points.T, w_key_points.T, w_value_points.T,
    )
    wk, wq, gp1, q1, q0, pu1, d1, sc = call(
        prep_body, "prep", [SMEM, VMEM] + [HBM] * 9,
        [((1280, C), BF16), ((LANES, C), BF16), ((rows, 768), F32), ((rows, 1024), F32), ((rows, 1024), F32),
         ((hr, CZ), F32), ((hr, keys), F32), ((8, 128), F32)],
        (head_weights, own, *in_hbm(*loads)),
        [pltpu.VMEM(x.shape, x.dtype) for x in loads] + [pltpu.SemaphoreType.DMA((len(loads),))],
    )
    if fast:
        one, two, wk, wq, gp1, q1, q0, pu1, d1, sc = lax.optimization_barrier(
            (one, two, wk, wq, gp1, q1, q0, pu1, d1, sc)
        )
        blocks = (pack, ownx, one, lax.ppermute(one, "row", CORE_SWAP), two, lax.ppermute(two, "row", CORE_SWAP))
    key_pack, kv1, pm, e1 = call(
        first_body, "first", [SMEM] + [VMEM] * 11,
        [((keys, PACK), F32), ((keys, 2048), F32), ((2, hr, keys), BF16), ((rows, 384), F32)],
        (flags, *blocks, wk, links, probs, gp1, d1),
    )
    e1_other = col_other(e1)
    kv0, e0, tail = call(
        second_body, "second", [VMEM] * 4,
        [((keys, 2048), F32), ((rows, 640 + EARLY * CZ), F32), ((rows, (H - EARLY) * CZ), F32)],
        (key_pack, wk, pm, pair),
        [pltpu.VMEM((hr, keys), F32), pltpu.VMEM((hr, CZ), F32)],
    )
    e0_other = col_other(e0)
    tail_other = col_other(tail)
    share = 1.0 / col_total
    e1_other, e0 = lax.optimization_barrier((e1_other, e0))
    z1, mine_a, mine_b, theirs, pts, grads = call(
        back_one_body, "back_one", [SMEM] + [VMEM] * 11,
        [((2 * hr, keys), F32), ((rows, C), F32), ((rows, C), F32), ((2 * rows, C), F32), ((rows, 1152), F32),
         ((keys, 768), F32)],
        (flags, e1, e1_other, pm, kv1, key_pack, own, q1, gp1, d1, wk, sc),
        [pltpu.VMEM((keys, C), F32)],
        6.0,
    )
    pieces, (frq, frk), (e0_other, tail_other) = reduce(
        mine_a, mine_b, theirs,
        lambda: call(
            functools.partial(query_one_body, share), "query_one", [VMEM] * 8,
            [((rows, C), F32), ((rows, 128), F32), ((keys, 128), F32)],
            (z1, kv1, own, q1, pts, grads, wq, sc),
            (),
            0.01,
        ),
        e0_other,
        tail_other,
    )
    z0, mine_a, mine_b, theirs, pts, single_one, pu0 = call(
        back_zero_body, "back_zero", [SMEM] + [VMEM] * 20,
        [((2 * hr, keys), F32), ((rows, 512), F32), ((rows, 512), F32), ((2 * rows, 512), F32), ((rows, 1152), F32),
         ((rows, C), F32), ((hr, CZ), F32)],
        (flags, cotangent, *pieces, e0, e0_other, tail, tail_other, pm, kv0, key_pack, own, q0, pair, w_out, wk, sc, frk),
        [pltpu.VMEM((keys, 512), F32), pltpu.VMEM((rows, 768), F32), pltpu.VMEM((hr, keys), F32)],
    )
    (d_pair,) = call(
        pair_body, "pair_grad", [VMEM] * 5, [((rows, keys, CZ), BF16)], (z1, z0, pu1, pu0, w_bias.T)
    )
    pieces, _, (_, d_pair) = reduce(
        mine_a, mine_b, theirs,
        lambda: call(
            functools.partial(query_zero_body, share), "query_zero", [VMEM] * 8, [((rows, 512), F32)],
            (z0, kv0, own, q0, pts, wq, sc, frq),
        ),
        (),
        d_pair,
    )
    d_single, d_frames = call(
        final_body, "final", [SMEM] + [VMEM] * 6, [((rows, C), F32), ((12, 2, rows), F32)],
        (flags, *pieces, single_one),
    )
    return (d_single, d_frames.transpose(1, 0, 2), d_pair)


def solution(mesh):
    return jax.shard_map(
        local,
        mesh=mesh,
        in_specs=(
            P(None, ("grp", "row"), None),
            P(None, None, ("grp", "row")),
            P(None, None, ("grp", "row"), "col"),
            P(("grp", "row"), "col", None),
            P(("grp", "row"), None),
            P(("grp", "row")),
            P("grp", None),
            P(),
            P(),
            P(),
            P(),
            P(),
            P(),
            P(),
            P(),
            P(),
        ),
        out_specs=(
            P(("grp", "row"), None),
            P(None, None, ("grp", "row")),
            P(("grp", "row"), "col", None),
        ),
        check_vma=False,
    )
```

```python
import functools
import math

import jax
import jax.numpy as jnp
from jax import lax
from jax.experimental import pallas as pl
from jax.experimental.pallas import tpu as pltpu
from jax.sharding import PartitionSpec as P

C = 384
H = 12
HD = 16
CZ = 128
PQ = 4
PV = 8
NCHAIN = 16
NORM_EPS = 1e-08
LOGIT_SCALE = math.sqrt(1.0 / 3.0)
PLAIN_SCALE = 1.0 / math.sqrt(HD)
POINT_SCALE = math.sqrt(2.0 / (9.0 * PQ))

LANES = 640
PACK = 896
FRAME_LANE = 768
CHAIN_LANE = 792
STAT = 96
EARLY = 4

F32 = jnp.float32
BF16 = jnp.bfloat16
NN = (((1,), (0,)), ((), ()))
NT = (((1,), (1,)), ((), ()))
TN = (((0,), (0,)), ((), ()))


def mm(a, b, dims=NN):
    return lax.dot_general(a, b, dims, preferred_element_type=F32)


def split(x):
    hi = x.astype(BF16)
    return hi, (x - hi.astype(F32)).astype(BF16)


def mm2(x, w, dims=NN):
    hi, lo = split(x)
    rows = x.shape[0]
    both = mm(jnp.concatenate([hi, lo], axis=0), w, dims)
    return both[:rows] + both[rows:]


def mm3(ah, al, bh, bl, dims=NN):
    return mm(ah, bh, dims) + mm(ah, bl, dims) + mm(al, bh, dims)


def iota(shape, axis):
    return lax.broadcasted_iota(jnp.int32, shape, axis)


def key_heads(rows):
    lane = iota((rows, LANES), 1)
    return jnp.where(lane < 256, lane >> 4, (lane & 127) >> 2)


def value_heads(rows):
    lane = iota((rows, LANES), 1)
    inner = lane & 127
    points = jnp.where(inner < STAT, inner >> 3, inner - STAT)
    return jnp.where(lane < 256, lane >> 4, points)


def pick(full, heads, rows):
    out = None
    for h in range(H):
        part = jnp.where(heads == h, full[h * rows : (h + 1) * rows], 0.0)
        out = part if out is None else out + part
    return out


def spread(x, heads):
    return jnp.concatenate([jnp.where(heads == h, x, 0.0) for h in range(H)], axis=0)


def spread2(x, heads):
    hi, lo = split(x)
    hi32, lo32 = hi.astype(F32), lo.astype(F32)
    return spread(hi32, heads).astype(BF16), spread(lo32, heads).astype(BF16)


def columns(frames_block, first):
    cols = [frames_block[:, first + n : first + n + 1] for n in range(12)]
    return [[cols[3 * a + b] for b in range(3)] for a in range(3)], cols[9:]


def block(x, a):
    return x[:, 256 + 128 * a : 384 + 128 * a]


def rotate(rot, pts):
    return [sum(rot[a][b] * pts[b] for b in range(3)) for a in range(3)]


def unrotate(rot, pts):
    return [sum(rot[a][b] * pts[a] for a in range(3)) for b in range(3)]


def place(rot, shift, flat):
    local_pts = [block(flat, a) for a in range(3)]
    turned = rotate(rot, local_pts)
    return jnp.concatenate(
        [flat[:, :256]] + [turned[a] + shift[a] for a in range(3)], axis=1
    )


def lane_matrix(rows, fn):
    r = iota((rows, 128), 0)
    c = iota((rows, 128), 1)
    return (fn(r) == c).astype(F32).astype(BF16)


def upstream_parts(g, w_out_ref, gp_ref, pu_ref, rows):
    hi, lo = split(g)
    both = jnp.concatenate([hi, lo], axis=0)

    def part(first, count):
        r = mm(both, w_out_ref[first : first + count, :], NT)
        return r[:rows] + r[rows:]

    gp_ref[...] = jnp.zeros(gp_ref.shape, F32)
    gp_ref[:, 0:192] = part(0, 192)
    for a in range(4):
        gp_ref[:, 256 + 128 * a : 352 + 128 * a] = part(192 + 96 * a, 96)
    wide = part(576, H * CZ)
    for h in range(H):
        pu_ref[h * rows : (h + 1) * rows, :] = (
            wide[:, h * CZ : (h + 1) * CZ].astype(BF16).astype(F32)
        )


def pair_products(pu_ref, pair_ref, d_ref, rows):
    for i in range(0, rows, 2):
        lhs = jnp.concatenate([pu_ref[pl.ds(i, H, stride=rows), :], pu_ref[pl.ds(i + 1, H, stride=rows), :]], axis=0)
        both = mm(lhs.astype(BF16), pair_ref[i : i + 2].reshape(-1, CZ), NT)
        keys = both.shape[1] // 2
        d_ref[pl.ds(i, H, stride=rows), :] = both[:H, :keys]
        d_ref[pl.ds(i + 1, H, stride=rows), :] = both[H:, keys:]


def split3(x):
    hi, _ = split(x)
    rest = x - hi.astype(F32)
    mid, lo = split(rest)
    return hi, mid, lo


def pack_body(single_hbm, frames_hbm, chains_hbm, pack_ref, frames_ref, chains_ref, sems):
    rows = pack_ref.shape[0]
    ends = (
        (frames_hbm, frames_ref), (chains_hbm, chains_ref), (single_hbm.at[1], pack_ref.at[:, 0:C]),
        (single_hbm.at[0], pack_ref.at[:, C : 2 * C]),
    )
    copies = [pltpu.make_async_copy(src, dst, sems.at[n]) for n, (src, dst) in enumerate(ends)]
    for copy in copies:
        copy.start()
    copies[0].wait()
    copies[1].wait()
    out = jnp.zeros((rows, 128), F32)
    for slot, l in ((0, 1), (12, 0)):
        hot = (iota((12, 128), 1) == iota((12, 128), 0) + slot).astype(F32).astype(BF16)
        for part in split3(frames_ref[:, l, :]):
            out = out + mm(part, hot, TN)
    hot = (iota((1, 128), 1) == CHAIN_LANE - FRAME_LANE).astype(F32).astype(BF16)
    pack_ref[:, 2 * C :] = out + mm(chains_ref[...].astype(F32).astype(BF16), hot, TN)
    copies[2].wait()
    copies[3].wait()


def prep_body(
    hw_ref, pack_ref, cot_hbm, w_out_hbm, pair_hbm, wq_hbm, wk_hbm, wv_hbm, wqp_hbm, wkp_hbm, wvp_hbm,
    wk_out, wq_out, gp_ref, q1_ref, q0_ref, pu_ref, d_ref, sc_ref,
    cot_ref, w_out_ref, pair_ref, wq_ref, wk_ref, wv_ref, wqp_ref, wkp_ref, wvp_ref, sems,
):
    rows = pack_ref.shape[0]
    ends = (
        (cot_hbm, cot_ref), (w_out_hbm, w_out_ref), (pair_hbm, pair_ref), (wq_hbm, wq_ref), (wk_hbm, wk_ref),
        (wv_hbm, wv_ref), (wqp_hbm, wqp_ref), (wkp_hbm, wkp_ref), (wvp_hbm, wvp_ref),
    )
    copies = [pltpu.make_async_copy(src, dst, sems.at[n]) for n, (src, dst) in enumerate(ends)]
    for copy in copies:
        copy.start()
    copies[0].wait()
    copies[1].wait()
    upstream_parts(cot_ref[...], w_out_ref, gp_ref, pu_ref, rows)
    copies[2].wait()
    pair_products(pu_ref, pair_ref, d_ref, rows)
    for copy in copies[3:]:
        copy.wait()
    wq_out[...] = jnp.zeros(wq_out.shape, BF16)
    wk_out[...] = jnp.zeros(wk_out.shape, BF16)
    wq_out[0:192, :] = wq_ref[...]
    wk_out[0:192, :] = wk_ref[...]
    wk_out[640:832, :] = wv_ref[...]
    for a in range(3):
        wq_out[256 + 128 * a : 304 + 128 * a, :] = wqp_ref[48 * a : 48 * a + 48, :]
        wk_out[256 + 128 * a : 304 + 128 * a, :] = wkp_ref[48 * a : 48 * a + 48, :]
        wk_out[896 + 128 * a : 992 + 128 * a, :] = wvp_ref[96 * a : 96 * a + 96, :]
    lane = iota((8, 128), 1)
    raw = jnp.zeros((8, 128), F32)
    for h in range(H):
        raw = jnp.where((lane >> 2) == h, hw_ref[h], raw)
    soft = jnp.maximum(raw, 0.0) + jnp.log(1.0 + jnp.exp(-jnp.abs(raw)))
    sc_ref[...] = soft * POINT_SCALE
    fr = pack_ref[:, FRAME_LANE : FRAME_LANE + 128]
    for out, first, fcol in ((q1_ref, 0, 0), (q0_ref, C, 12)):
        flat = mm2(pack_ref[:, first : first + C], wq_out[...], NT)
        rot, shift = columns(fr, fcol)
        out[:, :LANES] = place(rot, shift, flat)
        out[:, LANES:] = flat[:, 256:]


def project_keys(x, fr, fcol, wk_ref, kv_ref):
    flat = mm2(x, wk_ref[...], NT)
    rot, shift = columns(fr, fcol)
    kv_ref[:, 0:640] = place(rot, shift, flat[:, :640])
    kv_ref[:, 640:1280] = place(rot, shift, flat[:, 640:])
    kv_ref[:, 1280:1664] = flat[:, 256:640]
    kv_ref[:, 1664:2048] = flat[:, 896:1280]


def value_sums(probs, kv_ref, rows):
    values = kv_ref[:, 640:1280]
    lane = iota(values.shape, 1)
    values = jnp.where((lane >= 256 + STAT) & (lane < 256 + STAT + H), 1.0, values)
    hi, lo = split(values)
    return pick(mm(probs, hi) + mm(probs, lo), value_heads(rows), rows)


def head_dots(prod, rows):
    return mm2(prod, lane_matrix(256, lambda r: STAT + (r >> 4)))


def first_body(
    flag_ref, own_ref, ownx_ref, p1_ref, p1x_ref, p2_ref, p2x_ref, wk_ref, links_ref, probs_ref, gp_ref, d_ref,
    keys_ref, kv_ref, pm_ref, e_ref,
):
    rows = own_ref.shape[0]
    home = flag_ref[0] == 1
    zb = flag_ref[1]
    core = flag_ref[2]

    def put(z, k, value):
        keys_ref[pl.ds(pl.multiple_of((2 * z + k) * rows, rows), rows), :] = value

    put(zb, core, jnp.where(home, own_ref[...], p1_ref[...]))
    put(zb, 1 - core, jnp.where(home, ownx_ref[...], p1x_ref[...]))
    put(1 - zb, core, jnp.where(home, p1_ref[...], p2_ref[...]))
    put(1 - zb, 1 - core, jnp.where(home, p1x_ref[...], p2x_ref[...]))
    fr = keys_ref[:, FRAME_LANE : FRAME_LANE + 128]
    keys = fr.shape[0]
    at = CHAIN_LANE - FRAME_LANE
    key_chain = fr[:, at : at + 1]
    own_chain = own_ref[:, FRAME_LANE : FRAME_LANE + 128][:, at : at + 1]
    key_hot = (iota((keys, NCHAIN), 1).astype(F32) == key_chain).astype(F32).astype(BF16)
    own_hot = (iota((rows, NCHAIN), 1).astype(F32) == own_chain).astype(F32).astype(BF16)
    eye = iota((NCHAIN, NCHAIN), 0) == iota((NCHAIN, NCHAIN), 1)
    allowed = jnp.where(eye, 1.0, links_ref[...].astype(F32)).astype(BF16)
    mask = mm(mm(own_hot, allowed).astype(BF16), key_hot, NT)
    mask_all = jnp.concatenate([mask] * H, axis=0)
    for l in range(2):
        pm_ref[l] = (probs_ref[l].astype(F32) * mask_all).astype(BF16)
    project_keys(keys_ref[:, 0:C], fr, 0, wk_ref, kv_ref)
    probs = pm_ref[1]
    sums = value_sums(probs, kv_ref, rows)
    weighted = mm2(probs.astype(F32) * d_ref[...], jnp.ones((keys, 128), BF16))
    lane = iota((rows, 128), 1)
    dots = pick(weighted, lane - STAT, rows) + head_dots(gp_ref[:, 0:256] * sums[:, 0:256], rows)
    e_ref[:, 0:128] = block(sums, 0)
    e_ref[:, 128:256] = jnp.where(lane < STAT, block(sums, 1), dots)
    e_ref[:, 256:384] = block(sums, 2)


def second_body(keys_ref, wk_ref, pm_ref, pair_ref, kv_ref, e_ref, tail_ref, p32_ref, op_ref):
    rows = pair_ref.shape[0]
    fr = keys_ref[:, FRAME_LANE : FRAME_LANE + 128]
    project_keys(keys_ref[:, C : 2 * C], fr, 12, wk_ref, kv_ref)
    probs = pm_ref[0]
    sums = value_sums(probs, kv_ref, rows)
    for a in range(3):
        e_ref[:, 128 * a : 128 * a + 128] = block(sums, a)
    e_ref[:, 384:640] = sums[:, 0:256]
    p32_ref[...] = probs.astype(F32)
    for i in range(rows):
        lhs = p32_ref[pl.ds(i, H, stride=rows), :].astype(BF16)
        op_ref[pl.ds(i, H, stride=rows), :] = mm(lhs, pair_ref[i])
    for h in range(H):
        ref, first = (e_ref, 640 + CZ * h) if h < EARLY else (tail_ref, CZ * (h - EARLY))
        ref[:, first : first + CZ] = op_ref[h * rows : (h + 1) * rows, :]


def backward(
    flag_ref, e, dots, probs, kv_ref, key_fr, own_fr, fcol, q_ref, gp, d_ref, wk_ref, sc,
    z_ref, keys_out_ref,
):
    rows = e.shape[0]
    lane = iota((rows, 128), 1)
    stat = (lane >= STAT) & (lane < STAT + H)
    inv = jnp.where(stat, 1.0 / jnp.where(stat, e[:, 0:128], 1.0), 0.0)
    r128 = iota((128, LANES), 0)
    grow = (r128 - STAT == value_heads(128)) & ((iota((128, LANES), 1) & 127) < STAT)
    grow = grow | ((r128 - STAT == (iota((128, LANES), 1) >> 4)) & (iota((128, LANES), 1) < 256))
    inv_lanes = mm2(inv, grow.astype(F32).astype(BF16))
    rot, shift = columns(own_fr, fcol)
    inv_pts = block(inv_lanes, 0)
    ptg = [e[:, 128 * a : 128 * a + 128] * inv_pts for a in range(3)]
    off = [jnp.where(lane < STAT, ptg[a] - shift[a], 0.0) for a in range(3)]
    opt = unrotate(rot, off)
    length = jnp.sqrt(opt[0] * opt[0] + opt[1] * opt[1] + opt[2] * opt[2] + NORM_EPS)
    scale = gp[:, 640:768] / length
    gpt = [block(gp, a) + scale * opt[a] for a in range(3)]
    gptg = rotate(rot, gpt)
    upper = jnp.concatenate([gp[:, 0:256]] + gptg, axis=1)
    point_dots = gptg[0] * ptg[0] + gptg[1] * ptg[1] + gptg[2] * ptg[2]
    rd = dots * inv + mm2(point_dots, lane_matrix(128, lambda r: STAT + (r >> 3)))
    both = jnp.concatenate([spread(rd, lane - STAT), spread(inv, lane - STAT)], axis=0)
    wide = mm2(both, jnp.ones((128, 128), BF16))
    rd_all, inv_all = wide[: H * rows], wide[H * rows :]
    heads_v = value_heads(rows)
    heads_k = key_heads(rows)
    uh, ul = spread2(upper, heads_v)
    vh, vl = split(kv_ref[:, 640:1280])
    d_att = d_ref[...] + mm3(uh, ul, vh, vl, NT)
    p32 = probs.astype(F32)
    att = p32 * inv_all
    dl = LOGIT_SCALE * att * (d_att - rd_all)
    z_ref[0 : H * rows, :] = att
    z_ref[H * rows :, :] = dl
    dt = jnp.transpose(dl)
    th, tl = split(dt)
    qh, qlo = spread2(q_ref[:, 0:640], heads_k)
    kr = mm3(th, tl, qh, qlo)
    head_rows = iota((H * rows, 128), 0) // rows
    hot = ((iota((H * rows, 128), 1) >> 2) == head_rows).astype(F32).astype(BF16)
    cs = mm(th, hot) + mm(tl, hot)
    pt = jnp.transpose(p32).astype(BF16)
    sh, sl = spread2(upper * inv_lanes, heads_v)
    vr = mm(pt, sh) + mm(pt, sl)
    krot, _ = columns(key_fr, fcol)
    d_kg = [sc * (block(kr, a) - cs * kv_ref[:, 256 + 128 * a : 384 + 128 * a]) for a in range(3)]
    d_vg = [block(vr, a) for a in range(3)]
    d_kl = unrotate(krot, d_kg)
    d_vl = unrotate(krot, d_vg)
    flat = jnp.concatenate([PLAIN_SCALE * kr[:, 0:256]] + d_kl + [vr[:, 0:256]] + d_vl, axis=1)
    keys_out_ref[:, 0:C] = mm2(flat, wk_ref[...])
    return jnp.concatenate(off + gpt + gptg, axis=1), jnp.concatenate(d_kg + d_vg, axis=1)


def frame_sums(prods, first):
    def lane(r):
        q = first + (r >> 7)
        return q + 2 * ((q * 43) >> 8)

    return mm2(jnp.concatenate(prods, axis=1), lane_matrix(12 * 128, lane))


def frame_block(turned, at, rows):
    return jnp.concatenate([turned[8 * m : 8 * m + 8, at : at + rows] for m in range(4)], axis=1)


def store_piece(ref, at, grad, frames):
    rows = grad.shape[0]
    for t in range(3):
        ref[at + rows * t : at + rows * (t + 1), :] = grad[:, 128 * t : 128 * t + 128]
    ref[at + 3 * rows : at + 3 * rows + 8, :] = frames


def backward_frames(grads, kv_ref, first):
    d_kg = [grads[:, 128 * a : 128 * a + 128] for a in range(3)]
    d_vg = [grads[:, 384 + 128 * a : 512 + 128 * a] for a in range(3)]
    k_local = [kv_ref[:, 1280 + 128 * b : 1408 + 128 * b] for b in range(3)]
    v_local = [kv_ref[:, 1664 + 128 * b : 1792 + 128 * b] for b in range(3)]
    prods = [d_kg[a] * k_local[b] + d_vg[a] * v_local[b] for a in range(3) for b in range(3)]
    return frame_sums(prods + [d_kg[a] + d_vg[a] for a in range(3)], first)


def backward_query(dl, kv_ref, own_fr, fcol, q_ref, pts_ref, wq_ref, sc, first_lane, share):
    rows = own_fr.shape[0]
    dh, dlo = split(dl)
    kh, klo = split(kv_ref[:, 0:640])
    qr = pick(mm3(dh, dlo, kh, klo), key_heads(rows), rows)
    rot, _ = columns(own_fr, fcol)
    d_qg = [sc * block(qr, a) for a in range(3)]
    d_ql = unrotate(rot, d_qg)
    grad = mm2(jnp.concatenate([PLAIN_SCALE * qr[:, 0:256]] + d_ql, axis=1), wq_ref[...])
    q_local = [q_ref[:, 640 + 128 * b : 768 + 128 * b] for b in range(3)]
    off, gpt, gptg = [
        [pts_ref[:, 384 * n + 128 * a : 384 * n + 128 * a + 128] for a in range(3)] for n in range(3)
    ]
    prods = [d_qg[a] * q_local[b] + share * off[a] * gpt[b] for a in range(3) for b in range(3)]
    prods = prods + [d_qg[a] - share * gptg[a] for a in range(3)]
    return grad, frame_sums(prods, first_lane)


def send_blocks(flag_ref, src_ref, mine_a, mine_b, theirs, rows):
    zb = flag_ref[1]
    core = flag_ref[2]

    def get(z, k):
        return src_ref[pl.ds(pl.multiple_of((2 * z + k) * rows, 8), rows), :]

    mine_a[...] = get(zb, core)
    mine_b[...] = get(1 - zb, core)
    theirs[0:rows, :] = get(zb, 1 - core)
    theirs[rows:, :] = get(1 - zb, 1 - core)


def add_pieces(flag_ref, query, query_other, part, one, two):
    return (query[...] + query_other[...]) + (one[...] + jnp.where(flag_ref[0] == 1, part[...], two[...]))


def final_body(flag_ref, r0, r1, r2, r3, r4, one_ref, single_out, frames_out):
    total = add_pieces(flag_ref, r0, r1, r2, r3, r4)
    rows = one_ref.shape[0]
    for t in range(3):
        lanes = slice(128 * t, 128 * t + 128)
        single_out[:, lanes] = one_ref[:, lanes] + total[rows * t : rows * (t + 1), :]
    for m in range(4):
        first = 6 * (m % 2)
        frames_out[first : first + 6, m // 2, :] = total[3 * rows : 3 * rows + 6, rows * m : rows * (m + 1)]


def frame_part(ref):
    return ref[:, FRAME_LANE : FRAME_LANE + 128]


def back_one_body(
    flag_ref, e_mine, e_other, pm_ref, kv_ref, keys_ref, own_ref, q_ref, gp_ref, d_ref, wk_ref, sc_ref,
    z_ref, mine_a, mine_b, theirs, pts_ref, grads_ref, work_ref,
):
    e = e_mine[...] + e_other[...]
    pts_ref[...], grads_ref[...] = backward(
        flag_ref, e, e[:, 128:256], pm_ref[1], kv_ref, frame_part(keys_ref), frame_part(own_ref), 0, q_ref,
        gp_ref[...], d_ref, wk_ref, sc_ref[0:1, :], z_ref, work_ref,
    )
    send_blocks(flag_ref, work_ref, mine_a, mine_b, theirs, own_ref.shape[0])


def query_one_body(
    share, z_ref, kv_ref, own_ref, q_ref, pts_ref, grads_ref, wq_ref, sc_ref, query_out, frq_ref, frk_ref
):
    half = z_ref.shape[0] // 2
    query_out[...], frq_ref[...] = backward_query(
        z_ref[half:, :], kv_ref, frame_part(own_ref), 0, q_ref, pts_ref, wq_ref, sc_ref[0:1, :], 12, share
    )
    frk_ref[...] = backward_frames(grads_ref[...], kv_ref, 12)


def back_zero_body(
    flag_ref, cot_ref, r0, r1, r2, r3, r4, e_mine, e_other, tail_mine, tail_other, pm_ref, kv_ref, keys_ref, own_ref, q_ref, pair_ref,
    w_out_ref, wk_ref, sc_ref, frk_ref,
    z_ref, mine_a, mine_b, theirs, pts_ref, sum_ref, pu_ref, work_ref, pieces_ref, gp_ref, d_ref,
):
    rows = own_ref.shape[0]
    total = add_pieces(flag_ref, r0, r1, r2, r3, r4)
    sum_ref[...] = total
    upstream_parts(cot_ref[...] + total, w_out_ref, gp_ref, pu_ref, rows)
    pair_products(pu_ref, pair_ref, d_ref, rows)
    gp = gp_ref[...]
    e = e_mine[:, 0:384] + e_other[:, 0:384]
    plain = e_mine[:, 384:640] + e_other[:, 384:640]
    dots = head_dots(gp[:, 0:256] * plain, rows)
    wide = jnp.concatenate(
        [
            pu_ref[h * rows : (h + 1) * rows, :]
            * (
                e_mine[:, 640 + CZ * h : 640 + CZ * (h + 1)] + e_other[:, 640 + CZ * h : 640 + CZ * (h + 1)]
                if h < EARLY
                else tail_mine[:, CZ * (h - EARLY) : CZ * (h - EARLY + 1)]
                + tail_other[:, CZ * (h - EARLY) : CZ * (h - EARLY + 1)]
            )
            for h in range(H)
        ],
        axis=1,
    )
    dots = dots + mm2(wide, lane_matrix(H * CZ, lambda r: STAT + (r >> 7)))
    pts_ref[...], grads = backward(
        flag_ref, e, dots, pm_ref[0], kv_ref, frame_part(keys_ref), frame_part(own_ref), 12, q_ref, gp, d_ref, wk_ref,
        sc_ref[0:1, :], z_ref, work_ref,
    )
    turned = jnp.transpose(backward_frames(grads, kv_ref, 0) + frk_ref[...])
    for n in range(4):
        at = n * pieces_ref.shape[0] // 4
        store_piece(pieces_ref, at, work_ref[rows * n : rows * (n + 1), :], frame_block(turned, rows * n, rows))
    send_blocks(flag_ref, pieces_ref, mine_a, mine_b, theirs, mine_a.shape[0])


def query_zero_body(share, z_ref, kv_ref, own_ref, q_ref, pts_ref, wq_ref, sc_ref, frq_ref, query_out):
    half = z_ref.shape[0] // 2
    grad, frames = backward_query(
        z_ref[half:, :], kv_ref, frame_part(own_ref), 12, q_ref, pts_ref, wq_ref, sc_ref[0:1, :], 0, share
    )
    store_piece(query_out, 0, grad, frame_block(jnp.transpose(frames + frq_ref[...]), 0, own_ref.shape[0]))


def pair_body(z1_ref, z0_ref, pu1_ref, pu0_ref, wbt_ref, out_ref):
    rows = out_ref.shape[0]
    wbt = wbt_ref[...].astype(F32)
    for i in range(rows):
        left = jnp.concatenate(
            [z1_ref[pl.ds(i, 2 * H, stride=rows), :], z0_ref[pl.ds(i, 2 * H, stride=rows), :]], axis=0
        )
        right = jnp.concatenate(
            [pu1_ref[pl.ds(i, H, stride=rows), :], wbt, pu0_ref[pl.ds(i, H, stride=rows), :], wbt], axis=0
        ).astype(BF16)
        out_ref[i] = mm(left.astype(BF16), right, TN).astype(BF16)


VMEM = pl.BlockSpec(memory_space=pltpu.VMEM)
SMEM = pl.BlockSpec(memory_space=pltpu.SMEM)
HBM = pl.BlockSpec(memory_space=pltpu.HBM)


def call(body, name, in_specs, outs, args, scratch=(), micros=1.0):
    return pl.pallas_call(
        body,
        name=name,
        in_specs=in_specs,
        out_specs=tuple(VMEM for _ in outs),
        out_shape=tuple(jax.ShapeDtypeStruct(s, d) for s, d in outs),
        scratch_shapes=list(scratch),
        compiler_params=pltpu.CompilerParams(vmem_limit_bytes=16 * 1024 * 1024),
        cost_estimate=pl.CostEstimate(flops=int(micros * 1e9), transcendentals=0, bytes_accessed=int(micros * 3e6)),
    )(*args)


def in_hbm(*arrays):
    return tuple(pltpu.with_memory_space_constraint(x, pltpu.HBM) for x in arrays)


def joint(pairs):
    return [
        ((a * 2 + k) * 2 + x, (b * 2 + k) * 2 + y) for (x, a), (y, b) in pairs for k in range(2)
    ]


BOTH = ("row", "col")
FETCH_ONE = joint([((0, 0), (0, 1)), ((0, 1), (0, 0)), ((1, 0), (0, 2)), ((1, 1), (0, 3)), ((1, 2), (1, 3)), ((1, 3), (1, 2)), ((0, 2), (1, 0)), ((0, 3), (1, 1))])
FETCH_TWO = joint([((0, 0), (0, 3)), ((0, 1), (0, 2)), ((1, 2), (1, 1)), ((1, 3), (1, 0)), ((1, 0), (0, 0)), ((1, 1), (0, 1)), ((0, 2), (1, 2)), ((0, 3), (1, 3))])
SEND_ONE = joint([((0, 0), (1, 0)), ((0, 1), (1, 1)), ((0, 2), (0, 0)), ((0, 3), (0, 1)), ((1, 2), (0, 2)), ((1, 3), (0, 3)), ((1, 0), (1, 2)), ((1, 1), (1, 3))])
SEND_TWO = joint([((0, 2), (1, 0)), ((0, 3), (1, 1)), ((1, 0), (0, 2)), ((1, 1), (0, 3)), ((0, 0), (0, 1)), ((0, 1), (0, 0)), ((1, 2), (1, 3)), ((1, 3), (1, 2))])
CORE_SWAP = [(i, i ^ 1) for i in range(8)]
Z_SWAP = [(i, i ^ 2) for i in range(8)]
COL_SWAP = [(0, 1), (1, 0)]


def local(
    single, frames, saved_probs, pair, cotangent, chains, links, w_query, w_key, w_value, w_query_points,
    w_key_points, w_value_points, w_bias, w_out, head_weights,
):
    rows = single.shape[1]
    keys = pair.shape[1]
    row_total = lax.axis_size("row")
    col_total = lax.axis_size("col")
    fast = row_total == 8 and col_total == 2 and keys == 4 * rows
    (pack,) = call(
        pack_body, "pack", [HBM] * 3, [((rows, PACK), F32)], in_hbm(single, frames.transpose(1, 0, 2), chains[None]),
        [pltpu.VMEM((12, 2, rows), F32), pltpu.VMEM((1, rows), jnp.int32), pltpu.SemaphoreType.DMA((4,))],
    )
    col = lax.axis_index("col")
    row = lax.axis_index("row")
    if fast:
        home = (row // 4 == col).astype(jnp.int32)
        flags = jnp.stack([home, (row // 2) % 2, row % 2])
        ownx = lax.ppermute(pack, "row", CORE_SWAP)
        one = lax.ppermute(pack, BOTH, FETCH_ONE)
        two = lax.ppermute(pack, BOTH, FETCH_TWO)
        own = pack
    else:
        flags = jnp.array([1, 0, 0], jnp.int32)
        whole = lax.all_gather(pack, "row", axis=0, tiled=True)
        mine = lax.dynamic_slice_in_dim(whole, col * keys, keys, 0)
        quarter = keys // 4
        blocks = tuple(mine[quarter * n : quarter * (n + 1)] for n in (0, 1, 2, 3, 0, 0))
        own = pack

    def col_other(x):
        if col_total == 2:
            return lax.ppermute(x, "col", COL_SWAP)
        return lax.psum(x, "col") - x

    def reduce(mine_a, mine_b, theirs, late, first_beside, beside):
        if fast:
            got = lax.ppermute(theirs, "row", CORE_SWAP)
            query, *rest = late()
            got, query, first_beside = lax.optimization_barrier((got, query, first_beside))
            query_other = lax.ppermute(query, "col", COL_SWAP)
            count = mine_a.shape[0]
            half = lax.ppermute(mine_b + got[count:], "row", Z_SWAP)
            half, beside = lax.optimization_barrier((half, beside))
            part = mine_a + got[:count] + half
            sent = [lax.ppermute(part, BOTH, SEND_ONE), lax.ppermute(part, BOTH, SEND_TWO)]
            return [query, query_other, part] + sent, rest, (first_beside, beside)
        query, *rest = late()
        count = mine_a.shape[0]
        parts = jnp.concatenate([mine_a, theirs[:count], mine_b, theirs[count:]], axis=0)
        summed = lax.all_gather(lax.psum(parts, "row"), "col", axis=0, tiled=True)
        back = lax.dynamic_slice_in_dim(summed, row * count, count, 0)
        zero = jnp.zeros_like(query)
        return [lax.psum(query, "col"), zero, back, zero, zero], rest, (first_beside, beside)

    probs = saved_probs.reshape(2, H * rows, keys)
    hr = H * rows
    loads = (
        cotangent, w_out, pair, w_query.T, w_key.T, w_value.T, w_query_points.T, w_key_points.T, w_value_points.T,
    )
    wk, wq, gp1, q1, q0, pu1, d1, sc = call(
        prep_body, "prep", [SMEM, VMEM] + [HBM] * 9,
        [((1280, C), BF16), ((LANES, C), BF16), ((rows, 768), F32), ((rows, 1024), F32), ((rows, 1024), F32),
         ((hr, CZ), F32), ((hr, keys), F32), ((8, 128), F32)],
        (head_weights, own, *in_hbm(*loads)),
        [pltpu.VMEM(x.shape, x.dtype) for x in loads] + [pltpu.SemaphoreType.DMA((len(loads),))],
    )
    if fast:
        one, two, wk, wq, gp1, q1, q0, pu1, d1, sc = lax.optimization_barrier(
            (one, two, wk, wq, gp1, q1, q0, pu1, d1, sc)
        )
        blocks = (pack, ownx, one, lax.ppermute(one, "row", CORE_SWAP), two, lax.ppermute(two, "row", CORE_SWAP))
    key_pack, kv1, pm, e1 = call(
        first_body, "first", [SMEM] + [VMEM] * 11,
        [((keys, PACK), F32), ((keys, 2048), F32), ((2, hr, keys), BF16), ((rows, 384), F32)],
        (flags, *blocks, wk, links, probs, gp1, d1),
    )
    e1_other = col_other(e1)
    kv0, e0, tail = call(
        second_body, "second", [VMEM] * 4,
        [((keys, 2048), F32), ((rows, 640 + EARLY * CZ), F32), ((rows, (H - EARLY) * CZ), F32)],
        (key_pack, wk, pm, pair),
        [pltpu.VMEM((hr, keys), F32), pltpu.VMEM((hr, CZ), F32)],
    )
    e0_other = col_other(e0)
    tail_other = col_other(tail)
    share = 1.0 / col_total
    e1_other, e0 = lax.optimization_barrier((e1_other, e0))
    z1, mine_a, mine_b, theirs, pts, grads = call(
        back_one_body, "back_one", [SMEM] + [VMEM] * 11,
        [((2 * hr, keys), F32), ((rows, C), F32), ((rows, C), F32), ((2 * rows, C), F32), ((rows, 1152), F32),
         ((keys, 768), F32)],
        (flags, e1, e1_other, pm, kv1, key_pack, own, q1, gp1, d1, wk, sc),
        [pltpu.VMEM((keys, C), F32)],
        6.0,
    )
    pieces, (frq, frk), (e0_other, tail_other) = reduce(
        mine_a, mine_b, theirs,
        lambda: call(
            functools.partial(query_one_body, share), "query_one", [VMEM] * 8,
            [((rows, C), F32), ((rows, 128), F32), ((keys, 128), F32)],
            (z1, kv1, own, q1, pts, grads, wq, sc),
            (),
            0.01,
        ),
        e0_other,
        tail_other,
    )
    long = 3 * rows + 8
    z0, mine_a, mine_b, theirs, pts, single_one, pu0 = call(
        back_zero_body, "back_zero", [SMEM] + [VMEM] * 20,
        [((2 * hr, keys), F32), ((long, 128), F32), ((long, 128), F32), ((2 * long, 128), F32), ((rows, 1152), F32),
         ((rows, C), F32), ((hr, CZ), F32)],
        (flags, cotangent, *pieces, e0, e0_other, tail, tail_other, pm, kv0, key_pack, own, q0, pair, w_out, wk, sc, frk),
        [pltpu.VMEM((keys, C), F32), pltpu.VMEM((4 * long, 128), F32), pltpu.VMEM((rows, 768), F32), pltpu.VMEM((hr, keys), F32)],
    )
    (d_pair,) = call(
        pair_body, "pair_grad", [VMEM] * 5, [((rows, keys, CZ), BF16)], (z1, z0, pu1, pu0, w_bias.T)
    )
    pieces, _, (_, d_pair) = reduce(
        mine_a, mine_b, theirs,
        lambda: call(
            functools.partial(query_zero_body, share), "query_zero", [VMEM] * 8, [((long, 128), F32)],
            (z0, kv0, own, q0, pts, wq, sc, frq),
        ),
        (),
        d_pair,
    )
    d_single, d_frames = call(
        final_body, "final", [SMEM] + [VMEM] * 6, [((rows, C), F32), ((12, 2, rows), F32)],
        (flags, *pieces, single_one),
    )
    return (d_single, d_frames.transpose(1, 0, 2), d_pair)


def solution(mesh):
    return jax.shard_map(
        local,
        mesh=mesh,
        in_specs=(
            P(None, ("grp", "row"), None),
            P(None, None, ("grp", "row")),
            P(None, None, ("grp", "row"), "col"),
            P(("grp", "row"), "col", None),
            P(("grp", "row"), None),
            P(("grp", "row")),
            P("grp", None),
            P(),
            P(),
            P(),
            P(),
            P(),
            P(),
            P(),
            P(),
            P(),
        ),
        out_specs=(
            P(("grp", "row"), None),
            P(None, None, ("grp", "row")),
            P(("grp", "row"), "col", None),
        ),
        check_vma=False,
    )
```

```python
import functools
import math

import jax
import jax.numpy as jnp
from jax import lax
from jax.experimental import pallas as pl
from jax.experimental.pallas import tpu as pltpu
from jax.sharding import PartitionSpec as P

C = 384
H = 12
HD = 16
CZ = 128
PQ = 4
PV = 8
NCHAIN = 16
NORM_EPS = 1e-08
LOGIT_SCALE = math.sqrt(1.0 / 3.0)
PLAIN_SCALE = 1.0 / math.sqrt(HD)
POINT_SCALE = math.sqrt(2.0 / (9.0 * PQ))

LANES = 640
PACK = 896
FRAME_LANE = 768
CHAIN_LANE = 792
STAT = 96
EARLY = 4

F32 = jnp.float32
BF16 = jnp.bfloat16
NN = (((1,), (0,)), ((), ()))
NT = (((1,), (1,)), ((), ()))
TN = (((0,), (0,)), ((), ()))


def mm(a, b, dims=NN):
    return lax.dot_general(a, b, dims, preferred_element_type=F32)


def split(x):
    hi = x.astype(BF16)
    return hi, (x - hi.astype(F32)).astype(BF16)


def mm2(x, w, dims=NN):
    hi, lo = split(x)
    rows = x.shape[0]
    both = mm(jnp.concatenate([hi, lo], axis=0), w, dims)
    return both[:rows] + both[rows:]


def mm3(ah, al, bh, bl, dims=NN):
    return mm(ah, bh, dims) + mm(ah, bl, dims) + mm(al, bh, dims)


def iota(shape, axis):
    return lax.broadcasted_iota(jnp.int32, shape, axis)


def key_heads(rows):
    lane = iota((rows, LANES), 1)
    return jnp.where(lane < 256, lane >> 4, (lane & 127) >> 2)


def value_heads(rows):
    lane = iota((rows, LANES), 1)
    inner = lane & 127
    points = jnp.where(inner < STAT, inner >> 3, inner - STAT)
    return jnp.where(lane < 256, lane >> 4, points)


def pick(full, heads, rows):
    out = None
    for h in range(H):
        part = jnp.where(heads == h, full[h * rows : (h + 1) * rows], 0.0)
        out = part if out is None else out + part
    return out


def spread(x, heads):
    return jnp.concatenate([jnp.where(heads == h, x, 0.0) for h in range(H)], axis=0)


def spread2(x, heads):
    hi, lo = split(x)
    hi32, lo32 = hi.astype(F32), lo.astype(F32)
    return spread(hi32, heads).astype(BF16), spread(lo32, heads).astype(BF16)


def columns(frames_block, first):
    cols = [frames_block[:, first + n : first + n + 1] for n in range(12)]
    return [[cols[3 * a + b] for b in range(3)] for a in range(3)], cols[9:]


def block(x, a):
    return x[:, 256 + 128 * a : 384 + 128 * a]


def rotate(rot, pts):
    return [sum(rot[a][b] * pts[b] for b in range(3)) for a in range(3)]


def unrotate(rot, pts):
    return [sum(rot[a][b] * pts[a] for a in range(3)) for b in range(3)]


def place(rot, shift, flat):
    local_pts = [block(flat, a) for a in range(3)]
    turned = rotate(rot, local_pts)
    return jnp.concatenate(
        [flat[:, :256]] + [turned[a] + shift[a] for a in range(3)], axis=1
    )


def lane_matrix(rows, fn):
    r = iota((rows, 128), 0)
    c = iota((rows, 128), 1)
    return (fn(r) == c).astype(F32).astype(BF16)


def upstream_parts(g, w_out_ref, gp_ref, pu_ref, rows):
    hi, lo = split(g)
    both = jnp.concatenate([hi, lo], axis=0)

    def part(first, count):
        r = mm(both, w_out_ref[first : first + count, :], NT)
        return r[:rows] + r[rows:]

    gp_ref[...] = jnp.zeros(gp_ref.shape, F32)
    gp_ref[:, 0:192] = part(0, 192)
    for a in range(4):
        gp_ref[:, 256 + 128 * a : 352 + 128 * a] = part(192 + 96 * a, 96)
    wide = part(576, H * CZ)
    for h in range(H):
        pu_ref[h * rows : (h + 1) * rows, :] = (
            wide[:, h * CZ : (h + 1) * CZ].astype(BF16).astype(F32)
        )


def pair_products(pu_ref, pair_ref, d_ref, rows):
    for i in range(0, rows, 2):
        lhs = jnp.concatenate([pu_ref[pl.ds(i, H, stride=rows), :], pu_ref[pl.ds(i + 1, H, stride=rows), :]], axis=0)
        both = mm(lhs.astype(BF16), pair_ref[i : i + 2].reshape(-1, CZ), NT)
        keys = both.shape[1] // 2
        d_ref[pl.ds(i, H, stride=rows), :] = both[:H, :keys]
        d_ref[pl.ds(i + 1, H, stride=rows), :] = both[H:, keys:]


def split3(x):
    hi, _ = split(x)
    rest = x - hi.astype(F32)
    mid, lo = split(rest)
    return hi, mid, lo


def pack_body(single_hbm, frames_hbm, chains_hbm, pack_ref, frames_ref, chains_ref, sems):
    rows = pack_ref.shape[0]
    ends = (
        (frames_hbm, frames_ref), (chains_hbm, chains_ref), (single_hbm.at[1], pack_ref.at[:, 0:C]),
        (single_hbm.at[0], pack_ref.at[:, C : 2 * C]),
    )
    copies = [pltpu.make_async_copy(src, dst, sems.at[n]) for n, (src, dst) in enumerate(ends)]
    for copy in copies:
        copy.start()
    copies[0].wait()
    copies[1].wait()
    out = jnp.zeros((rows, 128), F32)
    for slot, l in ((0, 1), (12, 0)):
        hot = (iota((12, 128), 1) == iota((12, 128), 0) + slot).astype(F32).astype(BF16)
        for part in split3(frames_ref[:, l, :]):
            out = out + mm(part, hot, TN)
    hot = (iota((1, 128), 1) == CHAIN_LANE - FRAME_LANE).astype(F32).astype(BF16)
    pack_ref[:, 2 * C :] = out + mm(chains_ref[...].astype(F32).astype(BF16), hot, TN)
    copies[2].wait()
    copies[3].wait()


def prep_body(
    pack_ref, cot_hbm, w_out_hbm, pair_hbm, wq_hbm, wk_hbm, wv_hbm, wqp_hbm, wkp_hbm, wvp_hbm, hw_hbm,
    wk_out, wq_out, gp_ref, q1_ref, q0_ref, pu_ref, d_ref, sc_ref,
    cot_ref, w_out_ref, pair_ref, wq_ref, wk_ref, wv_ref, wqp_ref, wkp_ref, wvp_ref, hw_ref, sems,
):
    rows = pack_ref.shape[0]
    ends = (
        (cot_hbm, cot_ref), (w_out_hbm, w_out_ref), (pair_hbm, pair_ref), (wq_hbm, wq_ref), (wk_hbm, wk_ref),
        (wv_hbm, wv_ref), (wqp_hbm, wqp_ref), (wkp_hbm, wkp_ref), (wvp_hbm, wvp_ref), (hw_hbm, hw_ref),
    )
    copies = [pltpu.make_async_copy(src, dst, sems.at[n]) for n, (src, dst) in enumerate(ends)]
    for copy in copies:
        copy.start()
    copies[0].wait()
    copies[1].wait()
    upstream_parts(cot_ref[...], w_out_ref, gp_ref, pu_ref, rows)
    copies[2].wait()
    pair_products(pu_ref, pair_ref, d_ref, rows)
    for copy in copies[3:]:
        copy.wait()
    wq_out[...] = jnp.zeros(wq_out.shape, BF16)
    wk_out[...] = jnp.zeros(wk_out.shape, BF16)
    wq_out[0:192, :] = wq_ref[...]
    wk_out[0:192, :] = wk_ref[...]
    wk_out[640:832, :] = wv_ref[...]
    for a in range(3):
        wq_out[256 + 128 * a : 304 + 128 * a, :] = wqp_ref[48 * a : 48 * a + 48, :]
        wk_out[256 + 128 * a : 304 + 128 * a, :] = wkp_ref[48 * a : 48 * a + 48, :]
        wk_out[896 + 128 * a : 992 + 128 * a, :] = wvp_ref[96 * a : 96 * a + 96, :]
    lane = iota((8, 128), 1)
    raw = jnp.zeros((8, 128), F32)
    for h in range(H):
        raw = jnp.where((lane >> 2) == h, hw_ref[:, h : h + 1], raw)
    soft = jnp.maximum(raw, 0.0) + jnp.log(1.0 + jnp.exp(-jnp.abs(raw)))
    sc_ref[...] = soft * POINT_SCALE
    fr = pack_ref[:, FRAME_LANE : FRAME_LANE + 128]
    for out, first, fcol in ((q1_ref, 0, 0), (q0_ref, C, 12)):
        flat = mm2(pack_ref[:, first : first + C], wq_out[...], NT)
        rot, shift = columns(fr, fcol)
        out[:, :LANES] = place(rot, shift, flat)
        out[:, LANES:] = flat[:, 256:]


def project_keys(x, fr, fcol, wk_ref, kv_ref):
    flat = mm2(x, wk_ref[...], NT)
    rot, shift = columns(fr, fcol)
    kv_ref[:, 0:640] = place(rot, shift, flat[:, :640])
    kv_ref[:, 640:1280] = place(rot, shift, flat[:, 640:])
    kv_ref[:, 1280:1664] = flat[:, 256:640]
    kv_ref[:, 1664:2048] = flat[:, 896:1280]


def value_sums(probs, kv_ref, rows):
    values = kv_ref[:, 640:1280]
    lane = iota(values.shape, 1)
    values = jnp.where((lane >= 256 + STAT) & (lane < 256 + STAT + H), 1.0, values)
    hi, lo = split(values)
    return pick(mm(probs, hi) + mm(probs, lo), value_heads(rows), rows)


def head_dots(prod, rows):
    return mm2(prod, lane_matrix(256, lambda r: STAT + (r >> 4)))


def first_body(
    fast, own_ref, ownx_ref, p1_ref, p1x_ref, p2_ref, p2x_ref, wk_ref, links_ref, probs_ref, gp_ref, d_ref,
    keys_ref, kv_ref, pm_ref, e_ref,
):
    rows = own_ref.shape[0]
    home, zb, core = position(fast)

    def put(z, k, value):
        keys_ref[pl.ds(pl.multiple_of(jnp.int32((2 * z + k) * rows), rows), rows), :] = value

    put(zb, core, jnp.where(home, own_ref[...], p1_ref[...]))
    put(zb, 1 - core, jnp.where(home, ownx_ref[...], p1x_ref[...]))
    put(1 - zb, core, jnp.where(home, p1_ref[...], p2_ref[...]))
    put(1 - zb, 1 - core, jnp.where(home, p1x_ref[...], p2x_ref[...]))
    fr = keys_ref[:, FRAME_LANE : FRAME_LANE + 128]
    keys = fr.shape[0]
    at = CHAIN_LANE - FRAME_LANE
    key_chain = fr[:, at : at + 1]
    own_chain = own_ref[:, FRAME_LANE : FRAME_LANE + 128][:, at : at + 1]
    key_hot = (iota((keys, NCHAIN), 1).astype(F32) == key_chain).astype(F32).astype(BF16)
    own_hot = (iota((rows, NCHAIN), 1).astype(F32) == own_chain).astype(F32).astype(BF16)
    eye = iota((NCHAIN, NCHAIN), 0) == iota((NCHAIN, NCHAIN), 1)
    allowed = jnp.where(eye, 1.0, links_ref[...].astype(F32)).astype(BF16)
    mask = mm(mm(own_hot, allowed).astype(BF16), key_hot, NT)
    mask_all = jnp.concatenate([mask] * H, axis=0)
    for l in range(2):
        pm_ref[l] = (probs_ref[l].astype(F32) * mask_all).astype(BF16)
    project_keys(keys_ref[:, 0:C], fr, 0, wk_ref, kv_ref)
    probs = pm_ref[1]
    sums = value_sums(probs, kv_ref, rows)
    weighted = mm2(probs.astype(F32) * d_ref[...], jnp.ones((keys, 128), BF16))
    lane = iota((rows, 128), 1)
    dots = pick(weighted, lane - STAT, rows) + head_dots(gp_ref[:, 0:256] * sums[:, 0:256], rows)
    e_ref[:, 0:128] = block(sums, 0)
    e_ref[:, 128:256] = jnp.where(lane < STAT, block(sums, 1), dots)
    e_ref[:, 256:384] = block(sums, 2)


def second_body(keys_ref, wk_ref, pm_ref, pair_ref, kv_ref, e_ref, tail_ref, p32_ref, op_ref):
    rows = pair_ref.shape[0]
    fr = keys_ref[:, FRAME_LANE : FRAME_LANE + 128]
    project_keys(keys_ref[:, C : 2 * C], fr, 12, wk_ref, kv_ref)
    probs = pm_ref[0]
    sums = value_sums(probs, kv_ref, rows)
    for a in range(3):
        e_ref[:, 128 * a : 128 * a + 128] = block(sums, a)
    e_ref[:, 384:640] = sums[:, 0:256]
    p32_ref[...] = probs.astype(F32)
    for i in range(rows):
        lhs = p32_ref[pl.ds(i, H, stride=rows), :].astype(BF16)
        op_ref[pl.ds(i, H, stride=rows), :] = mm(lhs, pair_ref[i])
    for h in range(H):
        ref, first = (e_ref, 640 + CZ * h) if h < EARLY else (tail_ref, CZ * (h - EARLY))
        ref[:, first : first + CZ] = op_ref[h * rows : (h + 1) * rows, :]


def backward(
    e, dots, probs, kv_ref, key_fr, own_fr, fcol, q_ref, gp, d_ref, wk_ref, sc,
    z_ref, keys_out_ref,
):
    rows = e.shape[0]
    lane = iota((rows, 128), 1)
    stat = (lane >= STAT) & (lane < STAT + H)
    inv = jnp.where(stat, 1.0 / jnp.where(stat, e[:, 0:128], 1.0), 0.0)
    r128 = iota((128, LANES), 0)
    grow = (r128 - STAT == value_heads(128)) & ((iota((128, LANES), 1) & 127) < STAT)
    grow = grow | ((r128 - STAT == (iota((128, LANES), 1) >> 4)) & (iota((128, LANES), 1) < 256))
    inv_lanes = mm2(inv, grow.astype(F32).astype(BF16))
    rot, shift = columns(own_fr, fcol)
    inv_pts = block(inv_lanes, 0)
    ptg = [e[:, 128 * a : 128 * a + 128] * inv_pts for a in range(3)]
    off = [jnp.where(lane < STAT, ptg[a] - shift[a], 0.0) for a in range(3)]
    opt = unrotate(rot, off)
    length = jnp.sqrt(opt[0] * opt[0] + opt[1] * opt[1] + opt[2] * opt[2] + NORM_EPS)
    scale = gp[:, 640:768] / length
    gpt = [block(gp, a) + scale * opt[a] for a in range(3)]
    gptg = rotate(rot, gpt)
    upper = jnp.concatenate([gp[:, 0:256]] + gptg, axis=1)
    point_dots = gptg[0] * ptg[0] + gptg[1] * ptg[1] + gptg[2] * ptg[2]
    rd = dots * inv + mm2(point_dots, lane_matrix(128, lambda r: STAT + (r >> 3)))
    both = jnp.concatenate([spread(rd, lane - STAT), spread(inv, lane - STAT)], axis=0)
    wide = mm2(both, jnp.ones((128, 128), BF16))
    rd_all, inv_all = wide[: H * rows], wide[H * rows :]
    heads_v = value_heads(rows)
    heads_k = key_heads(rows)
    uh, ul = spread2(upper, heads_v)
    vh, vl = split(kv_ref[:, 640:1280])
    d_att = d_ref[...] + mm3(uh, ul, vh, vl, NT)
    p32 = probs.astype(F32)
    att = p32 * inv_all
    dl = LOGIT_SCALE * att * (d_att - rd_all)
    z_ref[0 : H * rows, :] = att
    z_ref[H * rows :, :] = dl
    dt = jnp.transpose(dl)
    th, tl = split(dt)
    qh, qlo = spread2(q_ref[:, 0:640], heads_k)
    kr = mm3(th, tl, qh, qlo)
    head_rows = iota((H * rows, 128), 0) // rows
    hot = ((iota((H * rows, 128), 1) >> 2) == head_rows).astype(F32).astype(BF16)
    cs = mm(th, hot) + mm(tl, hot)
    pt = jnp.transpose(p32).astype(BF16)
    sh, sl = spread2(upper * inv_lanes, heads_v)
    vr = mm(pt, sh) + mm(pt, sl)
    krot, _ = columns(key_fr, fcol)
    d_kg = [sc * (block(kr, a) - cs * kv_ref[:, 256 + 128 * a : 384 + 128 * a]) for a in range(3)]
    d_vg = [block(vr, a) for a in range(3)]
    d_kl = unrotate(krot, d_kg)
    d_vl = unrotate(krot, d_vg)
    flat = jnp.concatenate([PLAIN_SCALE * kr[:, 0:256]] + d_kl + [vr[:, 0:256]] + d_vl, axis=1)
    keys_out_ref[:, 0:C] = mm2(flat, wk_ref[...])
    return jnp.concatenate(off + gpt + gptg, axis=1), jnp.concatenate(d_kg + d_vg, axis=1)


def frame_sums(prods, first):
    def lane(r):
        q = first + (r >> 7)
        return q + 2 * ((q * 43) >> 8)

    return mm2(jnp.concatenate(prods, axis=1), lane_matrix(12 * 128, lane))


def frame_block(turned, at, rows):
    return jnp.concatenate([turned[8 * m : 8 * m + 8, at : at + rows] for m in range(4)], axis=1)


def store_piece(ref, at, grad, frames):
    rows = grad.shape[0]
    for t in range(3):
        ref[at + rows * t : at + rows * (t + 1), :] = grad[:, 128 * t : 128 * t + 128]
    ref[at + 3 * rows : at + 3 * rows + 8, :] = frames


def backward_frames(grads, kv_ref, first):
    d_kg = [grads[:, 128 * a : 128 * a + 128] for a in range(3)]
    d_vg = [grads[:, 384 + 128 * a : 512 + 128 * a] for a in range(3)]
    k_local = [kv_ref[:, 1280 + 128 * b : 1408 + 128 * b] for b in range(3)]
    v_local = [kv_ref[:, 1664 + 128 * b : 1792 + 128 * b] for b in range(3)]
    prods = [d_kg[a] * k_local[b] + d_vg[a] * v_local[b] for a in range(3) for b in range(3)]
    return frame_sums(prods + [d_kg[a] + d_vg[a] for a in range(3)], first)


def backward_query(dl, kv_ref, own_fr, fcol, q_ref, pts_ref, wq_ref, sc, first_lane, share):
    rows = own_fr.shape[0]
    dh, dlo = split(dl)
    kh, klo = split(kv_ref[:, 0:640])
    qr = pick(mm3(dh, dlo, kh, klo), key_heads(rows), rows)
    rot, _ = columns(own_fr, fcol)
    d_qg = [sc * block(qr, a) for a in range(3)]
    d_ql = unrotate(rot, d_qg)
    grad = mm2(jnp.concatenate([PLAIN_SCALE * qr[:, 0:256]] + d_ql, axis=1), wq_ref[...])
    q_local = [q_ref[:, 640 + 128 * b : 768 + 128 * b] for b in range(3)]
    off, gpt, gptg = [
        [pts_ref[:, 384 * n + 128 * a : 384 * n + 128 * a + 128] for a in range(3)] for n in range(3)
    ]
    prods = [d_qg[a] * q_local[b] + share * off[a] * gpt[b] for a in range(3) for b in range(3)]
    prods = prods + [d_qg[a] - share * gptg[a] for a in range(3)]
    return grad, frame_sums(prods, first_lane)


def position(fast):
    if not fast:
        return True, 0, 0
    row = lax.axis_index("row")
    return row // 4 == lax.axis_index("col"), (row // 2) % 2, row % 2


def send_blocks(fast, src_ref, mine_a, mine_b, theirs, rows):
    _, zb, core = position(fast)

    def get(z, k):
        return src_ref[pl.ds(pl.multiple_of(jnp.int32((2 * z + k) * rows), 8), rows), :]

    mine_a[...] = get(zb, core)
    mine_b[...] = get(1 - zb, core)
    theirs[0:rows, :] = get(zb, 1 - core)
    theirs[rows:, :] = get(1 - zb, 1 - core)


def add_pieces(fast, query, query_other, part, one, two):
    return (query[...] + query_other[...]) + (one[...] + jnp.where(position(fast)[0], part[...], two[...]))


def final_body(fast, r0, r1, r2, r3, r4, one_ref, single_out, frames_out):
    total = add_pieces(fast, r0, r1, r2, r3, r4)
    rows = one_ref.shape[0]
    for t in range(3):
        lanes = slice(128 * t, 128 * t + 128)
        single_out[:, lanes] = one_ref[:, lanes] + total[rows * t : rows * (t + 1), :]
    for m in range(4):
        first = 6 * (m % 2)
        frames_out[first : first + 6, m // 2, :] = total[3 * rows : 3 * rows + 6, rows * m : rows * (m + 1)]


def frame_part(ref):
    return ref[:, FRAME_LANE : FRAME_LANE + 128]


def back_one_body(
    fast, e_mine, e_other, pm_ref, kv_ref, keys_ref, own_ref, q_ref, gp_ref, d_ref, wk_ref, sc_ref,
    z_ref, mine_a, mine_b, theirs, pts_ref, grads_ref, work_ref,
):
    e = e_mine[...] + e_other[...]
    pts_ref[...], grads_ref[...] = backward(
        e, e[:, 128:256], pm_ref[1], kv_ref, frame_part(keys_ref), frame_part(own_ref), 0, q_ref,
        gp_ref[...], d_ref, wk_ref, sc_ref[0:1, :], z_ref, work_ref,
    )
    send_blocks(fast, work_ref, mine_a, mine_b, theirs, own_ref.shape[0])


def query_one_body(
    share, z_ref, kv_ref, own_ref, q_ref, pts_ref, grads_ref, wq_ref, sc_ref, query_out, frq_ref, frk_ref
):
    half = z_ref.shape[0] // 2
    query_out[...], frq_ref[...] = backward_query(
        z_ref[half:, :], kv_ref, frame_part(own_ref), 0, q_ref, pts_ref, wq_ref, sc_ref[0:1, :], 12, share
    )
    frk_ref[...] = backward_frames(grads_ref[...], kv_ref, 12)


def back_zero_body(
    fast, cot_ref, r0, r1, r2, r3, r4, e_mine, e_other, tail_mine, tail_other, pm_ref, kv_ref, keys_ref, own_ref, q_ref, pair_ref,
    w_out_ref, wk_ref, sc_ref, frk_ref,
    z_ref, mine_a, mine_b, theirs, pts_ref, sum_ref, pu_ref, work_ref, pieces_ref, gp_ref, d_ref,
):
    rows = own_ref.shape[0]
    total = add_pieces(fast, r0, r1, r2, r3, r4)
    sum_ref[...] = total
    upstream_parts(cot_ref[...] + total, w_out_ref, gp_ref, pu_ref, rows)
    pair_products(pu_ref, pair_ref, d_ref, rows)
    gp = gp_ref[...]
    e = e_mine[:, 0:384] + e_other[:, 0:384]
    plain = e_mine[:, 384:640] + e_other[:, 384:640]
    dots = head_dots(gp[:, 0:256] * plain, rows)
    wide = jnp.concatenate(
        [
            pu_ref[h * rows : (h + 1) * rows, :]
            * (
                e_mine[:, 640 + CZ * h : 640 + CZ * (h + 1)] + e_other[:, 640 + CZ * h : 640 + CZ * (h + 1)]
                if h < EARLY
                else tail_mine[:, CZ * (h - EARLY) : CZ * (h - EARLY + 1)]
                + tail_other[:, CZ * (h - EARLY) : CZ * (h - EARLY + 1)]
            )
            for h in range(H)
        ],
        axis=1,
    )
    dots = dots + mm2(wide, lane_matrix(H * CZ, lambda r: STAT + (r >> 7)))
    pts_ref[...], grads = backward(
        e, dots, pm_ref[0], kv_ref, frame_part(keys_ref), frame_part(own_ref), 12, q_ref, gp, d_ref, wk_ref,
        sc_ref[0:1, :], z_ref, work_ref,
    )
    turned = jnp.transpose(backward_frames(grads, kv_ref, 0) + frk_ref[...])
    for n in range(4):
        at = n * pieces_ref.shape[0] // 4
        store_piece(pieces_ref, at, work_ref[rows * n : rows * (n + 1), :], frame_block(turned, rows * n, rows))
    send_blocks(fast, pieces_ref, mine_a, mine_b, theirs, mine_a.shape[0])


def query_zero_body(share, z_ref, kv_ref, own_ref, q_ref, pts_ref, wq_ref, sc_ref, frq_ref, query_out):
    half = z_ref.shape[0] // 2
    grad, frames = backward_query(
        z_ref[half:, :], kv_ref, frame_part(own_ref), 12, q_ref, pts_ref, wq_ref, sc_ref[0:1, :], 0, share
    )
    store_piece(query_out, 0, grad, frame_block(jnp.transpose(frames + frq_ref[...]), 0, own_ref.shape[0]))


def pair_body(z1_ref, z0_ref, pu1_ref, pu0_ref, wbt_ref, out_ref):
    rows = out_ref.shape[0]
    wbt = wbt_ref[...].astype(F32)
    for i in range(rows):
        left = jnp.concatenate(
            [z1_ref[pl.ds(i, 2 * H, stride=rows), :], z0_ref[pl.ds(i, 2 * H, stride=rows), :]], axis=0
        )
        right = jnp.concatenate(
            [pu1_ref[pl.ds(i, H, stride=rows), :], wbt, pu0_ref[pl.ds(i, H, stride=rows), :], wbt], axis=0
        ).astype(BF16)
        out_ref[i] = mm(left.astype(BF16), right, TN).astype(BF16)


VMEM = pl.BlockSpec(memory_space=pltpu.VMEM)
HBM = pl.BlockSpec(memory_space=pltpu.HBM)


def call(body, name, in_specs, outs, args, scratch=(), micros=1.0):
    return pl.pallas_call(
        body,
        name=name,
        in_specs=in_specs,
        out_specs=tuple(VMEM for _ in outs),
        out_shape=tuple(jax.ShapeDtypeStruct(s, d) for s, d in outs),
        scratch_shapes=list(scratch),
        compiler_params=pltpu.CompilerParams(vmem_limit_bytes=16 * 1024 * 1024),
        cost_estimate=pl.CostEstimate(flops=int(micros * 1e9), transcendentals=0, bytes_accessed=int(micros * 3e6)),
    )(*args)


def in_hbm(*arrays):
    return tuple(pltpu.with_memory_space_constraint(x, pltpu.HBM) for x in arrays)


def joint(pairs):
    return [
        ((a * 2 + k) * 2 + x, (b * 2 + k) * 2 + y) for (x, a), (y, b) in pairs for k in range(2)
    ]


BOTH = ("row", "col")
FETCH_ONE = joint([((0, 0), (0, 1)), ((0, 1), (0, 0)), ((1, 0), (0, 2)), ((1, 1), (0, 3)), ((1, 2), (1, 3)), ((1, 3), (1, 2)), ((0, 2), (1, 0)), ((0, 3), (1, 1))])
FETCH_TWO = joint([((0, 0), (0, 3)), ((0, 1), (0, 2)), ((1, 2), (1, 1)), ((1, 3), (1, 0)), ((1, 0), (0, 0)), ((1, 1), (0, 1)), ((0, 2), (1, 2)), ((0, 3), (1, 3))])
SEND_ONE = joint([((0, 0), (1, 0)), ((0, 1), (1, 1)), ((0, 2), (0, 0)), ((0, 3), (0, 1)), ((1, 2), (0, 2)), ((1, 3), (0, 3)), ((1, 0), (1, 2)), ((1, 1), (1, 3))])
SEND_TWO = joint([((0, 2), (1, 0)), ((0, 3), (1, 1)), ((1, 0), (0, 2)), ((1, 1), (0, 3)), ((0, 0), (0, 1)), ((0, 1), (0, 0)), ((1, 2), (1, 3)), ((1, 3), (1, 2))])
CORE_SWAP = [(i, i ^ 1) for i in range(8)]
Z_SWAP = [(i, i ^ 2) for i in range(8)]
COL_SWAP = [(0, 1), (1, 0)]


def local(
    single, frames, saved_probs, pair, cotangent, chains, links, w_query, w_key, w_value, w_query_points,
    w_key_points, w_value_points, w_bias, w_out, head_weights,
):
    rows = single.shape[1]
    keys = pair.shape[1]
    row_total = lax.axis_size("row")
    col_total = lax.axis_size("col")
    fast = row_total == 8 and col_total == 2 and keys == 4 * rows
    (pack,) = call(
        pack_body, "pack", [HBM] * 3, [((rows, PACK), F32)], in_hbm(single, frames.transpose(1, 0, 2), chains[None]),
        [pltpu.VMEM((12, 2, rows), F32), pltpu.VMEM((1, rows), jnp.int32), pltpu.SemaphoreType.DMA((4,))],
    )
    col = lax.axis_index("col")
    row = lax.axis_index("row")
    if fast:
        ownx = lax.ppermute(pack, "row", CORE_SWAP)
        one = lax.ppermute(pack, BOTH, FETCH_ONE)
        two = lax.ppermute(pack, BOTH, FETCH_TWO)
        own = pack
    else:
        whole = lax.all_gather(pack, "row", axis=0, tiled=True)
        mine = lax.dynamic_slice_in_dim(whole, col * keys, keys, 0)
        quarter = keys // 4
        blocks = tuple(mine[quarter * n : quarter * (n + 1)] for n in (0, 1, 2, 3, 0, 0))
        own = pack

    def col_other(x):
        if col_total == 2:
            return lax.ppermute(x, "col", COL_SWAP)
        return lax.psum(x, "col") - x

    def reduce(mine_a, mine_b, theirs, late, first_beside, beside):
        if fast:
            got = lax.ppermute(theirs, "row", CORE_SWAP)
            query, *rest = late()
            got, query, first_beside = lax.optimization_barrier((got, query, first_beside))
            query_other = lax.ppermute(query, "col", COL_SWAP)
            count = mine_a.shape[0]
            half = lax.ppermute(mine_b + got[count:], "row", Z_SWAP)
            half, beside = lax.optimization_barrier((half, beside))
            part = mine_a + got[:count] + half
            sent = [lax.ppermute(part, BOTH, SEND_ONE), lax.ppermute(part, BOTH, SEND_TWO)]
            return [query, query_other, part] + sent, rest, (first_beside, beside)
        query, *rest = late()
        count = mine_a.shape[0]
        parts = jnp.concatenate([mine_a, theirs[:count], mine_b, theirs[count:]], axis=0)
        summed = lax.all_gather(lax.psum(parts, "row"), "col", axis=0, tiled=True)
        back = lax.dynamic_slice_in_dim(summed, row * count, count, 0)
        zero = jnp.zeros_like(query)
        return [lax.psum(query, "col"), zero, back, zero, zero], rest, (first_beside, beside)

    probs = saved_probs.reshape(2, H * rows, keys)
    hr = H * rows
    loads = (
        cotangent, w_out, pair, w_query.T, w_key.T, w_value.T, w_query_points.T, w_key_points.T, w_value_points.T,
        head_weights[None],
    )
    wk, wq, gp1, q1, q0, pu1, d1, sc = call(
        prep_body, "prep", [VMEM] + [HBM] * 10,
        [((1280, C), BF16), ((LANES, C), BF16), ((rows, 768), F32), ((rows, 1024), F32), ((rows, 1024), F32),
         ((hr, CZ), F32), ((hr, keys), F32), ((8, 128), F32)],
        (own, *in_hbm(*loads)),
        [pltpu.VMEM(x.shape, x.dtype) for x in loads] + [pltpu.SemaphoreType.DMA((len(loads),))],
    )
    if fast:
        one, two, wk, wq, gp1, q1, q0, pu1, d1, sc = lax.optimization_barrier(
            (one, two, wk, wq, gp1, q1, q0, pu1, d1, sc)
        )
        blocks = (pack, ownx, one, lax.ppermute(one, "row", CORE_SWAP), two, lax.ppermute(two, "row", CORE_SWAP))
    key_pack, kv1, pm, e1 = call(
        functools.partial(first_body, fast), "first", [VMEM] * 11,
        [((keys, PACK), F32), ((keys, 2048), F32), ((2, hr, keys), BF16), ((rows, 384), F32)],
        (*blocks, wk, links, probs, gp1, d1),
    )
    e1_other = col_other(e1)
    kv0, e0, tail = call(
        second_body, "second", [VMEM] * 4,
        [((keys, 2048), F32), ((rows, 640 + EARLY * CZ), F32), ((rows, (H - EARLY) * CZ), F32)],
        (key_pack, wk, pm, pair),
        [pltpu.VMEM((hr, keys), F32), pltpu.VMEM((hr, CZ), F32)],
    )
    e0_other = col_other(e0)
    tail_other = col_other(tail)
    share = 1.0 / col_total
    e1_other, e0 = lax.optimization_barrier((e1_other, e0))
    z1, mine_a, mine_b, theirs, pts, grads = call(
        functools.partial(back_one_body, fast), "back_one", [VMEM] * 11,
        [((2 * hr, keys), F32), ((rows, C), F32), ((rows, C), F32), ((2 * rows, C), F32), ((rows, 1152), F32),
         ((keys, 768), F32)],
        (e1, e1_other, pm, kv1, key_pack, own, q1, gp1, d1, wk, sc),
        [pltpu.VMEM((keys, C), F32)],
        6.0,
    )
    pieces, (frq, frk), (e0_other, tail_other) = reduce(
        mine_a, mine_b, theirs,
        lambda: call(
            functools.partial(query_one_body, share), "query_one", [VMEM] * 8,
            [((rows, C), F32), ((rows, 128), F32), ((keys, 128), F32)],
            (z1, kv1, own, q1, pts, grads, wq, sc),
            (),
            0.01,
        ),
        e0_other,
        tail_other,
    )
    long = 3 * rows + 8
    z0, mine_a, mine_b, theirs, pts, single_one, pu0 = call(
        functools.partial(back_zero_body, fast), "back_zero", [VMEM] * 20,
        [((2 * hr, keys), F32), ((long, 128), F32), ((long, 128), F32), ((2 * long, 128), F32), ((rows, 1152), F32),
         ((rows, C), F32), ((hr, CZ), F32)],
        (cotangent, *pieces, e0, e0_other, tail, tail_other, pm, kv0, key_pack, own, q0, pair, w_out, wk, sc, frk),
        [pltpu.VMEM((keys, C), F32), pltpu.VMEM((4 * long, 128), F32), pltpu.VMEM((rows, 768), F32), pltpu.VMEM((hr, keys), F32)],
    )
    (d_pair,) = call(
        pair_body, "pair_grad", [VMEM] * 5, [((rows, keys, CZ), BF16)], (z1, z0, pu1, pu0, w_bias.T)
    )
    pieces, _, (_, d_pair) = reduce(
        mine_a, mine_b, theirs,
        lambda: call(
            functools.partial(query_zero_body, share), "query_zero", [VMEM] * 8, [((long, 128), F32)],
            (z0, kv0, own, q0, pts, wq, sc, frq),
        ),
        (),
        d_pair,
    )
    d_single, d_frames = call(
        functools.partial(final_body, fast), "final", [VMEM] * 6, [((rows, C), F32), ((12, 2, rows), F32)],
        (*pieces, single_one),
    )
    return (d_single, d_frames.transpose(1, 0, 2), d_pair)


def solution(mesh):
    return jax.shard_map(
        local,
        mesh=mesh,
        in_specs=(
            P(None, ("grp", "row"), None),
            P(None, None, ("grp", "row")),
            P(None, None, ("grp", "row"), "col"),
            P(("grp", "row"), "col", None),
            P(("grp", "row"), None),
            P(("grp", "row")),
            P("grp", None),
            P(),
            P(),
            P(),
            P(),
            P(),
            P(),
            P(),
            P(),
            P(),
        ),
        out_specs=(
            P(("grp", "row"), None),
            P(None, None, ("grp", "row")),
            P(("grp", "row"), "col", None),
        ),
        check_vma=False,
    )
```

```python
import functools
import math

import jax
import jax.numpy as jnp
from jax import lax
from jax.experimental import pallas as pl
from jax.experimental.pallas import tpu as pltpu
from jax.sharding import PartitionSpec as P

C = 384
H = 12
HD = 16
CZ = 128
PQ = 4
PV = 8
NCHAIN = 16
NORM_EPS = 1e-08
LOGIT_SCALE = math.sqrt(1.0 / 3.0)
PLAIN_SCALE = 1.0 / math.sqrt(HD)
POINT_SCALE = math.sqrt(2.0 / (9.0 * PQ))

LANES = 640
PACK = 896
FRAME_LANE = 768
CHAIN_LANE = 792
STAT = 96
EARLY = 4

F32 = jnp.float32
BF16 = jnp.bfloat16
NN = (((1,), (0,)), ((), ()))
NT = (((1,), (1,)), ((), ()))
TN = (((0,), (0,)), ((), ()))


def mm(a, b, dims=NN):
    return lax.dot_general(a, b, dims, preferred_element_type=F32)


def split(x):
    hi = x.astype(BF16)
    return hi, (x - hi.astype(F32)).astype(BF16)


def mm2(x, w, dims=NN):
    hi, lo = split(x)
    rows = x.shape[0]
    both = mm(jnp.concatenate([hi, lo], axis=0), w, dims)
    return both[:rows] + both[rows:]


def mm3(ah, al, bh, bl, dims=NN):
    return mm(ah, bh, dims) + mm(ah, bl, dims) + mm(al, bh, dims)


def iota(shape, axis):
    return lax.broadcasted_iota(jnp.int32, shape, axis)


def key_heads(rows):
    lane = iota((rows, LANES), 1)
    return jnp.where(lane < 256, lane >> 4, (lane & 127) >> 2)


def value_heads(rows):
    lane = iota((rows, LANES), 1)
    inner = lane & 127
    points = jnp.where(inner < STAT, inner >> 3, inner - STAT)
    return jnp.where(lane < 256, lane >> 4, points)


def pick(full, heads, rows):
    out = None
    for h in range(H):
        part = jnp.where(heads == h, full[h * rows : (h + 1) * rows], 0.0)
        out = part if out is None else out + part
    return out


def spread(x, heads):
    return jnp.concatenate([jnp.where(heads == h, x, 0.0) for h in range(H)], axis=0)


def spread2(x, heads):
    hi, lo = split(x)
    hi32, lo32 = hi.astype(F32), lo.astype(F32)
    return spread(hi32, heads).astype(BF16), spread(lo32, heads).astype(BF16)


def columns(frames_block, first):
    cols = [frames_block[:, first + n : first + n + 1] for n in range(12)]
    return [[cols[3 * a + b] for b in range(3)] for a in range(3)], cols[9:]


def block(x, a):
    return x[:, 256 + 128 * a : 384 + 128 * a]


def rotate(rot, pts):
    return [sum(rot[a][b] * pts[b] for b in range(3)) for a in range(3)]


def unrotate(rot, pts):
    return [sum(rot[a][b] * pts[a] for a in range(3)) for b in range(3)]


def place(rot, shift, flat):
    local_pts = [block(flat, a) for a in range(3)]
    turned = rotate(rot, local_pts)
    return jnp.concatenate(
        [flat[:, :256]] + [turned[a] + shift[a] for a in range(3)], axis=1
    )


def lane_matrix(rows, fn):
    r = iota((rows, 128), 0)
    c = iota((rows, 128), 1)
    return (fn(r) == c).astype(F32).astype(BF16)


def upstream_parts(g, w_out_ref, gp_ref, pu_ref, rows):
    hi, lo = split(g)
    both = jnp.concatenate([hi, lo], axis=0)

    def part(first, count):
        r = mm(both, w_out_ref[first : first + count, :], NT)
        return r[:rows] + r[rows:]

    gp_ref[...] = jnp.zeros(gp_ref.shape, F32)
    gp_ref[:, 0:192] = part(0, 192)
    for a in range(4):
        gp_ref[:, 256 + 128 * a : 352 + 128 * a] = part(192 + 96 * a, 96)
    wide = part(576, H * CZ)
    for h in range(H):
        pu_ref[h * rows : (h + 1) * rows, :] = (
            wide[:, h * CZ : (h + 1) * CZ].astype(BF16).astype(F32)
        )


def pair_products(pu_ref, pair_ref, d_ref, rows):
    for i in range(0, rows, 2):
        lhs = jnp.concatenate([pu_ref[pl.ds(i, H, stride=rows), :], pu_ref[pl.ds(i + 1, H, stride=rows), :]], axis=0)
        both = mm(lhs.astype(BF16), pair_ref[i : i + 2].reshape(-1, CZ), NT)
        keys = both.shape[1] // 2
        d_ref[pl.ds(i, H, stride=rows), :] = both[:H, :keys]
        d_ref[pl.ds(i + 1, H, stride=rows), :] = both[H:, keys:]


def split3(x):
    hi, _ = split(x)
    rest = x - hi.astype(F32)
    mid, lo = split(rest)
    return hi, mid, lo


def pack_body(single_hbm, frames_hbm, chains_hbm, pack_ref, frames_ref, chains_ref, sems):
    rows = pack_ref.shape[0]
    ends = (
        (frames_hbm, frames_ref), (chains_hbm, chains_ref), (single_hbm.at[1], pack_ref.at[:, 0:C]),
        (single_hbm.at[0], pack_ref.at[:, C : 2 * C]),
    )
    copies = [pltpu.make_async_copy(src, dst, sems.at[n]) for n, (src, dst) in enumerate(ends)]
    for copy in copies:
        copy.start()
    copies[0].wait()
    copies[1].wait()
    out = jnp.zeros((rows, 128), F32)
    for slot, l in ((0, 1), (12, 0)):
        hot = (iota((12, 128), 1) == iota((12, 128), 0) + slot).astype(F32).astype(BF16)
        for part in split3(frames_ref[:, l, :]):
            out = out + mm(part, hot, TN)
    hot = (iota((1, 128), 1) == CHAIN_LANE - FRAME_LANE).astype(F32).astype(BF16)
    pack_ref[:, 2 * C :] = out + mm(chains_ref[...].astype(F32).astype(BF16), hot, TN)
    copies[2].wait()
    copies[3].wait()


def prep_body(
    pack_ref, cot_hbm, w_out_hbm, pair_hbm, wq_hbm, wk_hbm, wv_hbm, wqp_hbm, wkp_hbm, wvp_hbm, hw_hbm,
    wk_out, wq_out, gp_ref, q1_ref, q0_ref, pu_ref, d_ref, sc_ref,
    cot_ref, w_out_ref, pair_ref, wq_ref, wk_ref, wv_ref, wqp_ref, wkp_ref, wvp_ref, hw_ref, sems,
):
    rows = pack_ref.shape[0]
    ends = (
        (cot_hbm, cot_ref), (w_out_hbm, w_out_ref), (pair_hbm, pair_ref), (wq_hbm, wq_ref), (wk_hbm, wk_ref),
        (wv_hbm, wv_ref), (wqp_hbm, wqp_ref), (wkp_hbm, wkp_ref), (wvp_hbm, wvp_ref), (hw_hbm, hw_ref),
    )
    copies = [pltpu.make_async_copy(src, dst, sems.at[n]) for n, (src, dst) in enumerate(ends)]
    for copy in copies:
        copy.start()
    copies[0].wait()
    copies[1].wait()
    upstream_parts(cot_ref[...], w_out_ref, gp_ref, pu_ref, rows)
    copies[2].wait()
    pair_products(pu_ref, pair_ref, d_ref, rows)
    for copy in copies[3:]:
        copy.wait()
    wq_out[...] = jnp.zeros(wq_out.shape, BF16)
    wk_out[...] = jnp.zeros(wk_out.shape, BF16)
    wq_out[0:192, :] = wq_ref[...]
    wk_out[0:192, :] = wk_ref[...]
    wk_out[640:832, :] = wv_ref[...]
    for a in range(3):
        wq_out[256 + 128 * a : 304 + 128 * a, :] = wqp_ref[48 * a : 48 * a + 48, :]
        wk_out[256 + 128 * a : 304 + 128 * a, :] = wkp_ref[48 * a : 48 * a + 48, :]
        wk_out[896 + 128 * a : 992 + 128 * a, :] = wvp_ref[96 * a : 96 * a + 96, :]
    lane = iota((8, 128), 1)
    raw = jnp.zeros((8, 128), F32)
    for h in range(H):
        raw = jnp.where((lane >> 2) == h, hw_ref[:, h : h + 1], raw)
    soft = jnp.maximum(raw, 0.0) + jnp.log(1.0 + jnp.exp(-jnp.abs(raw)))
    sc_ref[...] = soft * POINT_SCALE
    fr = pack_ref[:, FRAME_LANE : FRAME_LANE + 128]
    for out, first, fcol in ((q1_ref, 0, 0), (q0_ref, C, 12)):
        flat = mm2(pack_ref[:, first : first + C], wq_out[...], NT)
        rot, shift = columns(fr, fcol)
        out[:, :LANES] = place(rot, shift, flat)
        out[:, LANES:] = flat[:, 256:]


def project_keys(x, fr, fcol, wk_ref, kv_ref):
    flat = mm2(x, wk_ref[...], NT)
    rot, shift = columns(fr, fcol)
    kv_ref[:, 0:640] = place(rot, shift, flat[:, :640])
    kv_ref[:, 640:1280] = place(rot, shift, flat[:, 640:])
    kv_ref[:, 1280:1664] = flat[:, 256:640]
    kv_ref[:, 1664:2048] = flat[:, 896:1280]


def value_sums(probs, kv_ref, rows):
    values = kv_ref[:, 640:1280]
    lane = iota(values.shape, 1)
    values = jnp.where((lane >= 256 + STAT) & (lane < 256 + STAT + H), 1.0, values)
    hi, lo = split(values)
    return pick(mm(probs, hi) + mm(probs, lo), value_heads(rows), rows)


def head_dots(prod, rows):
    return mm2(prod, lane_matrix(256, lambda r: STAT + (r >> 4)))


def first_body(
    fast, own_ref, ownx_ref, p1_ref, p1x_ref, p2_ref, p2x_ref, wk_ref, links_ref, probs_ref, gp_ref, d_ref,
    keys_ref, kv_ref, pm_ref, e_ref,
):
    rows = own_ref.shape[0]
    home, zb, core = position(fast)

    def put(z, k, value):
        keys_ref[pl.ds(pl.multiple_of(jnp.int32((2 * z + k) * rows), rows), rows), :] = value

    put(zb, core, jnp.where(home, own_ref[...], p1_ref[...]))
    put(zb, 1 - core, jnp.where(home, ownx_ref[...], p1x_ref[...]))
    put(1 - zb, core, jnp.where(home, p1_ref[...], p2_ref[...]))
    put(1 - zb, 1 - core, jnp.where(home, p1x_ref[...], p2x_ref[...]))
    fr = keys_ref[:, FRAME_LANE : FRAME_LANE + 128]
    keys = fr.shape[0]
    at = CHAIN_LANE - FRAME_LANE
    key_chain = fr[:, at : at + 1]
    own_chain = own_ref[:, FRAME_LANE : FRAME_LANE + 128][:, at : at + 1]
    key_hot = (iota((keys, NCHAIN), 1).astype(F32) == key_chain).astype(F32).astype(BF16)
    own_hot = (iota((rows, NCHAIN), 1).astype(F32) == own_chain).astype(F32).astype(BF16)
    eye = iota((NCHAIN, NCHAIN), 0) == iota((NCHAIN, NCHAIN), 1)
    allowed = jnp.where(eye, 1.0, links_ref[...].astype(F32)).astype(BF16)
    mask = mm(mm(own_hot, allowed).astype(BF16), key_hot, NT)
    mask_all = jnp.concatenate([mask] * H, axis=0)
    for l in range(2):
        pm_ref[l] = (probs_ref[l].astype(F32) * mask_all).astype(BF16)
    project_keys(keys_ref[:, 0:C], fr, 0, wk_ref, kv_ref)
    probs = pm_ref[1]
    sums = value_sums(probs, kv_ref, rows)
    weighted = mm2(probs.astype(F32) * d_ref[...], jnp.ones((keys, 128), BF16))
    lane = iota((rows, 128), 1)
    dots = pick(weighted, lane - STAT, rows) + head_dots(gp_ref[:, 0:256] * sums[:, 0:256], rows)
    e_ref[:, 0:128] = block(sums, 0)
    e_ref[:, 128:256] = jnp.where(lane < STAT, block(sums, 1), dots)
    e_ref[:, 256:384] = block(sums, 2)


def second_body(keys_ref, wk_ref, pm_ref, pair_ref, kv_ref, e_ref, tail_ref, p32_ref, op_ref):
    rows = pair_ref.shape[0]
    fr = keys_ref[:, FRAME_LANE : FRAME_LANE + 128]
    project_keys(keys_ref[:, C : 2 * C], fr, 12, wk_ref, kv_ref)
    probs = pm_ref[0]
    sums = value_sums(probs, kv_ref, rows)
    for a in range(3):
        e_ref[:, 128 * a : 128 * a + 128] = block(sums, a)
    e_ref[:, 384:640] = sums[:, 0:256]
    p32_ref[...] = probs.astype(F32)
    for i in range(rows):
        lhs = p32_ref[pl.ds(i, H, stride=rows), :].astype(BF16)
        op_ref[pl.ds(i, H, stride=rows), :] = mm(lhs, pair_ref[i])
    for h in range(H):
        ref, first = (e_ref, 640 + CZ * h) if h < EARLY else (tail_ref, CZ * (h - EARLY))
        ref[:, first : first + CZ] = op_ref[h * rows : (h + 1) * rows, :]


def backward(
    e, dots, probs, kv_ref, key_fr, own_fr, fcol, q_ref, gp, d_ref, wk_ref, sc,
    z_ref, keys_out_ref,
):
    rows = e.shape[0]
    lane = iota((rows, 128), 1)
    stat = (lane >= STAT) & (lane < STAT + H)
    inv = jnp.where(stat, 1.0 / jnp.where(stat, e[:, 0:128], 1.0), 0.0)
    r128 = iota((128, LANES), 0)
    grow = (r128 - STAT == value_heads(128)) & ((iota((128, LANES), 1) & 127) < STAT)
    grow = grow | ((r128 - STAT == (iota((128, LANES), 1) >> 4)) & (iota((128, LANES), 1) < 256))
    inv_lanes = mm2(inv, grow.astype(F32).astype(BF16))
    rot, shift = columns(own_fr, fcol)
    inv_pts = block(inv_lanes, 0)
    ptg = [e[:, 128 * a : 128 * a + 128] * inv_pts for a in range(3)]
    off = [jnp.where(lane < STAT, ptg[a] - shift[a], 0.0) for a in range(3)]
    opt = unrotate(rot, off)
    length = jnp.sqrt(opt[0] * opt[0] + opt[1] * opt[1] + opt[2] * opt[2] + NORM_EPS)
    scale = gp[:, 640:768] / length
    gpt = [block(gp, a) + scale * opt[a] for a in range(3)]
    gptg = rotate(rot, gpt)
    upper = jnp.concatenate([gp[:, 0:256]] + gptg, axis=1)
    point_dots = gptg[0] * ptg[0] + gptg[1] * ptg[1] + gptg[2] * ptg[2]
    rd = dots * inv + mm2(point_dots, lane_matrix(128, lambda r: STAT + (r >> 3)))
    both = jnp.concatenate([spread(rd, lane - STAT), spread(inv, lane - STAT)], axis=0)
    wide = mm2(both, jnp.ones((128, 128), BF16))
    rd_all, inv_all = wide[: H * rows], wide[H * rows :]
    heads_v = value_heads(rows)
    heads_k = key_heads(rows)
    uh, ul = spread2(upper, heads_v)
    vh, vl = split(kv_ref[:, 640:1280])
    d_att = d_ref[...] + mm3(uh, ul, vh, vl, NT)
    p32 = probs.astype(F32)
    att = p32 * inv_all
    dl = LOGIT_SCALE * att * (d_att - rd_all)
    z_ref[0 : H * rows, :] = att
    z_ref[H * rows :, :] = dl
    dt = jnp.transpose(dl)
    th, tl = split(dt)
    qh, qlo = spread2(q_ref[:, 0:640], heads_k)
    kr = mm3(th, tl, qh, qlo)
    head_rows = iota((H * rows, 128), 0) // rows
    hot = ((iota((H * rows, 128), 1) >> 2) == head_rows).astype(F32).astype(BF16)
    cs = mm(th, hot) + mm(tl, hot)
    pt = jnp.transpose(p32).astype(BF16)
    sh, sl = spread2(upper * inv_lanes, heads_v)
    vr = mm(pt, sh) + mm(pt, sl)
    krot, _ = columns(key_fr, fcol)
    d_kg = [sc * (block(kr, a) - cs * kv_ref[:, 256 + 128 * a : 384 + 128 * a]) for a in range(3)]
    d_vg = [block(vr, a) for a in range(3)]
    d_kl = unrotate(krot, d_kg)
    d_vl = unrotate(krot, d_vg)
    flat = jnp.concatenate([PLAIN_SCALE * kr[:, 0:256]] + d_kl + [vr[:, 0:256]] + d_vl, axis=1)
    keys_out_ref[:, 0:C] = mm2(flat, wk_ref[...])
    return jnp.concatenate(off + gpt + gptg, axis=1), jnp.concatenate(d_kg + d_vg, axis=1)


def frame_sums(prods, first):
    def lane(r):
        q = first + (r >> 7)
        return q + 2 * ((q * 43) >> 8)

    return mm2(jnp.concatenate(prods, axis=1), lane_matrix(12 * 128, lane))


def frame_block(turned, at, rows):
    return jnp.concatenate([turned[8 * m : 8 * m + 8, at : at + rows] for m in range(4)], axis=1)


def store_piece(ref, at, grad, frames):
    rows = grad.shape[0]
    for t in range(3):
        ref[at + rows * t : at + rows * (t + 1), :] = grad[:, 128 * t : 128 * t + 128]
    ref[at + 3 * rows : at + 3 * rows + 8, :] = frames


def backward_frames(grads, kv_ref, first):
    d_kg = [grads[:, 128 * a : 128 * a + 128] for a in range(3)]
    d_vg = [grads[:, 384 + 128 * a : 512 + 128 * a] for a in range(3)]
    k_local = [kv_ref[:, 1280 + 128 * b : 1408 + 128 * b] for b in range(3)]
    v_local = [kv_ref[:, 1664 + 128 * b : 1792 + 128 * b] for b in range(3)]
    prods = [d_kg[a] * k_local[b] + d_vg[a] * v_local[b] for a in range(3) for b in range(3)]
    return frame_sums(prods + [d_kg[a] + d_vg[a] for a in range(3)], first)


def backward_query(dl, kv_ref, own_fr, fcol, q_ref, pts_ref, wq_ref, sc, first_lane, share):
    rows = own_fr.shape[0]
    dh, dlo = split(dl)
    kh, klo = split(kv_ref[:, 0:640])
    qr = pick(mm3(dh, dlo, kh, klo), key_heads(rows), rows)
    rot, _ = columns(own_fr, fcol)
    d_qg = [sc * block(qr, a) for a in range(3)]
    d_ql = unrotate(rot, d_qg)
    grad = mm2(jnp.concatenate([PLAIN_SCALE * qr[:, 0:256]] + d_ql, axis=1), wq_ref[...])
    q_local = [q_ref[:, 640 + 128 * b : 768 + 128 * b] for b in range(3)]
    off, gpt, gptg = [
        [pts_ref[:, 384 * n + 128 * a : 384 * n + 128 * a + 128] for a in range(3)] for n in range(3)
    ]
    prods = [d_qg[a] * q_local[b] + share * off[a] * gpt[b] for a in range(3) for b in range(3)]
    prods = prods + [d_qg[a] - share * gptg[a] for a in range(3)]
    return grad, frame_sums(prods, first_lane)


def position(fast):
    if not fast:
        return True, 0, 0
    row = lax.axis_index("row")
    return row // 4 == lax.axis_index("col"), (row // 2) % 2, row % 2


def send_blocks(fast, src_ref, mine_a, mine_b, theirs, rows):
    _, zb, core = position(fast)

    def get(z, k):
        return src_ref[pl.ds(pl.multiple_of(jnp.int32((2 * z + k) * rows), 8), rows), :]

    mine_a[...] = get(zb, core)
    mine_b[...] = get(1 - zb, core)
    theirs[0:rows, :] = get(zb, 1 - core)
    theirs[rows:, :] = get(1 - zb, 1 - core)


def add_pieces(fast, query, query_other, part, one, two):
    return (query[...] + query_other[...]) + (one[...] + jnp.where(position(fast)[0], part[...], two[...]))


def final_body(fast, r0, r1, r2, r3, r4, one_ref, single_out, frames_out):
    total = add_pieces(fast, r0, r1, r2, r3, r4)
    rows = one_ref.shape[0]
    for t in range(3):
        lanes = slice(128 * t, 128 * t + 128)
        single_out[:, lanes] = one_ref[:, lanes] + total[rows * t : rows * (t + 1), :]
    for m in range(4):
        first = 6 * (m % 2)
        frames_out[first : first + 6, m // 2, :] = total[3 * rows : 3 * rows + 6, rows * m : rows * (m + 1)]


def frame_part(ref):
    return ref[:, FRAME_LANE : FRAME_LANE + 128]


def back_one_body(
    fast, e_mine, e_other, pm_ref, kv_ref, keys_ref, own_ref, q_ref, gp_ref, d_ref, wk_ref, sc_ref,
    z_ref, mine_a, mine_b, theirs, pts_ref, grads_ref, work_ref,
):
    e = e_mine[...] + e_other[...]
    pts_ref[...], grads_ref[...] = backward(
        e, e[:, 128:256], pm_ref[1], kv_ref, frame_part(keys_ref), frame_part(own_ref), 0, q_ref,
        gp_ref[...], d_ref, wk_ref, sc_ref[0:1, :], z_ref, work_ref,
    )
    send_blocks(fast, work_ref, mine_a, mine_b, theirs, own_ref.shape[0])


def query_one_body(
    share, z_ref, kv_ref, own_ref, q_ref, pts_ref, grads_ref, wq_ref, sc_ref, query_out, frq_ref, frk_ref
):
    half = z_ref.shape[0] // 2
    query_out[...], frq_ref[...] = backward_query(
        z_ref[half:, :], kv_ref, frame_part(own_ref), 0, q_ref, pts_ref, wq_ref, sc_ref[0:1, :], 12, share
    )
    frk_ref[...] = backward_frames(grads_ref[...], kv_ref, 12)


def back_zero_body(
    fast, cot_ref, r0, r1, r2, r3, r4, e_mine, e_other, tail_mine, tail_other, pm_ref, kv_ref, keys_ref, own_ref, q_ref, pair_ref,
    w_out_ref, wk_ref, sc_ref, frk_ref,
    z_ref, mine_a, mine_b, theirs, pts_ref, sum_ref, pu_ref, work_ref, pieces_ref, gp_ref, d_ref,
):
    rows = own_ref.shape[0]
    total = add_pieces(fast, r0, r1, r2, r3, r4)
    sum_ref[...] = total
    upstream_parts(cot_ref[...] + total, w_out_ref, gp_ref, pu_ref, rows)
    pair_products(pu_ref, pair_ref, d_ref, rows)
    gp = gp_ref[...]
    e = e_mine[:, 0:384] + e_other[:, 0:384]
    plain = e_mine[:, 384:640] + e_other[:, 384:640]
    dots = head_dots(gp[:, 0:256] * plain, rows)
    wide = jnp.concatenate(
        [
            pu_ref[h * rows : (h + 1) * rows, :]
            * (
                e_mine[:, 640 + CZ * h : 640 + CZ * (h + 1)] + e_other[:, 640 + CZ * h : 640 + CZ * (h + 1)]
                if h < EARLY
                else tail_mine[:, CZ * (h - EARLY) : CZ * (h - EARLY + 1)]
                + tail_other[:, CZ * (h - EARLY) : CZ * (h - EARLY + 1)]
            )
            for h in range(H)
        ],
        axis=1,
    )
    dots = dots + mm2(wide, lane_matrix(H * CZ, lambda r: STAT + (r >> 7)))
    pts_ref[...], grads = backward(
        e, dots, pm_ref[0], kv_ref, frame_part(keys_ref), frame_part(own_ref), 12, q_ref, gp, d_ref, wk_ref,
        sc_ref[0:1, :], z_ref, work_ref,
    )
    turned = jnp.transpose(backward_frames(grads, kv_ref, 0) + frk_ref[...])
    for n in range(4):
        at = n * pieces_ref.shape[0] // 4
        store_piece(pieces_ref, at, work_ref[rows * n : rows * (n + 1), :], frame_block(turned, rows * n, rows))
    send_blocks(fast, pieces_ref, mine_a, mine_b, theirs, mine_a.shape[0])


def query_zero_body(share, z_ref, kv_ref, own_ref, q_ref, pts_ref, wq_ref, sc_ref, frq_ref, query_out):
    half = z_ref.shape[0] // 2
    grad, frames = backward_query(
        z_ref[half:, :], kv_ref, frame_part(own_ref), 12, q_ref, pts_ref, wq_ref, sc_ref[0:1, :], 0, share
    )
    store_piece(query_out, 0, grad, frame_block(jnp.transpose(frames + frq_ref[...]), 0, own_ref.shape[0]))


def pair_body(z1_ref, z0_ref, pu1_ref, pu0_ref, wbt_ref, out_ref):
    rows = out_ref.shape[0]
    wbt = wbt_ref[...].astype(F32)
    for i in range(rows):
        left = jnp.concatenate(
            [z1_ref[pl.ds(i, 2 * H, stride=rows), :], z0_ref[pl.ds(i, 2 * H, stride=rows), :]], axis=0
        )
        right = jnp.concatenate(
            [pu1_ref[pl.ds(i, H, stride=rows), :], wbt, pu0_ref[pl.ds(i, H, stride=rows), :], wbt], axis=0
        ).astype(BF16)
        out_ref[i] = mm(left.astype(BF16), right, TN).astype(BF16)


VMEM = pl.BlockSpec(memory_space=pltpu.VMEM)
HBM = pl.BlockSpec(memory_space=pltpu.HBM)


def call(body, name, in_specs, outs, args, scratch=(), micros=1.0):
    return pl.pallas_call(
        body,
        name=name,
        in_specs=in_specs,
        out_specs=tuple(VMEM for _ in outs),
        out_shape=tuple(jax.ShapeDtypeStruct(s, d) for s, d in outs),
        scratch_shapes=list(scratch),
        compiler_params=pltpu.CompilerParams(vmem_limit_bytes=16 * 1024 * 1024),
        cost_estimate=pl.CostEstimate(flops=int(micros * 1e9), transcendentals=0, bytes_accessed=int(micros * 3e6)),
    )(*args)


def in_hbm(*arrays):
    return tuple(pltpu.with_memory_space_constraint(x, pltpu.HBM) for x in arrays)


def joint(pairs):
    return [
        ((a * 2 + k) * 2 + x, (b * 2 + k) * 2 + y) for (x, a), (y, b) in pairs for k in range(2)
    ]


BOTH = ("row", "col")
FETCH_ONE = joint([((0, 0), (0, 1)), ((0, 1), (0, 0)), ((1, 0), (0, 2)), ((1, 1), (0, 3)), ((1, 2), (1, 3)), ((1, 3), (1, 2)), ((0, 2), (1, 0)), ((0, 3), (1, 1))])
FETCH_TWO = joint([((0, 0), (0, 3)), ((0, 1), (0, 2)), ((1, 2), (1, 1)), ((1, 3), (1, 0)), ((1, 0), (0, 0)), ((1, 1), (0, 1)), ((0, 2), (1, 2)), ((0, 3), (1, 3))])
SEND_ONE = joint([((0, 0), (1, 0)), ((0, 1), (1, 1)), ((0, 2), (0, 0)), ((0, 3), (0, 1)), ((1, 2), (0, 2)), ((1, 3), (0, 3)), ((1, 0), (1, 2)), ((1, 1), (1, 3))])
SEND_TWO = joint([((0, 2), (1, 0)), ((0, 3), (1, 1)), ((1, 0), (0, 2)), ((1, 1), (0, 3)), ((0, 0), (0, 1)), ((0, 1), (0, 0)), ((1, 2), (1, 3)), ((1, 3), (1, 2))])
CORE_SWAP = [(i, i ^ 1) for i in range(8)]
Z_SWAP = [(i, i ^ 2) for i in range(8)]
COL_SWAP = [(0, 1), (1, 0)]


def local(
    single, frames, saved_probs, pair, cotangent, chains, links, w_query, w_key, w_value, w_query_points,
    w_key_points, w_value_points, w_bias, w_out, head_weights,
):
    rows = single.shape[1]
    keys = pair.shape[1]
    row_total = lax.axis_size("row")
    col_total = lax.axis_size("col")
    fast = row_total == 8 and col_total == 2 and keys == 4 * rows
    (pack,) = call(
        pack_body, "pack", [HBM] * 3, [((rows, PACK), F32)], in_hbm(single, frames.transpose(1, 0, 2), chains[None]),
        [pltpu.VMEM((12, 2, rows), F32), pltpu.VMEM((1, rows), jnp.int32), pltpu.SemaphoreType.DMA((4,))],
    )
    col = lax.axis_index("col")
    row = lax.axis_index("row")
    if fast:
        ownx = lax.ppermute(pack, "row", CORE_SWAP)
        one = lax.ppermute(pack, BOTH, FETCH_ONE)
        two = lax.ppermute(pack, BOTH, FETCH_TWO)
        own = pack
    else:
        whole = lax.all_gather(pack, "row", axis=0, tiled=True)
        mine = lax.dynamic_slice_in_dim(whole, col * keys, keys, 0)
        quarter = keys // 4
        blocks = tuple(mine[quarter * n : quarter * (n + 1)] for n in (0, 1, 2, 3, 0, 0))
        own = pack

    def col_other(x):
        if col_total == 2:
            return lax.ppermute(x, "col", COL_SWAP)
        return lax.psum(x, "col") - x

    def reduce(mine_a, mine_b, theirs, soon, late, first_beside, beside):
        if fast:
            got = lax.ppermute(theirs, "row", CORE_SWAP)
            if soon:
                query, *rest = late(())
                got, query = lax.optimization_barrier((got, query))
            else:
                got, first_beside = lax.optimization_barrier((got, first_beside))
                query, *rest = late(got)
            query_other = lax.ppermute(query, "col", COL_SWAP)
            count = mine_a.shape[0]
            half = lax.ppermute(mine_b + got[count:], "row", Z_SWAP)
            half, beside, query = lax.optimization_barrier((half, beside, query))
            part = mine_a + got[:count] + half
            sent = [lax.ppermute(part, BOTH, SEND_ONE), lax.ppermute(part, BOTH, SEND_TWO)]
            return [query, query_other, part] + sent, rest, (first_beside, beside)
        query, *rest = late(())
        count = mine_a.shape[0]
        parts = jnp.concatenate([mine_a, theirs[:count], mine_b, theirs[count:]], axis=0)
        summed = lax.all_gather(lax.psum(parts, "row"), "col", axis=0, tiled=True)
        back = lax.dynamic_slice_in_dim(summed, row * count, count, 0)
        zero = jnp.zeros_like(query)
        return [lax.psum(query, "col"), zero, back, zero, zero], rest, (first_beside, beside)

    probs = saved_probs.reshape(2, H * rows, keys)
    hr = H * rows
    loads = (
        cotangent, w_out, pair, w_query.T, w_key.T, w_value.T, w_query_points.T, w_key_points.T, w_value_points.T,
        head_weights[None],
    )
    wk, wq, gp1, q1, q0, pu1, d1, sc = call(
        prep_body, "prep", [VMEM] + [HBM] * 10,
        [((1280, C), BF16), ((LANES, C), BF16), ((rows, 768), F32), ((rows, 1024), F32), ((rows, 1024), F32),
         ((hr, CZ), F32), ((hr, keys), F32), ((8, 128), F32)],
        (own, *in_hbm(*loads)),
        [pltpu.VMEM(x.shape, x.dtype) for x in loads] + [pltpu.SemaphoreType.DMA((len(loads),))],
    )
    if fast:
        one, two, wk, wq, gp1, q1, q0, pu1, d1, sc = lax.optimization_barrier(
            (one, two, wk, wq, gp1, q1, q0, pu1, d1, sc)
        )
        blocks = (pack, ownx, one, lax.ppermute(one, "row", CORE_SWAP), two, lax.ppermute(two, "row", CORE_SWAP))
    key_pack, kv1, pm, e1 = call(
        functools.partial(first_body, fast), "first", [VMEM] * 11,
        [((keys, PACK), F32), ((keys, 2048), F32), ((2, hr, keys), BF16), ((rows, 384), F32)],
        (*blocks, wk, links, probs, gp1, d1),
    )
    e1_other = col_other(e1)
    kv0, e0, tail = call(
        second_body, "second", [VMEM] * 4,
        [((keys, 2048), F32), ((rows, 640 + EARLY * CZ), F32), ((rows, (H - EARLY) * CZ), F32)],
        (key_pack, wk, pm, pair),
        [pltpu.VMEM((hr, keys), F32), pltpu.VMEM((hr, CZ), F32)],
    )
    e0_other = col_other(e0)
    tail_other = col_other(tail)
    share = 1.0 / col_total
    e1_other, e0 = lax.optimization_barrier((e1_other, e0))
    z1, mine_a, mine_b, theirs, pts, grads = call(
        functools.partial(back_one_body, fast), "back_one", [VMEM] * 11,
        [((2 * hr, keys), F32), ((rows, C), F32), ((rows, C), F32), ((2 * rows, C), F32), ((rows, 1152), F32),
         ((keys, 768), F32)],
        (e1, e1_other, pm, kv1, key_pack, own, q1, gp1, d1, wk, sc),
        [pltpu.VMEM((keys, C), F32)],
        6.0,
    )
    pieces, (frq, frk), (e0_other, tail_other) = reduce(
        mine_a, mine_b, theirs, False,
        lambda after: call(
            functools.partial(query_one_body, share), "query_one", [VMEM] * 8,
            [((rows, C), F32), ((rows, 128), F32), ((keys, 128), F32)],
            (z1, kv1, own, q1, lax.optimization_barrier((pts, after))[0], grads, wq, sc),
            (),
            0.01,
        ),
        e0_other,
        tail_other,
    )
    long = 3 * rows + 8
    z0, mine_a, mine_b, theirs, pts, single_one, pu0 = call(
        functools.partial(back_zero_body, fast), "back_zero", [VMEM] * 20,
        [((2 * hr, keys), F32), ((long, 128), F32), ((long, 128), F32), ((2 * long, 128), F32), ((rows, 1152), F32),
         ((rows, C), F32), ((hr, CZ), F32)],
        (cotangent, *pieces, e0, e0_other, tail, tail_other, pm, kv0, key_pack, own, q0, pair, w_out, wk, sc, frk),
        [pltpu.VMEM((keys, C), F32), pltpu.VMEM((4 * long, 128), F32), pltpu.VMEM((rows, 768), F32), pltpu.VMEM((hr, keys), F32)],
    )
    (d_pair,) = call(
        pair_body, "pair_grad", [VMEM] * 5, [((rows, keys, CZ), BF16)], (z1, z0, pu1, pu0, w_bias.T)
    )
    pieces, _, (_, d_pair) = reduce(
        mine_a, mine_b, theirs, True,
        lambda after: call(
            functools.partial(query_zero_body, share), "query_zero", [VMEM] * 8, [((long, 128), F32)],
            (z0, kv0, own, q0, pts, wq, sc, frq),
        ),
        (),
        d_pair,
    )
    d_single, d_frames = call(
        functools.partial(final_body, fast), "final", [VMEM] * 6, [((rows, C), F32), ((12, 2, rows), F32)],
        (*pieces, single_one),
    )
    return (d_single, d_frames.transpose(1, 0, 2), d_pair)


def solution(mesh):
    return jax.shard_map(
        local,
        mesh=mesh,
        in_specs=(
            P(None, ("grp", "row"), None),
            P(None, None, ("grp", "row")),
            P(None, None, ("grp", "row"), "col"),
            P(("grp", "row"), "col", None),
            P(("grp", "row"), None),
            P(("grp", "row")),
            P("grp", None),
            P(),
            P(),
            P(),
            P(),
            P(),
            P(),
            P(),
            P(),
            P(),
        ),
        out_specs=(
            P(("grp", "row"), None),
            P(None, None, ("grp", "row")),
            P(("grp", "row"), "col", None),
        ),
        check_vma=False,
    )
```

```python
import functools
import math

import jax
import jax.numpy as jnp
from jax import lax
from jax.experimental import pallas as pl
from jax.experimental.pallas import tpu as pltpu
from jax.sharding import PartitionSpec as P

C = 384
H = 12
HD = 16
CZ = 128
PQ = 4
PV = 8
NCHAIN = 16
NORM_EPS = 1e-08
LOGIT_SCALE = math.sqrt(1.0 / 3.0)
PLAIN_SCALE = 1.0 / math.sqrt(HD)
POINT_SCALE = math.sqrt(2.0 / (9.0 * PQ))

LANES = 640
PACK = 896
FRAME_LANE = 768
CHAIN_LANE = 792
STAT = 96
EARLY = 4

F32 = jnp.float32
BF16 = jnp.bfloat16
NN = (((1,), (0,)), ((), ()))
NT = (((1,), (1,)), ((), ()))
TN = (((0,), (0,)), ((), ()))


def mm(a, b, dims=NN):
    return lax.dot_general(a, b, dims, preferred_element_type=F32)


def split(x):
    hi = x.astype(BF16)
    return hi, (x - hi.astype(F32)).astype(BF16)


def mm2(x, w, dims=NN):
    hi, lo = split(x)
    rows = x.shape[0]
    both = mm(jnp.concatenate([hi, lo], axis=0), w, dims)
    return both[:rows] + both[rows:]


def mm3(ah, al, bh, bl, dims=NN):
    return mm(ah, bh, dims) + mm(ah, bl, dims) + mm(al, bh, dims)


def iota(shape, axis):
    return lax.broadcasted_iota(jnp.int32, shape, axis)


def key_heads(rows):
    lane = iota((rows, LANES), 1)
    return jnp.where(lane < 256, lane >> 4, (lane & 127) >> 2)


def value_heads(rows):
    lane = iota((rows, LANES), 1)
    inner = lane & 127
    points = jnp.where(inner < STAT, inner >> 3, inner - STAT)
    return jnp.where(lane < 256, lane >> 4, points)


def pick(full, heads, rows):
    out = None
    for h in range(H):
        part = jnp.where(heads == h, full[h * rows : (h + 1) * rows], 0.0)
        out = part if out is None else out + part
    return out


def spread(x, heads):
    return jnp.concatenate([jnp.where(heads == h, x, 0.0) for h in range(H)], axis=0)


def spread2(x, heads):
    hi, lo = split(x)
    hi32, lo32 = hi.astype(F32), lo.astype(F32)
    return spread(hi32, heads).astype(BF16), spread(lo32, heads).astype(BF16)


def columns(frames_block, first):
    cols = [frames_block[:, first + n : first + n + 1] for n in range(12)]
    return [[cols[3 * a + b] for b in range(3)] for a in range(3)], cols[9:]


def block(x, a):
    return x[:, 256 + 128 * a : 384 + 128 * a]


def rotate(rot, pts):
    return [sum(rot[a][b] * pts[b] for b in range(3)) for a in range(3)]


def unrotate(rot, pts):
    return [sum(rot[a][b] * pts[a] for a in range(3)) for b in range(3)]


def place(rot, shift, flat):
    local_pts = [block(flat, a) for a in range(3)]
    turned = rotate(rot, local_pts)
    return jnp.concatenate(
        [flat[:, :256]] + [turned[a] + shift[a] for a in range(3)], axis=1
    )


def lane_matrix(rows, fn):
    r = iota((rows, 128), 0)
    c = iota((rows, 128), 1)
    return (fn(r) == c).astype(F32).astype(BF16)


def upstream_parts(g, w_out_ref, gp_ref, pu_ref, rows):
    hi, lo = split(g)
    both = jnp.concatenate([hi, lo], axis=0)

    def part(first, count):
        r = mm(both, w_out_ref[first : first + count, :], NT)
        return r[:rows] + r[rows:]

    gp_ref[...] = jnp.zeros(gp_ref.shape, F32)
    gp_ref[:, 0:192] = part(0, 192)
    for a in range(4):
        gp_ref[:, 256 + 128 * a : 352 + 128 * a] = part(192 + 96 * a, 96)
    wide = part(576, H * CZ)
    for h in range(H):
        pu_ref[h * rows : (h + 1) * rows, :] = (
            wide[:, h * CZ : (h + 1) * CZ].astype(BF16).astype(F32)
        )


def pair_products(pu_ref, pair_ref, d_ref, rows):
    for i in range(0, rows, 2):
        lhs = jnp.concatenate([pu_ref[pl.ds(i, H, stride=rows), :], pu_ref[pl.ds(i + 1, H, stride=rows), :]], axis=0)
        both = mm(lhs.astype(BF16), pair_ref[i : i + 2].reshape(-1, CZ), NT)
        keys = both.shape[1] // 2
        d_ref[pl.ds(i, H, stride=rows), :] = both[:H, :keys]
        d_ref[pl.ds(i + 1, H, stride=rows), :] = both[H:, keys:]


def split3(x):
    hi, _ = split(x)
    rest = x - hi.astype(F32)
    mid, lo = split(rest)
    return hi, mid, lo


def pack_body(single_hbm, frames_hbm, chains_hbm, pack_ref, frames_ref, chains_ref, sems):
    rows = pack_ref.shape[0]
    ends = (
        (frames_hbm, frames_ref), (chains_hbm, chains_ref), (single_hbm.at[1], pack_ref.at[:, 0:C]),
        (single_hbm.at[0], pack_ref.at[:, C : 2 * C]),
    )
    copies = [pltpu.make_async_copy(src, dst, sems.at[n]) for n, (src, dst) in enumerate(ends)]
    for copy in copies:
        copy.start()
    copies[0].wait()
    copies[1].wait()
    out = jnp.zeros((rows, 128), F32)
    for slot, l in ((0, 1), (12, 0)):
        hot = (iota((12, 128), 1) == iota((12, 128), 0) + slot).astype(F32).astype(BF16)
        for part in split3(frames_ref[:, l, :]):
            out = out + mm(part, hot, TN)
    hot = (iota((1, 128), 1) == CHAIN_LANE - FRAME_LANE).astype(F32).astype(BF16)
    pack_ref[:, 2 * C :] = out + mm(chains_ref[...].astype(F32).astype(BF16), hot, TN)
    copies[2].wait()
    copies[3].wait()


def prep_body(
    pack_ref, cot_hbm, w_out_hbm, pair_hbm, wq_hbm, wk_hbm, wv_hbm, wqp_hbm, wkp_hbm, wvp_hbm, hw_hbm,
    wk_out, wq_out, gp_ref, q1_ref, q0_ref, pu_ref, d_ref, sc_ref,
    cot_ref, w_out_ref, pair_ref, wq_ref, wk_ref, wv_ref, wqp_ref, wkp_ref, wvp_ref, hw_ref, sems,
):
    rows = pack_ref.shape[0]
    ends = (
        (cot_hbm, cot_ref), (w_out_hbm, w_out_ref), (pair_hbm, pair_ref), (wq_hbm, wq_ref), (wk_hbm, wk_ref),
        (wv_hbm, wv_ref), (wqp_hbm, wqp_ref), (wkp_hbm, wkp_ref), (wvp_hbm, wvp_ref), (hw_hbm, hw_ref),
    )
    copies = [pltpu.make_async_copy(src, dst, sems.at[n]) for n, (src, dst) in enumerate(ends)]
    for copy in copies:
        copy.start()
    copies[0].wait()
    copies[1].wait()
    upstream_parts(cot_ref[...], w_out_ref, gp_ref, pu_ref, rows)
    copies[2].wait()
    pair_products(pu_ref, pair_ref, d_ref, rows)
    for copy in copies[3:]:
        copy.wait()
    wq_out[...] = jnp.zeros(wq_out.shape, BF16)
    wk_out[...] = jnp.zeros(wk_out.shape, BF16)
    wq_out[0:192, :] = wq_ref[...]
    wk_out[0:192, :] = wk_ref[...]
    wk_out[640:832, :] = wv_ref[...]
    for a in range(3):
        wq_out[256 + 128 * a : 304 + 128 * a, :] = wqp_ref[48 * a : 48 * a + 48, :]
        wk_out[256 + 128 * a : 304 + 128 * a, :] = wkp_ref[48 * a : 48 * a + 48, :]
        wk_out[896 + 128 * a : 992 + 128 * a, :] = wvp_ref[96 * a : 96 * a + 96, :]
    lane = iota((8, 128), 1)
    raw = jnp.zeros((8, 128), F32)
    for h in range(H):
        raw = jnp.where((lane >> 2) == h, hw_ref[:, h : h + 1], raw)
    soft = jnp.maximum(raw, 0.0) + jnp.log(1.0 + jnp.exp(-jnp.abs(raw)))
    sc_ref[...] = soft * POINT_SCALE
    fr = pack_ref[:, FRAME_LANE : FRAME_LANE + 128]
    for out, first, fcol in ((q1_ref, 0, 0), (q0_ref, C, 12)):
        flat = mm2(pack_ref[:, first : first + C], wq_out[...], NT)
        rot, shift = columns(fr, fcol)
        out[:, :LANES] = place(rot, shift, flat)
        out[:, LANES:] = flat[:, 256:]


def project_keys(x, fr, fcol, wk_ref, kv_ref):
    flat = mm2(x, wk_ref[...], NT)
    rot, shift = columns(fr, fcol)
    kv_ref[:, 0:640] = place(rot, shift, flat[:, :640])
    kv_ref[:, 640:1280] = place(rot, shift, flat[:, 640:])
    kv_ref[:, 1280:1664] = flat[:, 256:640]
    kv_ref[:, 1664:2048] = flat[:, 896:1280]


def value_sums(probs, kv_ref, rows):
    values = kv_ref[:, 640:1280]
    lane = iota(values.shape, 1)
    values = jnp.where((lane >= 256 + STAT) & (lane < 256 + STAT + H), 1.0, values)
    hi, lo = split(values)
    return pick(mm(probs, hi) + mm(probs, lo), value_heads(rows), rows)


def head_dots(prod, rows):
    return mm2(prod, lane_matrix(256, lambda r: STAT + (r >> 4)))


def first_body(
    fast, self_ref, own_ref, ownx_ref, p1_ref, p1x_ref, p2_ref, p2x_ref, wk_ref, links_ref, probs_ref, gp_ref, d_ref,
    keys_ref, kv_ref, pm_ref, e_ref,
):
    rows = own_ref.shape[0]
    home, zb, core = position(fast)

    def put(z, k, value):
        keys_ref[pl.ds(pl.multiple_of(jnp.int32((2 * z + k) * rows), rows), rows), :] = value

    put(zb, core, jnp.where(home, own_ref[...], p1_ref[...]))
    put(zb, 1 - core, jnp.where(home, ownx_ref[...], p1x_ref[...]))
    put(1 - zb, core, jnp.where(home, p1_ref[...], p2_ref[...]))
    put(1 - zb, 1 - core, jnp.where(home, p1x_ref[...], p2x_ref[...]))
    fr = keys_ref[:, FRAME_LANE : FRAME_LANE + 128]
    keys = fr.shape[0]
    at = CHAIN_LANE - FRAME_LANE
    key_chain = fr[:, at : at + 1]
    own_chain = self_ref[:, FRAME_LANE : FRAME_LANE + 128][:, at : at + 1]
    key_hot = (iota((keys, NCHAIN), 1).astype(F32) == key_chain).astype(F32).astype(BF16)
    own_hot = (iota((rows, NCHAIN), 1).astype(F32) == own_chain).astype(F32).astype(BF16)
    eye = iota((NCHAIN, NCHAIN), 0) == iota((NCHAIN, NCHAIN), 1)
    allowed = jnp.where(eye, 1.0, links_ref[...].astype(F32)).astype(BF16)
    mask = mm(mm(own_hot, allowed).astype(BF16), key_hot, NT)
    mask_all = jnp.concatenate([mask] * H, axis=0)
    for l in range(2):
        pm_ref[l] = (probs_ref[l].astype(F32) * mask_all).astype(BF16)
    project_keys(keys_ref[:, 0:C], fr, 0, wk_ref, kv_ref)
    probs = pm_ref[1]
    sums = value_sums(probs, kv_ref, rows)
    weighted = mm2(probs.astype(F32) * d_ref[...], jnp.ones((keys, 128), BF16))
    lane = iota((rows, 128), 1)
    dots = pick(weighted, lane - STAT, rows) + head_dots(gp_ref[:, 0:256] * sums[:, 0:256], rows)
    e_ref[:, 0:128] = block(sums, 0)
    e_ref[:, 128:256] = jnp.where(lane < STAT, block(sums, 1), dots)
    e_ref[:, 256:384] = block(sums, 2)


def second_body(keys_ref, wk_ref, pm_ref, pair_ref, kv_ref, e_ref, tail_ref, p32_ref, op_ref):
    rows = pair_ref.shape[0]
    fr = keys_ref[:, FRAME_LANE : FRAME_LANE + 128]
    project_keys(keys_ref[:, C : 2 * C], fr, 12, wk_ref, kv_ref)
    probs = pm_ref[0]
    sums = value_sums(probs, kv_ref, rows)
    for a in range(3):
        e_ref[:, 128 * a : 128 * a + 128] = block(sums, a)
    e_ref[:, 384:640] = sums[:, 0:256]
    p32_ref[...] = probs.astype(F32)
    for i in range(rows):
        lhs = p32_ref[pl.ds(i, H, stride=rows), :].astype(BF16)
        op_ref[pl.ds(i, H, stride=rows), :] = mm(lhs, pair_ref[i])
    for h in range(H):
        ref, first = (e_ref, 640 + CZ * h) if h < EARLY else (tail_ref, CZ * (h - EARLY))
        ref[:, first : first + CZ] = op_ref[h * rows : (h + 1) * rows, :]


def backward(
    e, dots, probs, kv_ref, key_fr, own_fr, fcol, q_ref, gp, d_ref, wk_ref, sc,
    z_ref, keys_out_ref,
):
    rows = e.shape[0]
    lane = iota((rows, 128), 1)
    stat = (lane >= STAT) & (lane < STAT + H)
    inv = jnp.where(stat, 1.0 / jnp.where(stat, e[:, 0:128], 1.0), 0.0)
    r128 = iota((128, LANES), 0)
    grow = (r128 - STAT == value_heads(128)) & ((iota((128, LANES), 1) & 127) < STAT)
    grow = grow | ((r128 - STAT == (iota((128, LANES), 1) >> 4)) & (iota((128, LANES), 1) < 256))
    inv_lanes = mm2(inv, grow.astype(F32).astype(BF16))
    rot, shift = columns(own_fr, fcol)
    inv_pts = block(inv_lanes, 0)
    ptg = [e[:, 128 * a : 128 * a + 128] * inv_pts for a in range(3)]
    off = [jnp.where(lane < STAT, ptg[a] - shift[a], 0.0) for a in range(3)]
    opt = unrotate(rot, off)
    length = jnp.sqrt(opt[0] * opt[0] + opt[1] * opt[1] + opt[2] * opt[2] + NORM_EPS)
    scale = gp[:, 640:768] / length
    gpt = [block(gp, a) + scale * opt[a] for a in range(3)]
    gptg = rotate(rot, gpt)
    upper = jnp.concatenate([gp[:, 0:256]] + gptg, axis=1)
    point_dots = gptg[0] * ptg[0] + gptg[1] * ptg[1] + gptg[2] * ptg[2]
    rd = dots * inv + mm2(point_dots, lane_matrix(128, lambda r: STAT + (r >> 3)))
    both = jnp.concatenate([spread(rd, lane - STAT), spread(inv, lane - STAT)], axis=0)
    wide = mm2(both, jnp.ones((128, 128), BF16))
    rd_all, inv_all = wide[: H * rows], wide[H * rows :]
    heads_v = value_heads(rows)
    heads_k = key_heads(rows)
    uh, ul = spread2(upper, heads_v)
    vh, vl = split(kv_ref[:, 640:1280])
    d_att = d_ref[...] + mm3(uh, ul, vh, vl, NT)
    p32 = probs.astype(F32)
    att = p32 * inv_all
    dl = LOGIT_SCALE * att * (d_att - rd_all)
    z_ref[0 : H * rows, :] = att
    z_ref[H * rows :, :] = dl
    dt = jnp.transpose(dl)
    th, tl = split(dt)
    qh, qlo = spread2(q_ref[:, 0:640], heads_k)
    kr = mm3(th, tl, qh, qlo)
    head_rows = iota((H * rows, 128), 0) // rows
    hot = ((iota((H * rows, 128), 1) >> 2) == head_rows).astype(F32).astype(BF16)
    cs = mm(th, hot) + mm(tl, hot)
    pt = jnp.transpose(p32).astype(BF16)
    sh, sl = spread2(upper * inv_lanes, heads_v)
    vr = mm(pt, sh) + mm(pt, sl)
    krot, _ = columns(key_fr, fcol)
    d_kg = [sc * (block(kr, a) - cs * kv_ref[:, 256 + 128 * a : 384 + 128 * a]) for a in range(3)]
    d_vg = [block(vr, a) for a in range(3)]
    d_kl = unrotate(krot, d_kg)
    d_vl = unrotate(krot, d_vg)
    flat = jnp.concatenate([PLAIN_SCALE * kr[:, 0:256]] + d_kl + [vr[:, 0:256]] + d_vl, axis=1)
    keys_out_ref[:, 0:C] = mm2(flat, wk_ref[...])
    return jnp.concatenate(off + gpt + gptg, axis=1), jnp.concatenate(d_kg + d_vg, axis=1)


def frame_sums(prods, first):
    def lane(r):
        q = first + (r >> 7)
        return q + 2 * ((q * 43) >> 8)

    return mm2(jnp.concatenate(prods, axis=1), lane_matrix(12 * 128, lane))


def frame_block(turned, at, rows):
    return jnp.concatenate([turned[8 * m : 8 * m + 8, at : at + rows] for m in range(4)], axis=1)


def store_piece(ref, at, grad, frames):
    rows = grad.shape[0]
    for t in range(3):
        ref[at + rows * t : at + rows * (t + 1), :] = grad[:, 128 * t : 128 * t + 128]
    ref[at + 3 * rows : at + 3 * rows + 8, :] = frames


def backward_frames(grads, kv_ref, first):
    d_kg = [grads[:, 128 * a : 128 * a + 128] for a in range(3)]
    d_vg = [grads[:, 384 + 128 * a : 512 + 128 * a] for a in range(3)]
    k_local = [kv_ref[:, 1280 + 128 * b : 1408 + 128 * b] for b in range(3)]
    v_local = [kv_ref[:, 1664 + 128 * b : 1792 + 128 * b] for b in range(3)]
    prods = [d_kg[a] * k_local[b] + d_vg[a] * v_local[b] for a in range(3) for b in range(3)]
    return frame_sums(prods + [d_kg[a] + d_vg[a] for a in range(3)], first)


def backward_query(dl, kv_ref, own_fr, fcol, q_ref, pts_ref, wq_ref, sc, first_lane, share):
    rows = own_fr.shape[0]
    dh, dlo = split(dl)
    kh, klo = split(kv_ref[:, 0:640])
    qr = pick(mm3(dh, dlo, kh, klo), key_heads(rows), rows)
    rot, _ = columns(own_fr, fcol)
    d_qg = [sc * block(qr, a) for a in range(3)]
    d_ql = unrotate(rot, d_qg)
    grad = mm2(jnp.concatenate([PLAIN_SCALE * qr[:, 0:256]] + d_ql, axis=1), wq_ref[...])
    q_local = [q_ref[:, 640 + 128 * b : 768 + 128 * b] for b in range(3)]
    off, gpt, gptg = [
        [pts_ref[:, 384 * n + 128 * a : 384 * n + 128 * a + 128] for a in range(3)] for n in range(3)
    ]
    prods = [d_qg[a] * q_local[b] + share * off[a] * gpt[b] for a in range(3) for b in range(3)]
    prods = prods + [d_qg[a] - share * gptg[a] for a in range(3)]
    return grad, frame_sums(prods, first_lane)


def position(fast):
    if not fast:
        return True, 0, 0
    row = lax.axis_index("row")
    return row // 4 == lax.axis_index("col"), (row // 2) % 2, row % 2


def send_blocks(fast, src_ref, mine_a, mine_b, theirs, rows):
    _, zb, core = position(fast)

    def get(z, k):
        return src_ref[pl.ds(pl.multiple_of(jnp.int32((2 * z + k) * rows), 8), rows), :]

    mine_a[...] = get(zb, core)
    mine_b[...] = get(1 - zb, core)
    theirs[0:rows, :] = get(zb, 1 - core)
    theirs[rows:, :] = get(1 - zb, 1 - core)


def add_pieces(fast, query, query_other, part, one, two):
    return (query[...] + query_other[...]) + (one[...] + jnp.where(position(fast)[0], part[...], two[...]))


def final_body(fast, r0, r1, r2, r3, r4, one_ref, single_out, frames_out):
    total = add_pieces(fast, r0, r1, r2, r3, r4)
    rows = one_ref.shape[0]
    for t in range(3):
        lanes = slice(128 * t, 128 * t + 128)
        single_out[:, lanes] = one_ref[:, lanes] + total[rows * t : rows * (t + 1), :]
    for m in range(4):
        first = 6 * (m % 2)
        frames_out[first : first + 6, m // 2, :] = total[3 * rows : 3 * rows + 6, rows * m : rows * (m + 1)]


def frame_part(ref):
    return ref[:, FRAME_LANE : FRAME_LANE + 128]


def back_one_body(
    fast, e_mine, e_other, pm_ref, kv_ref, keys_ref, own_ref, q_ref, gp_ref, d_ref, wk_ref, sc_ref,
    z_ref, mine_a, mine_b, theirs, pts_ref, grads_ref, work_ref,
):
    e = e_mine[...] + e_other[...]
    pts_ref[...], grads_ref[...] = backward(
        e, e[:, 128:256], pm_ref[1], kv_ref, frame_part(keys_ref), frame_part(own_ref), 0, q_ref,
        gp_ref[...], d_ref, wk_ref, sc_ref[0:1, :], z_ref, work_ref,
    )
    send_blocks(fast, work_ref, mine_a, mine_b, theirs, own_ref.shape[0])


def query_one_body(
    share, z_ref, kv_ref, own_ref, q_ref, pts_ref, grads_ref, wq_ref, sc_ref, query_out, frq_ref, frk_ref
):
    half = z_ref.shape[0] // 2
    query_out[...], frq_ref[...] = backward_query(
        z_ref[half:, :], kv_ref, frame_part(own_ref), 0, q_ref, pts_ref, wq_ref, sc_ref[0:1, :], 12, share
    )
    frk_ref[...] = backward_frames(grads_ref[...], kv_ref, 12)


def back_zero_body(
    fast, cot_ref, r0, r1, r2, r3, r4, e_mine, e_other, tail_mine, tail_other, pm_ref, kv_ref, keys_ref, own_ref, q_ref, pair_ref,
    w_out_ref, wk_ref, sc_ref, frk_ref,
    z_ref, mine_a, mine_b, theirs, pts_ref, sum_ref, pu_ref, work_ref, pieces_ref, gp_ref, d_ref,
):
    rows = own_ref.shape[0]
    total = add_pieces(fast, r0, r1, r2, r3, r4)
    sum_ref[...] = total
    upstream_parts(cot_ref[...] + total, w_out_ref, gp_ref, pu_ref, rows)
    pair_products(pu_ref, pair_ref, d_ref, rows)
    gp = gp_ref[...]
    e = e_mine[:, 0:384] + e_other[:, 0:384]
    plain = e_mine[:, 384:640] + e_other[:, 384:640]
    dots = head_dots(gp[:, 0:256] * plain, rows)
    wide = jnp.concatenate(
        [
            pu_ref[h * rows : (h + 1) * rows, :]
            * (
                e_mine[:, 640 + CZ * h : 640 + CZ * (h + 1)] + e_other[:, 640 + CZ * h : 640 + CZ * (h + 1)]
                if h < EARLY
                else tail_mine[:, CZ * (h - EARLY) : CZ * (h - EARLY + 1)]
                + tail_other[:, CZ * (h - EARLY) : CZ * (h - EARLY + 1)]
            )
            for h in range(H)
        ],
        axis=1,
    )
    dots = dots + mm2(wide, lane_matrix(H * CZ, lambda r: STAT + (r >> 7)))
    pts_ref[...], grads = backward(
        e, dots, pm_ref[0], kv_ref, frame_part(keys_ref), frame_part(own_ref), 12, q_ref, gp, d_ref, wk_ref,
        sc_ref[0:1, :], z_ref, work_ref,
    )
    turned = jnp.transpose(backward_frames(grads, kv_ref, 0) + frk_ref[...])
    for n in range(4):
        at = n * pieces_ref.shape[0] // 4
        store_piece(pieces_ref, at, work_ref[rows * n : rows * (n + 1), :], frame_block(turned, rows * n, rows))
    send_blocks(fast, pieces_ref, mine_a, mine_b, theirs, mine_a.shape[0])


def query_zero_body(share, z_ref, kv_ref, own_ref, q_ref, pts_ref, wq_ref, sc_ref, frq_ref, query_out):
    half = z_ref.shape[0] // 2
    grad, frames = backward_query(
        z_ref[half:, :], kv_ref, frame_part(own_ref), 12, q_ref, pts_ref, wq_ref, sc_ref[0:1, :], 0, share
    )
    store_piece(query_out, 0, grad, frame_block(jnp.transpose(frames + frq_ref[...]), 0, own_ref.shape[0]))


def pair_body(z1_ref, z0_ref, pu1_ref, pu0_ref, wbt_ref, out_ref):
    rows = out_ref.shape[0]
    wbt = wbt_ref[...].astype(F32)
    for i in range(rows):
        left = jnp.concatenate(
            [z1_ref[pl.ds(i, 2 * H, stride=rows), :], z0_ref[pl.ds(i, 2 * H, stride=rows), :]], axis=0
        )
        right = jnp.concatenate(
            [pu1_ref[pl.ds(i, H, stride=rows), :], wbt, pu0_ref[pl.ds(i, H, stride=rows), :], wbt], axis=0
        ).astype(BF16)
        out_ref[i] = mm(left.astype(BF16), right, TN).astype(BF16)


VMEM = pl.BlockSpec(memory_space=pltpu.VMEM)
HBM = pl.BlockSpec(memory_space=pltpu.HBM)


def call(body, name, in_specs, outs, args, scratch=(), micros=1.0):
    return pl.pallas_call(
        body,
        name=name,
        in_specs=in_specs,
        out_specs=tuple(VMEM for _ in outs),
        out_shape=tuple(jax.ShapeDtypeStruct(s, d) for s, d in outs),
        scratch_shapes=list(scratch),
        compiler_params=pltpu.CompilerParams(vmem_limit_bytes=16 * 1024 * 1024),
        cost_estimate=pl.CostEstimate(flops=int(micros * 1e9), transcendentals=0, bytes_accessed=int(micros * 3e6)),
    )(*args)


def in_hbm(*arrays):
    return tuple(pltpu.with_memory_space_constraint(x, pltpu.HBM) for x in arrays)


def joint(pairs):
    return [
        ((a * 2 + k) * 2 + x, (b * 2 + k) * 2 + y) for (x, a), (y, b) in pairs for k in range(2)
    ]


BOTH = ("row", "col")
FETCH_ONE = joint([((0, 0), (0, 1)), ((0, 1), (0, 0)), ((1, 0), (0, 2)), ((1, 1), (0, 3)), ((1, 2), (1, 3)), ((1, 3), (1, 2)), ((0, 2), (1, 0)), ((0, 3), (1, 1))])
FETCH_TWO = joint([((0, 0), (0, 3)), ((0, 1), (0, 2)), ((1, 2), (1, 1)), ((1, 3), (1, 0)), ((1, 0), (0, 0)), ((1, 1), (0, 1)), ((0, 2), (1, 2)), ((0, 3), (1, 3))])
SEND_ONE = joint([((0, 0), (1, 0)), ((0, 1), (1, 1)), ((0, 2), (0, 0)), ((0, 3), (0, 1)), ((1, 2), (0, 2)), ((1, 3), (0, 3)), ((1, 0), (1, 2)), ((1, 1), (1, 3))])
SEND_TWO = joint([((0, 2), (1, 0)), ((0, 3), (1, 1)), ((1, 0), (0, 2)), ((1, 1), (0, 3)), ((0, 0), (0, 1)), ((0, 1), (0, 0)), ((1, 2), (1, 3)), ((1, 3), (1, 2))])
CORE_SWAP = [(i, i ^ 1) for i in range(8)]
Z_SWAP = [(i, i ^ 2) for i in range(8)]
COL_SWAP = [(0, 1), (1, 0)]


def local(
    single, frames, saved_probs, pair, cotangent, chains, links, w_query, w_key, w_value, w_query_points,
    w_key_points, w_value_points, w_bias, w_out, head_weights,
):
    rows = single.shape[1]
    keys = pair.shape[1]
    row_total = lax.axis_size("row")
    col_total = lax.axis_size("col")
    fast = row_total == 8 and col_total == 2 and keys == 4 * rows
    (pack,) = call(
        pack_body, "pack", [HBM] * 3, [((rows, PACK), F32)], in_hbm(single, frames.transpose(1, 0, 2), chains[None]),
        [pltpu.VMEM((12, 2, rows), F32), pltpu.VMEM((1, rows), jnp.int32), pltpu.SemaphoreType.DMA((4,))],
    )
    col = lax.axis_index("col")
    row = lax.axis_index("row")
    if fast:
        ownx = lax.ppermute(pack, "row", CORE_SWAP)
        one = lax.ppermute(pack, BOTH, FETCH_ONE)
        two = lax.ppermute(pack, BOTH, FETCH_TWO)
        own = pack
    else:
        whole = lax.all_gather(pack, "row", axis=0, tiled=True)
        mine = lax.dynamic_slice_in_dim(whole, col * keys, keys, 0)
        quarter = keys // 4
        blocks = tuple(mine[quarter * n : quarter * (n + 1)] for n in (0, 1, 2, 3, 0, 0))
        own = pack

    def col_other(x):
        if col_total == 2:
            return lax.ppermute(x, "col", COL_SWAP)
        return lax.psum(x, "col") - x

    def reduce(mine_a, mine_b, theirs, soon, late, first_beside, beside):
        if fast:
            got = lax.ppermute(theirs, "row", CORE_SWAP)
            if soon:
                query, *rest = late(())
                got, query = lax.optimization_barrier((got, query))
            else:
                got, first_beside = lax.optimization_barrier((got, first_beside))
                query, *rest = late(got)
            query_other = lax.ppermute(query, "col", COL_SWAP)
            count = mine_a.shape[0]
            half = lax.ppermute(mine_b + got[count:], "row", Z_SWAP)
            half, beside, query = lax.optimization_barrier((half, beside, query))
            part = mine_a + got[:count] + half
            sent = [lax.ppermute(part, BOTH, SEND_ONE), lax.ppermute(part, BOTH, SEND_TWO)]
            return [query, query_other, part] + sent, rest, (first_beside, beside)
        query, *rest = late(())
        count = mine_a.shape[0]
        parts = jnp.concatenate([mine_a, theirs[:count], mine_b, theirs[count:]], axis=0)
        summed = lax.all_gather(lax.psum(parts, "row"), "col", axis=0, tiled=True)
        back = lax.dynamic_slice_in_dim(summed, row * count, count, 0)
        zero = jnp.zeros_like(query)
        return [lax.psum(query, "col"), zero, back, zero, zero], rest, (first_beside, beside)

    probs = saved_probs.reshape(2, H * rows, keys)
    hr = H * rows
    loads = (
        cotangent, w_out, pair, w_query.T, w_key.T, w_value.T, w_query_points.T, w_key_points.T, w_value_points.T,
        head_weights[None],
    )
    wk, wq, gp1, q1, q0, pu1, d1, sc = call(
        prep_body, "prep", [VMEM] + [HBM] * 10,
        [((1280, C), BF16), ((LANES, C), BF16), ((rows, 768), F32), ((rows, 1024), F32), ((rows, 1024), F32),
         ((hr, CZ), F32), ((hr, keys), F32), ((8, 128), F32)],
        (own, *in_hbm(*loads)),
        [pltpu.VMEM(x.shape, x.dtype) for x in loads] + [pltpu.SemaphoreType.DMA((len(loads),))],
    )
    if fast:
        one, two, wk, wq, gp1, q1, q0, pu1, d1, sc = lax.optimization_barrier(
            (one, two, wk, wq, gp1, q1, q0, pu1, d1, sc)
        )
        blocks = (pack, ownx, one, lax.ppermute(one, "row", CORE_SWAP), two, lax.ppermute(two, "row", CORE_SWAP))
    key_pack, kv1, pm, e1 = call(
        functools.partial(first_body, fast), "first", [VMEM] * 12,
        [((keys, PACK), F32), ((keys, 2048), F32), ((2, hr, keys), BF16), ((rows, 384), F32)],
        (own, *blocks, wk, links, probs, gp1, d1),
    )
    e1_other = col_other(e1)
    kv0, e0, tail = call(
        second_body, "second", [VMEM] * 4,
        [((keys, 2048), F32), ((rows, 640 + EARLY * CZ), F32), ((rows, (H - EARLY) * CZ), F32)],
        (key_pack, wk, pm, pair),
        [pltpu.VMEM((hr, keys), F32), pltpu.VMEM((hr, CZ), F32)],
    )
    e0_other = col_other(e0)
    tail_other = col_other(tail)
    share = 1.0 / col_total
    e1_other, e0 = lax.optimization_barrier((e1_other, e0))
    z1, mine_a, mine_b, theirs, pts, grads = call(
        functools.partial(back_one_body, fast), "back_one", [VMEM] * 11,
        [((2 * hr, keys), F32), ((rows, C), F32), ((rows, C), F32), ((2 * rows, C), F32), ((rows, 1152), F32),
         ((keys, 768), F32)],
        (e1, e1_other, pm, kv1, key_pack, own, q1, gp1, d1, wk, sc),
        [pltpu.VMEM((keys, C), F32)],
        6.0,
    )
    pieces, (frq, frk), (e0_other, tail_other) = reduce(
        mine_a, mine_b, theirs, False,
        lambda after: call(
            functools.partial(query_one_body, share), "query_one", [VMEM] * 8,
            [((rows, C), F32), ((rows, 128), F32), ((keys, 128), F32)],
            (z1, kv1, own, q1, lax.optimization_barrier((pts, after))[0], grads, wq, sc),
            (),
            0.01,
        ),
        e0_other,
        tail_other,
    )
    long = 3 * rows + 8
    z0, mine_a, mine_b, theirs, pts, single_one, pu0 = call(
        functools.partial(back_zero_body, fast), "back_zero", [VMEM] * 20,
        [((2 * hr, keys), F32), ((long, 128), F32), ((long, 128), F32), ((2 * long, 128), F32), ((rows, 1152), F32),
         ((rows, C), F32), ((hr, CZ), F32)],
        (cotangent, *pieces, e0, e0_other, tail, tail_other, pm, kv0, key_pack, own, q0, pair, w_out, wk, sc, frk),
        [pltpu.VMEM((keys, C), F32), pltpu.VMEM((4 * long, 128), F32), pltpu.VMEM((rows, 768), F32), pltpu.VMEM((hr, keys), F32)],
    )
    (d_pair,) = call(
        pair_body, "pair_grad", [VMEM] * 5, [((rows, keys, CZ), BF16)], (z1, z0, pu1, pu0, w_bias.T)
    )
    pieces, _, (_, d_pair) = reduce(
        mine_a, mine_b, theirs, True,
        lambda after: call(
            functools.partial(query_zero_body, share), "query_zero", [VMEM] * 8, [((long, 128), F32)],
            (z0, kv0, own, q0, pts, wq, sc, frq),
        ),
        (),
        d_pair,
    )
    d_single, d_frames = call(
        functools.partial(final_body, fast), "final", [VMEM] * 6, [((rows, C), F32), ((12, 2, rows), F32)],
        (*pieces, single_one),
    )
    return (d_single, d_frames.transpose(1, 0, 2), d_pair)


def solution(mesh):
    return jax.shard_map(
        local,
        mesh=mesh,
        in_specs=(
            P(None, ("grp", "row"), None),
            P(None, None, ("grp", "row")),
            P(None, None, ("grp", "row"), "col"),
            P(("grp", "row"), "col", None),
            P(("grp", "row"), None),
            P(("grp", "row")),
            P("grp", None),
            P(),
            P(),
            P(),
            P(),
            P(),
            P(),
            P(),
            P(),
            P(),
        ),
        out_specs=(
            P(("grp", "row"), None),
            P(None, None, ("grp", "row")),
            P(("grp", "row"), "col", None),
        ),
        check_vma=False,
    )
```

```python
import functools
import math

import jax
import jax.numpy as jnp
from jax import lax
from jax.experimental import pallas as pl
from jax.experimental.pallas import tpu as pltpu
from jax.sharding import PartitionSpec as P

C = 384
H = 12
HD = 16
CZ = 128
PQ = 4
PV = 8
NCHAIN = 16
NORM_EPS = 1e-08
LOGIT_SCALE = math.sqrt(1.0 / 3.0)
PLAIN_SCALE = 1.0 / math.sqrt(HD)
POINT_SCALE = math.sqrt(2.0 / (9.0 * PQ))

LANES = 640
PACK = 896
FRAME_LANE = 768
CHAIN_LANE = 792
STAT = 96
EARLY = 4

F32 = jnp.float32
BF16 = jnp.bfloat16
NN = (((1,), (0,)), ((), ()))
NT = (((1,), (1,)), ((), ()))
TN = (((0,), (0,)), ((), ()))


def mm(a, b, dims=NN):
    return lax.dot_general(a, b, dims, preferred_element_type=F32)


def split(x):
    hi = x.astype(BF16)
    return hi, (x - hi.astype(F32)).astype(BF16)


def mm2(x, w, dims=NN):
    hi, lo = split(x)
    rows = x.shape[0]
    both = mm(jnp.concatenate([hi, lo], axis=0), w, dims)
    return both[:rows] + both[rows:]


def mm3(ah, al, bh, bl, dims=NN):
    return mm(ah, bh, dims) + mm(ah, bl, dims) + mm(al, bh, dims)


def iota(shape, axis):
    return lax.broadcasted_iota(jnp.int32, shape, axis)


def key_heads(rows):
    lane = iota((rows, LANES), 1)
    return jnp.where(lane < 256, lane >> 4, (lane & 127) >> 2)


def value_heads(rows):
    lane = iota((rows, LANES), 1)
    inner = lane & 127
    points = jnp.where(inner < STAT, inner >> 3, inner - STAT)
    return jnp.where(lane < 256, lane >> 4, points)


def pick(full, heads, rows):
    out = None
    for h in range(H):
        part = jnp.where(heads == h, full[h * rows : (h + 1) * rows], 0.0)
        out = part if out is None else out + part
    return out


def spread(x, heads):
    return jnp.concatenate([jnp.where(heads == h, x, 0.0) for h in range(H)], axis=0)


def spread2(x, heads):
    hi, lo = split(x)
    hi32, lo32 = hi.astype(F32), lo.astype(F32)
    return spread(hi32, heads).astype(BF16), spread(lo32, heads).astype(BF16)


def columns(frames_block, first):
    cols = [frames_block[:, first + n : first + n + 1] for n in range(12)]
    return [[cols[3 * a + b] for b in range(3)] for a in range(3)], cols[9:]


def block(x, a):
    return x[:, 256 + 128 * a : 384 + 128 * a]


def rotate(rot, pts):
    return [sum(rot[a][b] * pts[b] for b in range(3)) for a in range(3)]


def unrotate(rot, pts):
    return [sum(rot[a][b] * pts[a] for a in range(3)) for b in range(3)]


def place(rot, shift, flat):
    local_pts = [block(flat, a) for a in range(3)]
    turned = rotate(rot, local_pts)
    return jnp.concatenate(
        [flat[:, :256]] + [turned[a] + shift[a] for a in range(3)], axis=1
    )


def lane_matrix(rows, fn):
    r = iota((rows, 128), 0)
    c = iota((rows, 128), 1)
    return (fn(r) == c).astype(F32).astype(BF16)


def upstream_parts(g, w_out_ref, gp_ref, pu_ref, rows):
    hi, lo = split(g)
    both = jnp.concatenate([hi, lo], axis=0)

    def part(first, count):
        r = mm(both, w_out_ref[first : first + count, :], NT)
        return r[:rows] + r[rows:]

    gp_ref[...] = jnp.zeros(gp_ref.shape, F32)
    gp_ref[:, 0:192] = part(0, 192)
    for a in range(4):
        gp_ref[:, 256 + 128 * a : 352 + 128 * a] = part(192 + 96 * a, 96)
    wide = part(576, H * CZ)
    for h in range(H):
        pu_ref[h * rows : (h + 1) * rows, :] = (
            wide[:, h * CZ : (h + 1) * CZ].astype(BF16).astype(F32)
        )


def pair_products(pu_ref, pair_ref, d_ref, rows):
    step = 4
    for i in range(0, rows, step):
        lhs = jnp.concatenate([pu_ref[pl.ds(i + n, H, stride=rows), :] for n in range(step)], axis=0)
        both = mm(lhs.astype(BF16), pair_ref[i : i + step].reshape(-1, CZ), NT)
        keys = both.shape[1] // step
        for n in range(step):
            d_ref[pl.ds(i + n, H, stride=rows), :] = both[H * n : H * (n + 1), keys * n : keys * (n + 1)]


def split3(x):
    hi, _ = split(x)
    rest = x - hi.astype(F32)
    mid, lo = split(rest)
    return hi, mid, lo


def pack_body(single_hbm, frames_hbm, chains_hbm, pack_ref, frames_ref, chains_ref, sems):
    rows = pack_ref.shape[0]
    ends = (
        (frames_hbm, frames_ref), (chains_hbm, chains_ref), (single_hbm.at[1], pack_ref.at[:, 0:C]),
        (single_hbm.at[0], pack_ref.at[:, C : 2 * C]),
    )
    copies = [pltpu.make_async_copy(src, dst, sems.at[n]) for n, (src, dst) in enumerate(ends)]
    for copy in copies:
        copy.start()
    copies[0].wait()
    copies[1].wait()
    out = jnp.zeros((rows, 128), F32)
    for slot, l in ((0, 1), (12, 0)):
        hot = (iota((12, 128), 1) == iota((12, 128), 0) + slot).astype(F32).astype(BF16)
        for part in split3(frames_ref[:, l, :]):
            out = out + mm(part, hot, TN)
    hot = (iota((1, 128), 1) == CHAIN_LANE - FRAME_LANE).astype(F32).astype(BF16)
    pack_ref[:, 2 * C :] = out + mm(chains_ref[...].astype(F32).astype(BF16), hot, TN)
    copies[2].wait()
    copies[3].wait()


def prep_body(
    pack_ref, cot_hbm, w_out_hbm, pair_hbm, wq_hbm, wk_hbm, wv_hbm, wqp_hbm, wkp_hbm, wvp_hbm, hw_hbm,
    wk_out, wq_out, gp_ref, q1_ref, q0_ref, pu_ref, d_ref, sc_ref,
    cot_ref, w_out_ref, pair_ref, wq_ref, wk_ref, wv_ref, wqp_ref, wkp_ref, wvp_ref, hw_ref, sems,
):
    rows = pack_ref.shape[0]
    ends = (
        (cot_hbm, cot_ref), (w_out_hbm, w_out_ref), (pair_hbm, pair_ref), (wq_hbm, wq_ref), (wk_hbm, wk_ref),
        (wv_hbm, wv_ref), (wqp_hbm, wqp_ref), (wkp_hbm, wkp_ref), (wvp_hbm, wvp_ref), (hw_hbm, hw_ref),
    )
    copies = [pltpu.make_async_copy(src, dst, sems.at[n]) for n, (src, dst) in enumerate(ends)]
    for copy in copies:
        copy.start()
    copies[0].wait()
    copies[1].wait()
    upstream_parts(cot_ref[...], w_out_ref, gp_ref, pu_ref, rows)
    copies[2].wait()
    pair_products(pu_ref, pair_ref, d_ref, rows)
    for copy in copies[3:]:
        copy.wait()
    wq_out[...] = jnp.zeros(wq_out.shape, BF16)
    wk_out[...] = jnp.zeros(wk_out.shape, BF16)
    wq_out[0:192, :] = wq_ref[...]
    wk_out[0:192, :] = wk_ref[...]
    wk_out[640:832, :] = wv_ref[...]
    for a in range(3):
        wq_out[256 + 128 * a : 304 + 128 * a, :] = wqp_ref[48 * a : 48 * a + 48, :]
        wk_out[256 + 128 * a : 304 + 128 * a, :] = wkp_ref[48 * a : 48 * a + 48, :]
        wk_out[896 + 128 * a : 992 + 128 * a, :] = wvp_ref[96 * a : 96 * a + 96, :]
    lane = iota((8, 128), 1)
    raw = jnp.zeros((8, 128), F32)
    for h in range(H):
        raw = jnp.where((lane >> 2) == h, hw_ref[:, h : h + 1], raw)
    soft = jnp.maximum(raw, 0.0) + jnp.log(1.0 + jnp.exp(-jnp.abs(raw)))
    sc_ref[...] = soft * POINT_SCALE
    fr = pack_ref[:, FRAME_LANE : FRAME_LANE + 128]
    for out, first, fcol in ((q1_ref, 0, 0), (q0_ref, C, 12)):
        flat = mm2(pack_ref[:, first : first + C], wq_out[...], NT)
        rot, shift = columns(fr, fcol)
        out[:, :LANES] = place(rot, shift, flat)
        out[:, LANES:] = flat[:, 256:]


def project_keys(x, fr, fcol, wk_ref, kv_ref):
    flat = mm2(x, wk_ref[...], NT)
    rot, shift = columns(fr, fcol)
    kv_ref[:, 0:640] = place(rot, shift, flat[:, :640])
    kv_ref[:, 640:1280] = place(rot, shift, flat[:, 640:])
    kv_ref[:, 1280:1664] = flat[:, 256:640]
    kv_ref[:, 1664:2048] = flat[:, 896:1280]


def value_sums(probs, kv_ref, rows):
    values = kv_ref[:, 640:1280]
    lane = iota(values.shape, 1)
    values = jnp.where((lane >= 256 + STAT) & (lane < 256 + STAT + H), 1.0, values)
    hi, lo = split(values)
    return pick(mm(probs, hi) + mm(probs, lo), value_heads(rows), rows)


def head_dots(prod, rows):
    return mm2(prod, lane_matrix(256, lambda r: STAT + (r >> 4)))


def first_body(
    fast, self_ref, own_ref, ownx_ref, p1_ref, p1x_ref, p2_ref, p2x_ref, wk_ref, links_ref, probs_ref, gp_ref, d_ref,
    keys_ref, kv_ref, pm_ref, mask_ref, e_ref,
):
    rows = own_ref.shape[0]
    home, zb, core = position(fast)

    def put(z, k, value):
        keys_ref[pl.ds(pl.multiple_of(jnp.int32((2 * z + k) * rows), rows), rows), :] = value

    put(zb, core, jnp.where(home, own_ref[...], p1_ref[...]))
    put(zb, 1 - core, jnp.where(home, ownx_ref[...], p1x_ref[...]))
    put(1 - zb, core, jnp.where(home, p1_ref[...], p2_ref[...]))
    put(1 - zb, 1 - core, jnp.where(home, p1x_ref[...], p2x_ref[...]))
    fr = keys_ref[:, FRAME_LANE : FRAME_LANE + 128]
    keys = fr.shape[0]
    at = CHAIN_LANE - FRAME_LANE
    key_chain = fr[:, at : at + 1]
    own_chain = self_ref[:, FRAME_LANE : FRAME_LANE + 128][:, at : at + 1]
    key_hot = (iota((keys, NCHAIN), 1).astype(F32) == key_chain).astype(F32).astype(BF16)
    own_hot = (iota((rows, NCHAIN), 1).astype(F32) == own_chain).astype(F32).astype(BF16)
    eye = iota((NCHAIN, NCHAIN), 0) == iota((NCHAIN, NCHAIN), 1)
    allowed = jnp.where(eye, 1.0, links_ref[...].astype(F32)).astype(BF16)
    mask = mm(mm(own_hot, allowed).astype(BF16), key_hot, NT)
    mask_ref[...] = mask
    pm_ref[...] = (probs_ref[1].astype(F32) * jnp.concatenate([mask] * H, axis=0)).astype(BF16)
    project_keys(keys_ref[:, 0:C], fr, 0, wk_ref, kv_ref)
    probs = pm_ref[...]
    sums = value_sums(probs, kv_ref, rows)
    weighted = mm2(probs.astype(F32) * d_ref[...], jnp.ones((keys, 128), BF16))
    lane = iota((rows, 128), 1)
    dots = pick(weighted, lane - STAT, rows) + head_dots(gp_ref[:, 0:256] * sums[:, 0:256], rows)
    e_ref[:, 0:128] = block(sums, 0)
    e_ref[:, 128:256] = jnp.where(lane < STAT, block(sums, 1), dots)
    e_ref[:, 256:384] = block(sums, 2)


def second_body(
    keys_ref, wk_ref, probs_ref, mask_ref, pair_ref, kv_ref, pm_ref, e_ref, tail_ref, p32_ref, op_ref
):
    rows = pair_ref.shape[0]
    fr = keys_ref[:, FRAME_LANE : FRAME_LANE + 128]
    project_keys(keys_ref[:, C : 2 * C], fr, 12, wk_ref, kv_ref)
    probs = (probs_ref[0].astype(F32) * jnp.concatenate([mask_ref[...]] * H, axis=0)).astype(BF16)
    pm_ref[...] = probs
    sums = value_sums(probs, kv_ref, rows)
    for a in range(3):
        e_ref[:, 128 * a : 128 * a + 128] = block(sums, a)
    e_ref[:, 384:640] = sums[:, 0:256]
    p32_ref[...] = probs.astype(F32)
    for i in range(rows):
        lhs = p32_ref[pl.ds(i, H, stride=rows), :].astype(BF16)
        op_ref[pl.ds(i, H, stride=rows), :] = mm(lhs, pair_ref[i])
    for h in range(H):
        ref, first = (e_ref, 640 + CZ * h) if h < EARLY else (tail_ref, CZ * (h - EARLY))
        ref[:, first : first + CZ] = op_ref[h * rows : (h + 1) * rows, :]


def backward(
    e, dots, probs, kv_ref, key_fr, own_fr, fcol, q_ref, gp, d_ref, wk_ref, sc,
    z_ref, keys_out_ref,
):
    rows = e.shape[0]
    lane = iota((rows, 128), 1)
    stat = (lane >= STAT) & (lane < STAT + H)
    inv = jnp.where(stat, 1.0 / jnp.where(stat, e[:, 0:128], 1.0), 0.0)
    r128 = iota((128, LANES), 0)
    grow = (r128 - STAT == value_heads(128)) & ((iota((128, LANES), 1) & 127) < STAT)
    grow = grow | ((r128 - STAT == (iota((128, LANES), 1) >> 4)) & (iota((128, LANES), 1) < 256))
    inv_lanes = mm2(inv, grow.astype(F32).astype(BF16))
    rot, shift = columns(own_fr, fcol)
    inv_pts = block(inv_lanes, 0)
    ptg = [e[:, 128 * a : 128 * a + 128] * inv_pts for a in range(3)]
    off = [jnp.where(lane < STAT, ptg[a] - shift[a], 0.0) for a in range(3)]
    opt = unrotate(rot, off)
    length = jnp.sqrt(opt[0] * opt[0] + opt[1] * opt[1] + opt[2] * opt[2] + NORM_EPS)
    scale = gp[:, 640:768] / length
    gpt = [block(gp, a) + scale * opt[a] for a in range(3)]
    gptg = rotate(rot, gpt)
    upper = jnp.concatenate([gp[:, 0:256]] + gptg, axis=1)
    point_dots = gptg[0] * ptg[0] + gptg[1] * ptg[1] + gptg[2] * ptg[2]
    rd = dots * inv + mm2(point_dots, lane_matrix(128, lambda r: STAT + (r >> 3)))
    both = jnp.concatenate([spread(rd, lane - STAT), spread(inv, lane - STAT)], axis=0)
    wide = mm2(both, jnp.ones((128, 128), BF16))
    rd_all, inv_all = wide[: H * rows], wide[H * rows :]
    heads_v = value_heads(rows)
    heads_k = key_heads(rows)
    uh, ul = spread2(upper, heads_v)
    vh, vl = split(kv_ref[:, 640:1280])
    d_att = d_ref[...] + mm3(uh, ul, vh, vl, NT)
    p32 = probs.astype(F32)
    att = p32 * inv_all
    dl = LOGIT_SCALE * att * (d_att - rd_all)
    z_ref[0 : H * rows, :] = att
    z_ref[H * rows :, :] = dl
    dt = jnp.transpose(dl)
    th, tl = split(dt)
    qh, qlo = spread2(q_ref[:, 0:640], heads_k)
    kr = mm3(th, tl, qh, qlo)
    head_rows = iota((H * rows, 128), 0) // rows
    hot = ((iota((H * rows, 128), 1) >> 2) == head_rows).astype(F32).astype(BF16)
    cs = mm(th, hot) + mm(tl, hot)
    pt = jnp.transpose(p32).astype(BF16)
    sh, sl = spread2(upper * inv_lanes, heads_v)
    vr = mm(pt, sh) + mm(pt, sl)
    krot, _ = columns(key_fr, fcol)
    d_kg = [sc * (block(kr, a) - cs * kv_ref[:, 256 + 128 * a : 384 + 128 * a]) for a in range(3)]
    d_vg = [block(vr, a) for a in range(3)]
    d_kl = unrotate(krot, d_kg)
    d_vl = unrotate(krot, d_vg)
    flat = jnp.concatenate([PLAIN_SCALE * kr[:, 0:256]] + d_kl + [vr[:, 0:256]] + d_vl, axis=1)
    keys_out_ref[:, 0:C] = mm2(flat, wk_ref[...])
    return jnp.concatenate(off + gpt + gptg, axis=1), jnp.concatenate(d_kg + d_vg, axis=1)


def frame_sums(prods, first):
    def lane(r):
        q = first + (r >> 7)
        return q + 2 * ((q * 43) >> 8)

    return mm2(jnp.concatenate(prods, axis=1), lane_matrix(12 * 128, lane))


def frame_block(turned, at, rows):
    return jnp.concatenate([turned[8 * m : 8 * m + 8, at : at + rows] for m in range(4)], axis=1)


def store_piece(ref, at, grad, frames):
    rows = grad.shape[0]
    for t in range(3):
        ref[at + rows * t : at + rows * (t + 1), :] = grad[:, 128 * t : 128 * t + 128]
    ref[at + 3 * rows : at + 3 * rows + 8, :] = frames


def backward_frames(grads, kv_ref, first):
    d_kg = [grads[:, 128 * a : 128 * a + 128] for a in range(3)]
    d_vg = [grads[:, 384 + 128 * a : 512 + 128 * a] for a in range(3)]
    k_local = [kv_ref[:, 1280 + 128 * b : 1408 + 128 * b] for b in range(3)]
    v_local = [kv_ref[:, 1664 + 128 * b : 1792 + 128 * b] for b in range(3)]
    prods = [d_kg[a] * k_local[b] + d_vg[a] * v_local[b] for a in range(3) for b in range(3)]
    return frame_sums(prods + [d_kg[a] + d_vg[a] for a in range(3)], first)


def backward_query(dl, kv_ref, own_fr, fcol, q_ref, pts_ref, wq_ref, sc, first_lane, share):
    rows = own_fr.shape[0]
    dh, dlo = split(dl)
    kh, klo = split(kv_ref[:, 0:640])
    qr = pick(mm3(dh, dlo, kh, klo), key_heads(rows), rows)
    rot, _ = columns(own_fr, fcol)
    d_qg = [sc * block(qr, a) for a in range(3)]
    d_ql = unrotate(rot, d_qg)
    grad = mm2(jnp.concatenate([PLAIN_SCALE * qr[:, 0:256]] + d_ql, axis=1), wq_ref[...])
    q_local = [q_ref[:, 640 + 128 * b : 768 + 128 * b] for b in range(3)]
    off, gpt, gptg = [
        [pts_ref[:, 384 * n + 128 * a : 384 * n + 128 * a + 128] for a in range(3)] for n in range(3)
    ]
    prods = [d_qg[a] * q_local[b] + share * off[a] * gpt[b] for a in range(3) for b in range(3)]
    prods = prods + [d_qg[a] - share * gptg[a] for a in range(3)]
    return grad, frame_sums(prods, first_lane)


def position(fast):
    if not fast:
        return True, 0, 0
    row = lax.axis_index("row")
    return row // 4 == lax.axis_index("col"), (row // 2) % 2, row % 2


def send_blocks(fast, src_ref, mine_a, mine_b, theirs, rows):
    _, zb, core = position(fast)

    def get(z, k):
        return src_ref[pl.ds(pl.multiple_of(jnp.int32((2 * z + k) * rows), 8), rows), :]

    mine_a[...] = get(zb, core)
    mine_b[...] = get(1 - zb, core)
    theirs[0:rows, :] = get(zb, 1 - core)
    theirs[rows:, :] = get(1 - zb, 1 - core)


def add_pieces(fast, query, query_other, part, one, two):
    return (query[...] + query_other[...]) + (one[...] + jnp.where(position(fast)[0], part[...], two[...]))


def final_body(fast, r0, r1, r2, r3, r4, one_ref, single_out, frames_out):
    total = add_pieces(fast, r0, r1, r2, r3, r4)
    rows = one_ref.shape[0]
    for t in range(3):
        lanes = slice(128 * t, 128 * t + 128)
        single_out[:, lanes] = one_ref[:, lanes] + total[rows * t : rows * (t + 1), :]
    for m in range(4):
        first = 6 * (m % 2)
        frames_out[first : first + 6, m // 2, :] = total[3 * rows : 3 * rows + 6, rows * m : rows * (m + 1)]


def frame_part(ref):
    return ref[:, FRAME_LANE : FRAME_LANE + 128]


def back_one_body(
    fast, e_mine, e_other, pm_ref, kv_ref, keys_ref, own_ref, q_ref, gp_ref, d_ref, wk_ref, sc_ref,
    z_ref, mine_a, mine_b, theirs, pts_ref, grads_ref, work_ref,
):
    e = e_mine[...] + e_other[...]
    pts_ref[...], grads_ref[...] = backward(
        e, e[:, 128:256], pm_ref[...], kv_ref, frame_part(keys_ref), frame_part(own_ref), 0, q_ref,
        gp_ref[...], d_ref, wk_ref, sc_ref[0:1, :], z_ref, work_ref,
    )
    send_blocks(fast, work_ref, mine_a, mine_b, theirs, own_ref.shape[0])


def query_one_body(
    share, z_ref, kv_ref, own_ref, q_ref, pts_ref, grads_ref, wq_ref, sc_ref, query_out, frq_ref, frk_ref
):
    half = z_ref.shape[0] // 2
    query_out[...], frq_ref[...] = backward_query(
        z_ref[half:, :], kv_ref, frame_part(own_ref), 0, q_ref, pts_ref, wq_ref, sc_ref[0:1, :], 12, share
    )
    frk_ref[...] = backward_frames(grads_ref[...], kv_ref, 12)


def back_zero_body(
    fast, cot_ref, r0, r1, r2, r3, r4, e_mine, e_other, tail_mine, tail_other, pm_ref, kv_ref, keys_ref, own_ref, q_ref, pair_ref,
    w_out_ref, wk_ref, sc_ref, frk_ref,
    z_ref, mine_a, mine_b, theirs, pts_ref, sum_ref, pu_ref, work_ref, pieces_ref, gp_ref, d_ref,
):
    rows = own_ref.shape[0]
    total = add_pieces(fast, r0, r1, r2, r3, r4)
    sum_ref[...] = total
    upstream_parts(cot_ref[...] + total, w_out_ref, gp_ref, pu_ref, rows)
    pair_products(pu_ref, pair_ref, d_ref, rows)
    gp = gp_ref[...]
    e = e_mine[:, 0:384] + e_other[:, 0:384]
    plain = e_mine[:, 384:640] + e_other[:, 384:640]
    dots = head_dots(gp[:, 0:256] * plain, rows)
    wide = jnp.concatenate(
        [
            pu_ref[h * rows : (h + 1) * rows, :]
            * (
                e_mine[:, 640 + CZ * h : 640 + CZ * (h + 1)] + e_other[:, 640 + CZ * h : 640 + CZ * (h + 1)]
                if h < EARLY
                else tail_mine[:, CZ * (h - EARLY) : CZ * (h - EARLY + 1)]
                + tail_other[:, CZ * (h - EARLY) : CZ * (h - EARLY + 1)]
            )
            for h in range(H)
        ],
        axis=1,
    )
    dots = dots + mm2(wide, lane_matrix(H * CZ, lambda r: STAT + (r >> 7)))
    pts_ref[...], grads = backward(
        e, dots, pm_ref[...], kv_ref, frame_part(keys_ref), frame_part(own_ref), 12, q_ref, gp, d_ref, wk_ref,
        sc_ref[0:1, :], z_ref, work_ref,
    )
    turned = jnp.transpose(backward_frames(grads, kv_ref, 0) + frk_ref[...])
    for n in range(4):
        at = n * pieces_ref.shape[0] // 4
        store_piece(pieces_ref, at, work_ref[rows * n : rows * (n + 1), :], frame_block(turned, rows * n, rows))
    send_blocks(fast, pieces_ref, mine_a, mine_b, theirs, mine_a.shape[0])


def query_zero_body(share, z_ref, kv_ref, own_ref, q_ref, pts_ref, wq_ref, sc_ref, frq_ref, query_out):
    half = z_ref.shape[0] // 2
    grad, frames = backward_query(
        z_ref[half:, :], kv_ref, frame_part(own_ref), 12, q_ref, pts_ref, wq_ref, sc_ref[0:1, :], 0, share
    )
    store_piece(query_out, 0, grad, frame_block(jnp.transpose(frames + frq_ref[...]), 0, own_ref.shape[0]))


def pair_body(z1_ref, z0_ref, pu1_ref, pu0_ref, wbt_ref, out_ref):
    rows = out_ref.shape[0]
    wbt = wbt_ref[...].astype(F32)
    for i in range(rows):
        left = jnp.concatenate(
            [z1_ref[pl.ds(i, 2 * H, stride=rows), :], z0_ref[pl.ds(i, 2 * H, stride=rows), :]], axis=0
        )
        right = jnp.concatenate(
            [pu1_ref[pl.ds(i, H, stride=rows), :], wbt, pu0_ref[pl.ds(i, H, stride=rows), :], wbt], axis=0
        ).astype(BF16)
        out_ref[i] = mm(left.astype(BF16), right, TN).astype(BF16)


VMEM = pl.BlockSpec(memory_space=pltpu.VMEM)
HBM = pl.BlockSpec(memory_space=pltpu.HBM)


def call(body, name, in_specs, outs, args, scratch=(), micros=1.0):
    return pl.pallas_call(
        body,
        name=name,
        in_specs=in_specs,
        out_specs=tuple(VMEM for _ in outs),
        out_shape=tuple(jax.ShapeDtypeStruct(s, d) for s, d in outs),
        scratch_shapes=list(scratch),
        compiler_params=pltpu.CompilerParams(vmem_limit_bytes=16 * 1024 * 1024),
        cost_estimate=pl.CostEstimate(flops=int(micros * 1e9), transcendentals=0, bytes_accessed=int(micros * 3e6)),
    )(*args)


def in_hbm(*arrays):
    return tuple(pltpu.with_memory_space_constraint(x, pltpu.HBM) for x in arrays)


def joint(pairs):
    return [
        ((a * 2 + k) * 2 + x, (b * 2 + k) * 2 + y) for (x, a), (y, b) in pairs for k in range(2)
    ]


BOTH = ("row", "col")
FETCH_ONE = joint([((0, 0), (0, 1)), ((0, 1), (0, 0)), ((1, 0), (0, 2)), ((1, 1), (0, 3)), ((1, 2), (1, 3)), ((1, 3), (1, 2)), ((0, 2), (1, 0)), ((0, 3), (1, 1))])
FETCH_TWO = joint([((0, 0), (0, 3)), ((0, 1), (0, 2)), ((1, 2), (1, 1)), ((1, 3), (1, 0)), ((1, 0), (0, 0)), ((1, 1), (0, 1)), ((0, 2), (1, 2)), ((0, 3), (1, 3))])
SEND_ONE = joint([((0, 0), (1, 0)), ((0, 1), (1, 1)), ((0, 2), (0, 0)), ((0, 3), (0, 1)), ((1, 2), (0, 2)), ((1, 3), (0, 3)), ((1, 0), (1, 2)), ((1, 1), (1, 3))])
SEND_TWO = joint([((0, 2), (1, 0)), ((0, 3), (1, 1)), ((1, 0), (0, 2)), ((1, 1), (0, 3)), ((0, 0), (0, 1)), ((0, 1), (0, 0)), ((1, 2), (1, 3)), ((1, 3), (1, 2))])
CORE_SWAP = [(i, i ^ 1) for i in range(8)]
Z_SWAP = [(i, i ^ 2) for i in range(8)]
COL_SWAP = [(0, 1), (1, 0)]


def local(
    single, frames, saved_probs, pair, cotangent, chains, links, w_query, w_key, w_value, w_query_points,
    w_key_points, w_value_points, w_bias, w_out, head_weights,
):
    rows = single.shape[1]
    keys = pair.shape[1]
    row_total = lax.axis_size("row")
    col_total = lax.axis_size("col")
    fast = row_total == 8 and col_total == 2 and keys == 4 * rows
    (pack,) = call(
        pack_body, "pack", [HBM] * 3, [((rows, PACK), F32)], in_hbm(single, frames.transpose(1, 0, 2), chains[None]),
        [pltpu.VMEM((12, 2, rows), F32), pltpu.VMEM((1, rows), jnp.int32), pltpu.SemaphoreType.DMA((4,))],
    )
    col = lax.axis_index("col")
    row = lax.axis_index("row")
    if fast:
        ownx = lax.ppermute(pack, "row", CORE_SWAP)
        one = lax.ppermute(pack, BOTH, FETCH_ONE)
        two = lax.ppermute(pack, BOTH, FETCH_TWO)
        own = pack
    else:
        whole = lax.all_gather(pack, "row", axis=0, tiled=True)
        mine = lax.dynamic_slice_in_dim(whole, col * keys, keys, 0)
        quarter = keys // 4
        blocks = tuple(mine[quarter * n : quarter * (n + 1)] for n in (0, 1, 2, 3, 0, 0))
        own = pack

    def col_other(x):
        if col_total == 2:
            return lax.ppermute(x, "col", COL_SWAP)
        return lax.psum(x, "col") - x

    def reduce(mine_a, mine_b, theirs, soon, late, first_beside, beside):
        if fast:
            got = lax.ppermute(theirs, "row", CORE_SWAP)
            if soon:
                query, *rest = late(())
                got, query = lax.optimization_barrier((got, query))
            else:
                got, first_beside = lax.optimization_barrier((got, first_beside))
                query, *rest = late(got)
            query_other = lax.ppermute(query, "col", COL_SWAP)
            count = mine_a.shape[0]
            half = lax.ppermute(mine_b + got[count:], "row", Z_SWAP)
            half, beside, query = lax.optimization_barrier((half, beside, query))
            part = mine_a + got[:count] + half
            sent = [lax.ppermute(part, BOTH, SEND_ONE), lax.ppermute(part, BOTH, SEND_TWO)]
            return [query, query_other, part] + sent, rest, (first_beside, beside)
        query, *rest = late(())
        count = mine_a.shape[0]
        parts = jnp.concatenate([mine_a, theirs[:count], mine_b, theirs[count:]], axis=0)
        summed = lax.all_gather(lax.psum(parts, "row"), "col", axis=0, tiled=True)
        back = lax.dynamic_slice_in_dim(summed, row * count, count, 0)
        zero = jnp.zeros_like(query)
        return [lax.psum(query, "col"), zero, back, zero, zero], rest, (first_beside, beside)

    probs = saved_probs.reshape(2, H * rows, keys)
    hr = H * rows
    loads = (
        cotangent, w_out, pair, w_query.T, w_key.T, w_value.T, w_query_points.T, w_key_points.T, w_value_points.T,
        head_weights[None],
    )
    wk, wq, gp1, q1, q0, pu1, d1, sc = call(
        prep_body, "prep", [VMEM] + [HBM] * 10,
        [((1280, C), BF16), ((LANES, C), BF16), ((rows, 768), F32), ((rows, 1024), F32), ((rows, 1024), F32),
         ((hr, CZ), F32), ((hr, keys), F32), ((8, 128), F32)],
        (own, *in_hbm(*loads)),
        [pltpu.VMEM(x.shape, x.dtype) for x in loads] + [pltpu.SemaphoreType.DMA((len(loads),))],
    )
    if fast:
        one, two, wk, wq, gp1, q1, q0, pu1, d1, sc = lax.optimization_barrier(
            (one, two, wk, wq, gp1, q1, q0, pu1, d1, sc)
        )
        blocks = (pack, ownx, one, lax.ppermute(one, "row", CORE_SWAP), two, lax.ppermute(two, "row", CORE_SWAP))
    key_pack, kv1, pm1, mask, e1 = call(
        functools.partial(first_body, fast), "first", [VMEM] * 12,
        [((keys, PACK), F32), ((keys, 2048), F32), ((hr, keys), BF16), ((rows, keys), F32), ((rows, 384), F32)],
        (own, *blocks, wk, links, probs, gp1, d1),
    )
    e1_other = col_other(e1)
    kv0, pm0, e0, tail = call(
        second_body, "second", [VMEM] * 5,
        [((keys, 2048), F32), ((hr, keys), BF16), ((rows, 640 + EARLY * CZ), F32), ((rows, (H - EARLY) * CZ), F32)],
        (key_pack, wk, probs, mask, pair),
        [pltpu.VMEM((hr, keys), F32), pltpu.VMEM((hr, CZ), F32)],
    )
    e0_other = col_other(e0)
    tail_other = col_other(tail)
    share = 1.0 / col_total
    e1_other, e0 = lax.optimization_barrier((e1_other, e0))
    z1, mine_a, mine_b, theirs, pts, grads = call(
        functools.partial(back_one_body, fast), "back_one", [VMEM] * 11,
        [((2 * hr, keys), F32), ((rows, C), F32), ((rows, C), F32), ((2 * rows, C), F32), ((rows, 1152), F32),
         ((keys, 768), F32)],
        (e1, e1_other, pm1, kv1, key_pack, own, q1, gp1, d1, wk, sc),
        [pltpu.VMEM((keys, C), F32)],
        6.0,
    )
    pieces, (frq, frk), (e0_other, tail_other) = reduce(
        mine_a, mine_b, theirs, False,
        lambda after: call(
            functools.partial(query_one_body, share), "query_one", [VMEM] * 8,
            [((rows, C), F32), ((rows, 128), F32), ((keys, 128), F32)],
            (z1, kv1, own, q1, lax.optimization_barrier((pts, after))[0], grads, wq, sc),
            (),
            0.01,
        ),
        e0_other,
        tail_other,
    )
    long = 3 * rows + 8
    z0, mine_a, mine_b, theirs, pts, single_one, pu0 = call(
        functools.partial(back_zero_body, fast), "back_zero", [VMEM] * 20,
        [((2 * hr, keys), F32), ((long, 128), F32), ((long, 128), F32), ((2 * long, 128), F32), ((rows, 1152), F32),
         ((rows, C), F32), ((hr, CZ), F32)],
        (cotangent, *pieces, e0, e0_other, tail, tail_other, pm0, kv0, key_pack, own, q0, pair, w_out, wk, sc, frk),
        [pltpu.VMEM((keys, C), F32), pltpu.VMEM((4 * long, 128), F32), pltpu.VMEM((rows, 768), F32), pltpu.VMEM((hr, keys), F32)],
    )
    (d_pair,) = call(
        pair_body, "pair_grad", [VMEM] * 5, [((rows, keys, CZ), BF16)], (z1, z0, pu1, pu0, w_bias.T)
    )
    pieces, _, (_, d_pair) = reduce(
        mine_a, mine_b, theirs, True,
        lambda after: call(
            functools.partial(query_zero_body, share), "query_zero", [VMEM] * 8, [((long, 128), F32)],
            (z0, kv0, own, q0, pts, wq, sc, frq),
        ),
        (),
        d_pair,
    )
    d_single, d_frames = call(
        functools.partial(final_body, fast), "final", [VMEM] * 6, [((rows, C), F32), ((12, 2, rows), F32)],
        (*pieces, single_one),
    )
    return (d_single, d_frames.transpose(1, 0, 2), d_pair)


def solution(mesh):
    return jax.shard_map(
        local,
        mesh=mesh,
        in_specs=(
            P(None, ("grp", "row"), None),
            P(None, None, ("grp", "row")),
            P(None, None, ("grp", "row"), "col"),
            P(("grp", "row"), "col", None),
            P(("grp", "row"), None),
            P(("grp", "row")),
            P("grp", None),
            P(),
            P(),
            P(),
            P(),
            P(),
            P(),
            P(),
            P(),
            P(),
        ),
        out_specs=(
            P(("grp", "row"), None),
            P(None, None, ("grp", "row")),
            P(("grp", "row"), "col", None),
        ),
        check_vma=False,
    )
```
